128 devices in a mesh: wa: 4 (over z), facet: 32 (over x, y, core).
Axes of the slice: x: 4, y: 4, z: 4, core: 2. Of those that a mesh axis runs over, the one named last changes fastest.
Arguments:
- visibilities: bfloat16 [16384, 2, 64], P(('wa', 'facet')), may hold values from -6 to 6
- uv_angles: float32 [16384, 2, 64], P(('wa', 'facet')), may hold values from -3.140625 to 3.140625
- routes: int32 [16384, 1], P(('wa', 'facet')), may hold values from 0 to 127; in each aligned block of 128 rows (0 to 127, 128 to 255, ...) at most 2 rows name the same one
- offsets: int32 [16384, 2], P(('wa', 'facet')), may hold values from 0 to 448
- pixel_phase: float32 [32, 512, 512], P('facet'), may hold values from -3.140625 to 3.140625
Outputs:
- partial_images: float32 [4, 32, 512, 1024], P('wa', 'facet')
The draws below stay inside these ranges and needn't reach their ends.
Inputs may be any that keep to these rules, and one draw needn't show every extreme that they name: `routes`: the subgrids of one device name each owner at most 2 times; some owner is named exactly 2 times.
All inputs are finite; a program needn't handle non-finite values.
Results may differ from the reference program's by a relative error of at most 0.0076.
Values may be sent and summed in bfloat16 or wider, within the bound.
A program may use at most 64 MiB of HBM per device.

```python
import math
import jax
import jax.numpy as jnp
import numpy as np
from jax import lax

SUB = 64
GRID = 512
NVIS = 64
SUB_DEV = 128
OWNERS = 128
FACETS = 32
SUBGRIDS = 16384
CAP = 2
N_WA = 4
N_FACET = 32


def touch_ends(array, key, low, high):
    longest = array.shape.index(max(array.shape))
    spots = []
    for shift in (0, 1):
        where = [jax.random.randint(jax.random.fold_in(key, axis), (), 0, length) for axis, length in enumerate(array.shape)]
        where[longest] = (where[longest] + shift) % array.shape[longest]
        spots.append(tuple(where))
    return array.at[spots[0]].set(low).at[spots[1]].set(high)


def level_of(key, dims, pieces, smallest, top_value):
    gain, own = 1.0, jax.random.fold_in(key, 6)
    for dim, parts in pieces:
        draws = jnp.exp(jax.random.uniform(jax.random.fold_in(own, dim), (parts,), jnp.float32, smallest / len(pieces), top_value / len(pieces)))
        gain = gain * jnp.repeat(draws, dims[dim] // parts).reshape([-1 if axis == dim else 1 for axis in range(len(dims))])
    return gain


def deal_out(own_key, own, number, rows, number_of, top, limit, skew):
    order = jax.random.permutation(own_key, number_of)
    heavy_load, ordinary = load_shares(number_of, rows * top, limit, skew, True), load_shares(number_of, rows * top, limit, skew, False)
    places = jnp.arange(number_of)

    def named(tallies, rotation):
        used = int((tallies > 0).sum())
        fixed = max(1, used // 4)
        passed = fixed + (places - fixed + rotation * (used - fixed)) % max(1, number_of - fixed)
        return jnp.zeros((number_of,), jnp.int32).at[order[jnp.where(places < fixed, places, passed)]].set(jnp.asarray(tallies, jnp.int32))

    tallies = jnp.where(number % 4 == 0, named(heavy_load, number // 4), named(ordinary, number - number // 4 - 1))
    mixed = jax.random.permutation(jax.random.fold_in(own, 3), number_of)
    source_of, sink = mixed[0:number_of // 2 * 2:2], mixed[1:number_of // 2 * 2:2]
    margin = jnp.minimum(tallies[source_of] - 1, limit - tallies[sink]) // 2
    margin = jnp.where((source_of == order[0]) | (sink == order[0]) | (tallies[sink] == 0), 0, jnp.maximum(margin, 0))
    passed = jax.random.randint(jax.random.fold_in(own, 4), (number_of // 2,), 0, 1 << 20) % (margin + 1)
    tallies = tallies.at[source_of].add(-passed).at[sink].add(passed)
    items = jnp.searchsorted(jnp.cumsum(tallies), jnp.arange(rows * top), side="right").astype(jnp.int32)
    listing = items.reshape(top, rows).T
    listing = listing[jax.random.permutation(jax.random.fold_in(own, 1), rows)]
    rotation = jax.random.randint(jax.random.fold_in(own, 2), (rows, 1), 0, top)
    return jnp.take_along_axis(listing, (jnp.arange(top)[None, :] + rotation) % top, axis=1)


def load_shares(count, total, reach, skew, full):
    weights = [(1 << 20) // math.isqrt(rank ** skew) + 1 for rank in range(1, count + 1)]
    largest = reach if full else min(reach, max(-(-total // count), total * weights[0] // sum(weights)))
    least = 1 if total - largest >= count - 1 else 0
    counts, surplus = [largest] + [least] * (count - 1), total - largest - least * (count - 1)
    while surplus > 0:
        free = [i for i in range(1, count) if counts[i] < largest] or [i for i in range(1, count) if counts[i] < reach]
        whole, left = sum([weights[i] for i in free]), surplus
        for i in free:
            extra = min(reach - counts[i], max(1, left * weights[i] // whole), surplus)
            counts[i] = counts[i] + extra
            surplus = surplus - extra
    return np.array(counts)


def normal_values(key, shape, spread, most, split=(), kind=jnp.bfloat16):
    factor_of = level_of(key, shape, split, -0.22, 0.18) if split else 1.0
    drawn = jax.random.normal(key, shape, jnp.float32) * spread * factor_of
    return jnp.minimum(jnp.maximum(drawn, -most), most).astype(kind)


def setup_inputs(seed: int = 0) -> dict:
    streams_of = jax.random.split(jax.random.key(seed), 6)
    visibilities = normal_values(streams_of[0], (SUBGRIDS, 2, NVIS), 1.0, 6.0, ((0, 128),))
    uv_angles = jnp.clip(jax.random.uniform(streams_of[1], (SUBGRIDS, 2, NVIS), jnp.float32, -3.140625, 3.140625), -3.140625, 3.140625)
    routes_keys = jax.random.split(jax.random.fold_in(streams_of[2], 1), SUBGRIDS // SUB_DEV)
    routes_turns = jax.random.permutation(jax.random.fold_in(streams_of[2], 3), SUBGRIDS // SUB_DEV)
    routes = jax.vmap(lambda own, number: deal_out(jax.random.fold_in(streams_of[2], 2), own, number, SUB_DEV, OWNERS, 1, CAP, 2))(routes_keys, routes_turns).reshape((SUBGRIDS, 1))
    offsets = touch_ends(jax.random.randint(streams_of[3], (SUBGRIDS, 2), 0, GRID - SUB + 1), jax.random.fold_in(streams_of[3], 1), 0, GRID - SUB).astype(jnp.int32)
    pixel_phase = jnp.clip(jax.random.uniform(streams_of[4], (FACETS, GRID, GRID), jnp.float32, -3.140625, 3.140625), -3.140625, 3.140625)
    return dict(visibilities=visibilities, uv_angles=uv_angles, routes=routes, offsets=offsets, pixel_phase=pixel_phase)


def form_tables(vis_block, angle_block, sub_n):
    centred = (jnp.arange(sub_n) - sub_n // 2).astype(jnp.float32)
    count_vis = vis_block.shape[2]
    norm_scale = 1.0 / math.sqrt(count_vis)
    phase_u = centred[None, :, None] * angle_block[:, 0][:, None, :]
    phase_v = centred[None, :, None] * angle_block[:, 1][:, None, :]
    cos_u = jnp.cos(phase_u)
    sin_u = jnp.sin(phase_u)
    cos_v = jnp.cos(phase_v)
    sin_v = jnp.sin(phase_v)
    vis_re = vis_block[:, 0].astype(jnp.float32)[:, None, :]
    vis_im = vis_block[:, 1].astype(jnp.float32)[:, None, :]
    left_re = (cos_u * vis_re - sin_u * vis_im) * norm_scale
    left_im = (cos_u * vis_im + sin_u * vis_re) * norm_scale
    left_side = jnp.concatenate([left_re, left_im], axis=2).astype(jnp.bfloat16)
    right_side = jnp.concatenate([jnp.concatenate([cos_v, -sin_v], axis=2), jnp.concatenate([sin_v, cos_v], axis=2)], axis=1).astype(jnp.bfloat16)
    return (left_side, right_side)

def dft_tables(grid_n):
    index_line = jnp.arange(grid_n, dtype=jnp.int32)
    product = index_line[:, None] * index_line[None, :] % grid_n
    angle_table = product.astype(jnp.float32) * (2.0 * math.pi / grid_n)
    root_scale = 1.0 / math.sqrt(grid_n)
    cos_table = jnp.cos(angle_table) * root_scale
    sin_table = jnp.sin(angle_table) * root_scale
    row_table = jnp.concatenate([cos_table, sin_table], axis=0).astype(jnp.bfloat16)
    col_table = jnp.concatenate([jnp.concatenate([cos_table, sin_table], axis=1), jnp.concatenate([-sin_table, cos_table], axis=1)], axis=0).astype(jnp.bfloat16)
    return (row_table, col_table)

def inverse_dft(grid_bf, row_table, col_table, grid_n):
    stacked = jnp.dot(row_table, grid_bf, preferred_element_type=jnp.float32)
    half_re = stacked[:grid_n, :grid_n] - stacked[grid_n:, grid_n:]
    half_im = stacked[:grid_n, grid_n:] + stacked[grid_n:, :grid_n]
    half_band = jnp.concatenate([half_re, half_im], axis=1).astype(jnp.bfloat16)
    return jnp.dot(half_band, col_table, preferred_element_type=jnp.float32)

def phase_times(phase_re, phase_im, field, grid_n):
    field_re = field[..., :grid_n]
    field_im = field[..., grid_n:]
    return jnp.concatenate([phase_re * field_re - phase_im * field_im, phase_re * field_im + phase_im * field_re], axis=-1)

def reference(visibilities, uv_angles, routes, offsets, pixel_phase):
    block_n = 64
    owners_n = N_WA * N_FACET
    count_blocks = SUBGRIDS // block_n
    vis_blocks = visibilities.reshape(count_blocks, block_n, 2, NVIS)
    angle_blocks = uv_angles.reshape(count_blocks, block_n, 2, NVIS)
    route_blocks = routes.reshape(count_blocks, block_n)
    offset_blocks = offsets.reshape(count_blocks, block_n, 2)
    col_base = jnp.arange(2 * SUB, dtype=jnp.int32)
    col_shift = col_base // SUB * GRID + col_base % SUB
    sub_line = jnp.arange(SUB, dtype=jnp.int32)

    def add_block(grids, items):
        vis_block, angle_block, route_block, offset_block = items
        left_side, right_side = form_tables(vis_block, angle_block, SUB)
        subgrids = jnp.einsum('bak,bck->bac', left_side.astype(jnp.float32), right_side.astype(jnp.float32)).astype(jnp.bfloat16)
        owner_index = route_block.astype(jnp.int32)[:, None, None]
        row_index = offset_block[:, 0].astype(jnp.int32)[:, None, None] + sub_line[None, :, None]
        col_index = offset_block[:, 1].astype(jnp.int32)[:, None, None] + col_shift[None, None, :]
        grids = grids.at[owner_index, row_index, col_index].add(subgrids.astype(jnp.float32))
        return (grids, None)
    grids = jnp.zeros((owners_n, GRID, 2 * GRID), jnp.float32)
    grids, _ = lax.scan(add_block, grids, (vis_blocks, angle_blocks, route_blocks, offset_blocks))
    grids_bf = grids.astype(jnp.bfloat16)
    row_table, col_table = dft_tables(GRID)
    images = lax.map(lambda one_grid: inverse_dft(one_grid, row_table, col_table, GRID), grids_bf)
    images = images.reshape(N_WA, N_FACET, GRID, 2 * GRID)
    phase_re = jnp.cos(pixel_phase)
    phase_im = jnp.sin(pixel_phase)
    running = images[0]
    results = [running]
    for plane in range(1, N_WA):
        running = phase_times(phase_re, phase_im, running, GRID) + images[plane]
        results.append(running)
    return jnp.stack(results, axis=0)
```

```python
import functools
import math

import jax
import jax.numpy as jnp
import ml_dtypes
import numpy as np
from jax import lax
from jax.experimental import pallas as pl
from jax.experimental.pallas import tpu as pltpu
from jax.sharding import PartitionSpec as P

SUB = 64
GRID = 512
NVIS = 64
SUBS = 128
CAP = 2
KINDS = 4
ROWS = CAP * KINDS
CHUNK = 64
CHUNKS = GRID // CHUNK
UNROLL = 8
BF16 = jnp.bfloat16
F32 = jnp.float32
MESH = pl.DeviceIdType.MESH
VMEM = pl.BlockSpec(memory_space=pltpu.VMEM)
NT = (((1,), (1,)), ((), ()))


def sincos(x):
    h = x * 0.5
    q = h * h
    s = h + h * q * (
        -1.6666666666666602e-1
        + q * (8.333333333320001e-3
        + q * (-1.9841269829589539e-4
        + q * (2.7557314297030280e-6
        + q * (-2.5050747762850355e-8
        + q * 1.5891812000000000e-10))))
    )
    c = 1.0 + q * (
        -0.5
        + q * (4.16666666666665929218e-2
        + q * (-1.38888888888730564116e-3
        + q * (2.48015872888517045348e-5
        + q * (-2.75573141792967388112e-7
        + q * 2.08757008419747316778e-9))))
    )
    return 1.0 - 2.0 * s * s, 2.0 * s * c


def pack_kernel(vis_ref, ang_ref, route_ref, off_ref, send_ref):
    owner = route_ref[...]
    facet = owner % 32
    plane = owner // 32
    odd = facet % 2
    seat_odd = jnp.where(plane < 2, plane + 6, 7 - plane)
    seat = jnp.where(odd == 1, seat_odd, plane)
    device = (seat // 2) * 32 + (facet - odd) + seat % 2
    owner_b = jnp.broadcast_to(owner.astype(F32), (SUBS, SUBS))
    row_i = lax.broadcasted_iota(jnp.int32, (SUBS, SUBS), 0)
    col_i = lax.broadcasted_iota(jnp.int32, (SUBS, SUBS), 1)
    earlier = jnp.where((owner_b == owner_b.T) & (row_i < col_i), 1.0, 0.0)
    rank = jnp.sum(earlier, axis=0, keepdims=True).astype(jnp.int32)
    slot = device * CAP + rank
    total = SUBS * CAP
    col_key = jnp.concatenate([slot + kind * total for kind in range(KINDS)], axis=1)

    angle = ang_ref[...]
    high = angle.astype(BF16)
    low = (angle - high.astype(F32)).astype(BF16)
    off_u, off_v = off_ref[0:1, :], off_ref[1:2, :]
    meta = jnp.where(row_i == 0, off_u // 16, 0)
    meta = jnp.where(row_i == 1, off_u % 16, meta)
    meta = jnp.where(row_i == 2, off_v // 16, meta)
    meta = jnp.where(row_i == 3, off_v % 16, meta)
    meta = meta.astype(F32).astype(BF16)
    data = jnp.concatenate([high, low, vis_ref[...], meta], axis=1)

    for block in range(ROWS):
        row = lax.broadcasted_iota(jnp.int32, (SUBS, KINDS * SUBS), 0) + block * SUBS
        place = row % ROWS
        row_key = (place // CAP) * total + (row // ROWS) * CAP + place % CAP
        one_hot = jnp.where(row_key == col_key, 1.0, 0.0).astype(BF16)
        picked = lax.dot_general(one_hot, data, NT, preferred_element_type=F32)
        send_ref[pl.ds(block * SUBS, SUBS), :] = picked.astype(BF16)


def pack(vis, ang, route, off):
    return pl.pallas_call(
        pack_kernel,
        out_shape=jax.ShapeDtypeStruct((SUBS * ROWS, 128), BF16),
        in_specs=[VMEM] * 4,
        out_specs=VMEM,
        name="pack",
    )(vis, ang, route, off)


def complex_mul(a, b):
    return a[0] * b[0] - a[1] * b[1], a[0] * b[1] + a[1] * b[0]


def grid_kernel(
    recv_ref, gj_ref, wide, pos_v, pos_s, pos_sem, au_r, au_i, av_r, av_i, bu, bv, acc
):
    slots = SUBS * CAP
    wide[...] = recv_ref[...].astype(F32)

    lane8 = lax.broadcasted_iota(jnp.int32, (8, 128), 1)
    weight = jnp.where(lane8 == 0, 8192.0, 0.0)
    weight = jnp.where(lane8 == 1, 512.0, weight)
    weight = jnp.where(lane8 == 2, 16.0, weight)
    weight = jnp.where(lane8 == 3, 1.0, weight).astype(BF16)
    for j in range(CAP):
        meta = wide[pl.ds((KINDS - 1) * CAP + j, SUBS, stride=ROWS), :].astype(BF16)
        packed = lax.dot_general(weight, meta, NT, preferred_element_type=F32)
        pos_v[j] = packed.astype(jnp.int32)
    to_scalar = pltpu.make_async_copy(pos_v, pos_s, pos_sem)
    to_scalar.start()

    acc[...] = jnp.zeros_like(acc)

    group = 16
    first = lax.broadcasted_iota(jnp.int32, (group, 128), 1) < 64

    def tables(g, carry):
        for j in range(CAP):
            start = g * group

            def rows(kind):
                at = start * ROWS + kind * CAP + j
                return wide[pl.ds(at, group, stride=ROWS), :]

            cos_t, sin_t = sincos(rows(0) + rows(1))
            vis = rows(2) * (1.0 / math.sqrt(NVIS))
            cos_o, sin_o = pltpu.roll(cos_t, 64, 1), pltpu.roll(sin_t, 64, 1)
            vis_o = pltpu.roll(vis, 64, 1)
            vis2 = (vis, jnp.where(first, vis_o, -vis_o))
            slot = pl.multiple_of(start + j * SUBS, group)
            for side in range(2):
                if side == 0:
                    e1 = (jnp.where(first, cos_t, cos_o), jnp.where(first, sin_t, sin_o))
                else:
                    e1 = (jnp.where(first, cos_o, cos_t), jnp.where(first, sin_o, sin_t))
                e2 = complex_mul(e1, e1)
                e3 = complex_mul(e2, e1)
                e4 = complex_mul(e2, e2)
                e5 = complex_mul(e4, e1)
                e6 = complex_mul(e4, e2)
                e7 = complex_mul(e4, e3)
                e8 = complex_mul(e4, e4)
                e16 = complex_mul(e8, e8)
                e24 = complex_mul(e16, e8)
                e32 = complex_mul(e16, e16)
                one = (jnp.ones_like(cos_t), jnp.zeros_like(cos_t))
                for a, e in enumerate((one, e1, e2, e3, e4, e5, e6, e7)):
                    where = pl.ds(slot * 8 + a, group, stride=8)
                    if side == 0:
                        re, im = complex_mul(e, vis2)
                        au_r[where, :] = re
                        au_i[where, :] = im
                    else:
                        av_r[where, :] = jnp.where(first, e[0], -e[1])
                        av_i[where, :] = jnp.where(first, e[1], e[0])
                steps = bu if side == 0 else bv
                for b, e in enumerate((e8, e16, e24, e32)):
                    steps[2 * b, pl.ds(slot, group), :] = e[0]
                    steps[2 * b + 1, pl.ds(slot, group), :] = e[1]
        return carry

    lax.fori_loop(0, SUBS // group, tables, 0)
    to_scalar.wait()

    lane_in = lax.broadcasted_iota(jnp.int32, (SUB, 128), 1) % 64

    def form(slot):
        base = pl.multiple_of(slot * 8, 8)
        ur, ui = au_r[pl.ds(base, 8), :], au_i[pl.ds(base, 8), :]
        vr, vi = av_r[pl.ds(base, 8), :], av_i[pl.ds(base, 8), :]

        def step(table, b):
            return table[2 * b, pl.ds(slot, 1), :], table[2 * b + 1, pl.ds(slot, 1), :]

        left = [None] * 8
        right_r = [None] * 8
        right_i = [None] * 8
        left[4], right_r[4], right_i[4] = ur, vr, vi
        for b in range(4):
            br, bi = step(bu, b)
            x, y = br * ur, bi * ui
            left[3 - b] = x + y
            if b < 3:
                left[5 + b] = x - y
            br, bi = step(bv, b)
            x, y, z, w = br * vr, bi * vi, br * vi, bi * vr
            right_r[3 - b] = x + y
            right_i[3 - b] = z - w
            if b < 3:
                right_r[5 + b] = x - y
                right_i[5 + b] = z + w
        left = jnp.concatenate(left, axis=0).astype(BF16)
        right = jnp.concatenate(right_r + right_i, axis=0).astype(BF16)
        return lax.dot_general(left, right, NT, preferred_element_type=F32)

    def place(slot, sub):
        packed = pos_s[slot // SUBS, 0, slot % SUBS]
        off_u, off_v = packed // 512, packed % 512
        tile, shift = off_v // 64, off_v % 64
        near = jnp.where(lane_in >= shift, pltpu.roll(sub, shift, 1), 0.0)
        far = jnp.where(lane_in < shift, pltpu.roll(sub, shift + 64, 1), 0.0)
        acc[tile, pl.ds(off_u, SUB), :] += near
        acc[tile + 1, pl.ds(off_u, SUB), :] += far

    def work(i, carry):
        subs = [form(i * UNROLL + n) for n in range(UNROLL)]
        for n in range(UNROLL):
            place(i * UNROLL + n, subs[n])
        return carry

    lax.fori_loop(0, slots // UNROLL, work, 0)

    sign = jnp.where(lax.broadcasted_iota(jnp.int32, (GRID, 128), 1) < 64, -1.0, 1.0)
    for tile in range(GRID // SUB):
        here = acc[tile]
        cols = pl.ds(tile * 128, 128)
        gj_ref[pl.ds(0, GRID), cols] = here.astype(BF16)
        gj_ref[pl.ds(GRID, GRID), cols] = (pltpu.roll(here, 64, 1) * sign).astype(BF16)


def grid_owner(recv):
    slots = SUBS * CAP
    return pl.pallas_call(
        grid_kernel,
        out_shape=jax.ShapeDtypeStruct((2 * GRID, 2 * GRID), BF16),
        in_specs=[VMEM],
        out_specs=VMEM,
        scratch_shapes=[
            pltpu.VMEM((SUBS * ROWS, 128), F32),
            pltpu.VMEM((CAP, 8, 128), jnp.int32),
            pltpu.SMEM((CAP, 8, 128), jnp.int32),
            pltpu.SemaphoreType.DMA,
        ]
        + [pltpu.VMEM((slots * 8, 128), F32)] * 4
        + [pltpu.VMEM((8, slots, 128), F32)] * 2
        + [pltpu.VMEM((GRID // SUB + 1, GRID, 128), F32)],
        name="grid",
    )(recv)


def chain_kernel(
    gj_ref, row_ref, phase_ref, out_ref, col, phase, from_h, from_s, mine,
    h_recv, s_recv, h_send, s_send, p_sems,
):
    z, f = lax.axis_index("wa"), lax.axis_index("facet")
    core = f % 2
    seat = 2 * z + core
    pair = f - core

    def at(other_seat):
        return (other_seat // 2, pair + other_seat % 2)

    def is_seat(*seats):
        hit = seat == seats[0]
        for other in seats[1:]:
            hit = jnp.logical_or(hit, seat == other)
        return hit

    barrier = pltpu.get_barrier_semaphore()
    for step in range(1, 8):
        pl.semaphore_signal(barrier, inc=1, device_id=at((seat + step) % 8), device_id_type=MESH)

    for tile in range(GRID // SUB):
        rows = row_ref[pl.ds(tile * SUB, SUB), :]
        col[pl.ds(tile * 128, SUB), :] = rows
        col[pl.ds(tile * 128 + SUB, SUB), pl.ds(0, GRID)] = -rows[:, GRID:]
        col[pl.ds(tile * 128 + SUB, SUB), pl.ds(GRID, GRID)] = rows[:, :GRID]

    pl.semaphore_wait(barrier, 7)

    partner = at(seat + 1 - 2 * core)
    gives = is_seat(0, 2, 5)
    takes = is_seat(1, 3, 4)

    def phase_out():
        return pltpu.make_async_remote_copy(
            src_ref=phase_ref, dst_ref=phase, send_sem=p_sems.at[0], recv_sem=p_sems.at[1],
            device_id=partner, device_id_type=MESH,
        )

    def phase_own():
        return pltpu.make_async_copy(phase_ref, phase, p_sems.at[2])

    @pl.when(gives)
    def _():
        phase_out().start()

    @pl.when(jnp.logical_not(takes))
    def _():
        phase_own().start()
        phase_own().wait()

    @pl.when(takes)
    def _():
        phase_out().wait_recv()

    to_h = jnp.where(seat == 5, 4, jnp.where(seat == 7, 5, seat + 1))
    sends_h = is_seat(0, 1, 2, 5, 6, 7)
    takes_h = is_seat(1, 2, 3, 4, 5, 7)
    to_s = jnp.where(seat == 0, 6, jnp.where(seat == 2, 4, jnp.where(seat == 3, 0,
           jnp.where(seat == 4, 7, jnp.where(seat == 5, 3, 1)))))
    takes_s = is_seat(0, 1, 3, 4, 6, 7)

    def copy_h(i):
        rows = pl.ds(pl.multiple_of(i * CHUNK, CHUNK), CHUNK)
        return pltpu.make_async_remote_copy(
            src_ref=mine.at[rows], dst_ref=from_h.at[rows], send_sem=h_send.at[i], recv_sem=h_recv.at[i],
            device_id=at(to_h), device_id_type=MESH,
        )

    def copy_s(i, source):
        rows = pl.ds(pl.multiple_of(i * CHUNK, CHUNK), CHUNK)
        return pltpu.make_async_remote_copy(
            src_ref=source.at[rows], dst_ref=from_s.at[rows], send_sem=s_send.at[i], recv_sem=s_recv.at[i],
            device_id=at(to_s), device_id_type=MESH,
        )

    def work(i, carry):
        rows = pl.ds(pl.multiple_of(i * CHUNK, CHUNK), CHUNK)
        half = jnp.dot(row_ref[rows, :], gj_ref[...], preferred_element_type=F32).astype(BF16)
        image = jnp.dot(half, col[...], preferred_element_type=F32)

        @pl.when(takes_h)
        def _():
            copy_h(i).wait_recv()

            @pl.when(seat == 5)
            def _():
                copy_s(i, from_h).start()

            p_re, p_im = sincos(phase[rows, :])
            f_re = from_h[rows, pl.ds(0, GRID)].astype(F32)
            f_im = from_h[rows, pl.ds(GRID, GRID)].astype(F32)
            mine[rows, pl.ds(0, GRID)] = (p_re * f_re - p_im * f_im + image[:, :GRID]).astype(BF16)
            mine[rows, pl.ds(GRID, GRID)] = (p_re * f_im + p_im * f_re + image[:, GRID:]).astype(BF16)

        @pl.when(jnp.logical_not(takes_h))
        def _():
            mine[rows, :] = image.astype(BF16)

        @pl.when(sends_h)
        def _():
            copy_h(i).start()

        @pl.when(is_seat(2, 3, 4, 6))
        def _():
            copy_s(i, mine).start()

        @pl.when(is_seat(0, 5))
        def _():
            out_ref[rows, :] = mine[rows, :]

        @pl.when(seat == 2)
        def _():
            out_ref[rows, :] = from_h[rows, :]

        return carry

    lax.fori_loop(0, CHUNKS, work, 0)

    def finish(i, carry):
        rows = pl.ds(pl.multiple_of(i * CHUNK, CHUNK), CHUNK)

        @pl.when(takes_s)
        def _():
            copy_s(i, mine).wait_recv()

        @pl.when(seat == 0)
        def _():
            copy_s(i, from_s).start()

        @pl.when(is_seat(1, 3, 4, 6, 7))
        def _():
            out_ref[rows, :] = from_s[rows, :]

        return carry

    lax.fori_loop(0, CHUNKS, finish, 0)

    @pl.when(gives)
    def _():
        phase_out().wait_send()

    def drain(i, carry):
        @pl.when(sends_h)
        def _():
            copy_h(i).wait_send()

        @pl.when(is_seat(0, 2, 3, 4, 5, 6))
        def _():
            copy_s(i, mine).wait_send()

        return carry

    lax.fori_loop(0, CHUNKS, drain, 0)


def chain(gj, row_table, phase):
    return pl.pallas_call(
        chain_kernel,
        out_shape=jax.ShapeDtypeStruct((GRID, 2 * GRID), BF16),
        in_specs=[VMEM, VMEM, pl.BlockSpec(memory_space=pl.ANY)],
        out_specs=VMEM,
        scratch_shapes=[
            pltpu.VMEM((2 * GRID, 2 * GRID), BF16),
            pltpu.VMEM((GRID, GRID), F32),
            pltpu.VMEM((GRID, 2 * GRID), BF16),
            pltpu.VMEM((GRID, 2 * GRID), BF16),
            pltpu.VMEM((GRID, 2 * GRID), BF16),
            pltpu.SemaphoreType.DMA((CHUNKS,)),
            pltpu.SemaphoreType.DMA((CHUNKS,)),
            pltpu.SemaphoreType.DMA((CHUNKS,)),
            pltpu.SemaphoreType.DMA((CHUNKS,)),
            pltpu.SemaphoreType.DMA((3,)),
        ],
        compiler_params=pltpu.CompilerParams(collective_id=1, has_side_effects=True),
        name="chain",
    )(gj, row_table, phase)


def dft_rows():
    line = np.arange(GRID)
    angle = (line[:, None] * line[None, :] % GRID) * (2.0 * math.pi / GRID)
    table = np.concatenate([np.cos(angle), np.sin(angle)], axis=1) / math.sqrt(GRID)
    return table.astype(np.float32).astype(ml_dtypes.bfloat16)


def on_device(visibilities, uv_angles, routes, offsets, pixel_phase):
    vis = visibilities.transpose(1, 2, 0).reshape(2 * NVIS, SUBS)
    ang = uv_angles.transpose(1, 2, 0).reshape(2 * NVIS, SUBS)
    send = pack(vis, ang, routes.reshape(1, SUBS), offsets.T)
    recv = lax.all_to_all(
        send.reshape(SUBS, ROWS, 128), ("wa", "facet"), split_axis=0, concat_axis=0, tiled=True
    )
    gj = grid_owner(recv.reshape(SUBS * ROWS, 128))
    result = chain(gj, jnp.asarray(dft_rows()), pixel_phase[0])
    return result.astype(F32).reshape(1, 1, GRID, 2 * GRID)


def solution(mesh):
    in_specs = (
        P(("wa", "facet"), None, None),
        P(("wa", "facet"), None, None),
        P(("wa", "facet"), None),
        P(("wa", "facet"), None),
        P("facet", None, None),
    )
    out_specs = P("wa", "facet", None, None)
    return jax.shard_map(
        on_device, mesh=mesh, in_specs=in_specs, out_specs=out_specs, check_vma=False
    )
```

```python
import functools
import math

import jax
import jax.numpy as jnp
import ml_dtypes
import numpy as np
from jax import lax
from jax.experimental import pallas as pl
from jax.experimental.pallas import tpu as pltpu
from jax.sharding import PartitionSpec as P

SUB = 64
GRID = 512
NVIS = 64
SUBS = 128
CAP = 2
KINDS = 4
ROWS = CAP * KINDS
BLOCK = 64
CHUNK = 32
CHUNKS = GRID // CHUNK
UNROLL = 4
BF16 = jnp.bfloat16
F32 = jnp.float32
MESH = pl.DeviceIdType.MESH
VMEM = pl.BlockSpec(memory_space=pltpu.VMEM)
NT = (((1,), (1,)), ((), ()))


def sincos(x):
    h = x * 0.5
    q = h * h
    s = h + h * q * (
        -1.6666666666666602e-1
        + q * (8.333333333320001e-3
        + q * (-1.9841269829589539e-4
        + q * (2.7557314297030280e-6
        + q * (-2.5050747762850355e-8
        + q * 1.5891812000000000e-10))))
    )
    c = 1.0 + q * (
        -0.5
        + q * (4.16666666666665929218e-2
        + q * (-1.38888888888730564116e-3
        + q * (2.48015872888517045348e-5
        + q * (-2.75573141792967388112e-7
        + q * 2.08757008419747316778e-9))))
    )
    return 1.0 - 2.0 * s * s, 2.0 * s * c


def route_kernel(vis_ref, ang_ref, route_ref, off_ref, out_ref, send, recv, send_sem, recv_sem):
    z, f = lax.axis_index("wa"), lax.axis_index("facet")
    x, y, core = f >> 3, (f >> 1) & 3, f & 1
    me = z * 32 + f

    def peer(k):
        def far_first(n):
            return jnp.where(n == 0, 2, jnp.where(n == 3, 0, jnp.where(n == 1, 1, 3)))

        z_to = (z + far_first(k >> 5)) & 3
        x_to = (x + far_first((k >> 3) & 3)) & 3
        y_to = (y + far_first((k >> 1) & 3)) & 3
        return z_to, (x_to << 3) | (y_to << 1) | (core ^ (k & 1) ^ 1)

    barrier = pltpu.get_barrier_semaphore()

    def greet(k, carry):
        pl.semaphore_signal(barrier, inc=1, device_id=peer(k), device_id_type=MESH)
        return carry

    lax.fori_loop(0, SUBS - 1, greet, 0)

    owner = route_ref[...]
    facet = owner & 31
    plane = owner >> 5
    odd = facet & 1
    seat = jnp.where(odd == 1, 6, 0)
    seat = jnp.where(plane == 1, jnp.where(odd == 1, 4, 2), seat)
    seat = jnp.where(plane == 2, jnp.where(odd == 1, 5, 3), seat)
    seat = jnp.where(plane == 3, jnp.where(odd == 1, 7, 1), seat)
    device = ((seat >> 1) << 5) + (facet - odd) + (seat & 1)
    owner_b = jnp.broadcast_to(owner.astype(F32), (SUBS, SUBS))
    row_i = lax.broadcasted_iota(jnp.int32, (SUBS, SUBS), 0)
    col_i = lax.broadcasted_iota(jnp.int32, (SUBS, SUBS), 1)
    earlier = jnp.where((owner_b == owner_b.T) & (row_i < col_i), 1.0, 0.0)
    rank = jnp.sum(earlier, axis=0, keepdims=True).astype(jnp.int32)
    slot = device * CAP + rank
    total = SUBS * CAP
    col_key = jnp.concatenate([slot + kind * total for kind in range(KINDS)], axis=1)

    angle = ang_ref[...]
    high = angle.astype(BF16)
    low = (angle - high.astype(F32)).astype(BF16)
    off_u, off_v = off_ref[0:1, :], off_ref[1:2, :]
    meta = jnp.where(row_i == 0, off_u >> 4, 0)
    meta = jnp.where(row_i == 1, off_u & 15, meta)
    meta = jnp.where(row_i == 2, off_v >> 4, meta)
    meta = jnp.where(row_i == 3, off_v & 15, meta)
    meta = meta.astype(F32).astype(BF16)
    data = jnp.concatenate([high, low, vis_ref[...], meta], axis=1)

    for block in range(ROWS):
        row = lax.broadcasted_iota(jnp.int32, (SUBS, KINDS * SUBS), 0) + block * SUBS
        place = row & (ROWS - 1)
        row_key = (place // CAP) * total + (row // ROWS) * CAP + place % CAP
        one_hot = jnp.where(row_key == col_key, 1.0, 0.0).astype(BF16)
        picked = lax.dot_general(one_hot, data, NT, preferred_element_type=F32)
        per = SUBS // ROWS
        send[pl.ds(block * per, per)] = picked.astype(BF16).reshape(per, ROWS, 128)

    pl.semaphore_wait(barrier, SUBS - 1)

    def post(k, carry):
        z_to, f_to = peer(k)
        pltpu.make_async_remote_copy(
            src_ref=send.at[z_to * 32 + f_to], dst_ref=recv.at[me], send_sem=send_sem, recv_sem=recv_sem,
            device_id=(z_to, f_to), device_id_type=MESH,
        ).start()
        return carry

    lax.fori_loop(0, SUBS - 1, post, 0)
    recv[me] = send[me]
    others = pl.ds(0, SUBS - 1)
    pltpu.make_async_copy(send.at[others], recv.at[others], recv_sem).wait()
    out_ref[...] = recv[...]
    pltpu.make_async_copy(send.at[others], recv.at[others], send_sem).wait()


def route(vis, ang, owners, off):
    return pl.pallas_call(
        route_kernel,
        out_shape=jax.ShapeDtypeStruct((SUBS, ROWS, 128), BF16),
        in_specs=[VMEM] * 4,
        out_specs=VMEM,
        scratch_shapes=[
            pltpu.VMEM((SUBS, ROWS, 128), BF16),
            pltpu.VMEM((SUBS, ROWS, 128), BF16),
            pltpu.SemaphoreType.DMA,
            pltpu.SemaphoreType.DMA,
        ],
        compiler_params=pltpu.CompilerParams(
            collective_id=0, has_side_effects=True, vmem_limit_bytes=8 << 20
        ),
        name="route",
    )(vis, ang, owners, off)


def complex_mul(a, b):
    return a[0] * b[0] - a[1] * b[1], a[0] * b[1] + a[1] * b[0]


def grid_kernel(
    recv_ref, grid_ref, wide, pos_v, pos_s, pos_sem, au_r, au_i, av_r, av_i, bu, bv, acc_a, acc_b, sub_a, sub_b
):
    slots = SUBS * CAP
    wide[...] = recv_ref[...].astype(F32)

    lane8 = lax.broadcasted_iota(jnp.int32, (8, 128), 1)
    weight = jnp.where(lane8 == 0, 8192.0, 0.0)
    weight = jnp.where(lane8 == 1, 512.0, weight)
    weight = jnp.where(lane8 == 2, 16.0, weight)
    weight = jnp.where(lane8 == 3, 1.0, weight).astype(BF16)
    for j in range(CAP):
        meta = wide[pl.ds((KINDS - 1) * CAP + j, SUBS, stride=ROWS), :].astype(BF16)
        packed = lax.dot_general(weight, meta, NT, preferred_element_type=F32)
        pos_v[j] = packed.astype(jnp.int32)
    to_scalar = pltpu.make_async_copy(pos_v, pos_s, pos_sem)
    to_scalar.start()

    acc_a[...] = jnp.zeros_like(acc_a)
    acc_b[...] = jnp.zeros_like(acc_b)
    sub_b[...] = jnp.zeros_like(sub_b)

    group = 16
    first = lax.broadcasted_iota(jnp.int32, (group, 128), 1) < 64

    def tables(g, carry):
        for j in range(CAP):
            start = g * group

            def rows(kind):
                at = start * ROWS + kind * CAP + j
                return wide[pl.ds(at, group, stride=ROWS), :]

            cos_t, sin_t = sincos(rows(0) + rows(1))
            vis = rows(2) * (1.0 / math.sqrt(NVIS))
            cos_o, sin_o = pltpu.roll(cos_t, 64, 1), pltpu.roll(sin_t, 64, 1)
            vis_o = pltpu.roll(vis, 64, 1)
            vis2 = (vis, jnp.where(first, vis_o, -vis_o))
            slot = pl.multiple_of(start + j * SUBS, group)
            for side in range(2):
                if side == 0:
                    e1 = (jnp.where(first, cos_t, cos_o), jnp.where(first, sin_t, sin_o))
                else:
                    e1 = (jnp.where(first, cos_o, cos_t), jnp.where(first, sin_o, sin_t))
                e2 = complex_mul(e1, e1)
                e3 = complex_mul(e2, e1)
                e4 = complex_mul(e2, e2)
                e5 = complex_mul(e4, e1)
                e6 = complex_mul(e4, e2)
                e7 = complex_mul(e4, e3)
                e8 = complex_mul(e4, e4)
                e16 = complex_mul(e8, e8)
                e24 = complex_mul(e16, e8)
                e32 = complex_mul(e16, e16)
                one = (jnp.ones_like(cos_t), jnp.zeros_like(cos_t))
                for a, e in enumerate((one, e1, e2, e3, e4, e5, e6, e7)):
                    where = pl.ds(slot * 8 + a, group, stride=8)
                    if side == 0:
                        re, im = complex_mul(e, vis2)
                        au_r[where, :] = re
                        au_i[where, :] = im
                    else:
                        av_r[where, :] = jnp.where(first, e[0], -e[1])
                        av_i[where, :] = jnp.where(first, e[1], e[0])
                steps = bu if side == 0 else bv
                for b, e in enumerate((e8, e16, e24, e32)):
                    steps[2 * b, pl.ds(slot, group), :] = e[0]
                    steps[2 * b + 1, pl.ds(slot, group), :] = e[1]
        return carry

    lax.fori_loop(0, SUBS // group, tables, 0)
    to_scalar.wait()

    lane_in = lax.broadcasted_iota(jnp.int32, (SUB, 128), 1) & 63

    def form(slot):
        base = pl.multiple_of(slot * 8, 8)
        ur, ui = au_r[pl.ds(base, 8), :], au_i[pl.ds(base, 8), :]
        vr, vi = av_r[pl.ds(base, 8), :], av_i[pl.ds(base, 8), :]

        def step(table, b):
            return table[2 * b, pl.ds(slot, 1), :], table[2 * b + 1, pl.ds(slot, 1), :]

        left = [None] * 8
        right_r = [None] * 8
        right_i = [None] * 8
        left[4], right_r[4], right_i[4] = ur, vr, vi
        for b in range(4):
            br, bi = step(bu, b)
            x, y = br * ur, bi * ui
            left[3 - b] = x + y
            if b < 3:
                left[5 + b] = x - y
            br, bi = step(bv, b)
            x, y, z, w = br * vr, bi * vi, br * vi, bi * vr
            right_r[3 - b] = x + y
            right_i[3 - b] = z - w
            if b < 3:
                right_r[5 + b] = x - y
                right_i[5 + b] = z + w
        left = jnp.concatenate(left, axis=0).astype(BF16)
        right = jnp.concatenate(right_r + right_i, axis=0).astype(BF16)
        return lax.dot_general(left, right, NT, preferred_element_type=F32)

    def place(slot, sub, acc):
        packed = pos_s[slot >> 7, 0, slot & (SUBS - 1)]
        off_u, off_v = packed >> 9, packed & 511
        tile, shift = off_v >> 6, off_v & 63
        turned = pltpu.roll(sub, shift, 1)
        rows = pl.ds(off_u, SUB)
        here, there = acc.at[tile, rows, :], acc.at[tile + 1, rows, :]
        near = here[...] + turned
        far = there[...] + pltpu.roll(turned, 64, 1)
        pltpu.store(here, near, mask=lane_in >= shift)
        pltpu.store(there, far, mask=lane_in < shift)

    def work(i, carry):
        now = i * (2 * UNROLL)
        before = jnp.maximum(now - UNROLL, 0)
        for n in range(UNROLL):
            sub_a[n] = form(now + n)
        for n in range(UNROLL):
            place(before + n, sub_b[n], (acc_a, acc_b)[n % 2])
        for n in range(UNROLL):
            sub_b[n] = form(now + UNROLL + n)
        for n in range(UNROLL):
            place(now + n, sub_a[n], (acc_a, acc_b)[n % 2])
        return carry

    lax.fori_loop(0, slots // (2 * UNROLL), work, 0)
    for n in range(UNROLL):
        place(slots - UNROLL + n, sub_b[n], (acc_a, acc_b)[n % 2])

    for tile in range(GRID // SUB):
        grid_ref[:, pl.ds(tile * 128, 128)] = (acc_a[tile] + acc_b[tile]).astype(BF16)


def grid_owner(recv):
    slots = SUBS * CAP
    return pl.pallas_call(
        grid_kernel,
        out_shape=jax.ShapeDtypeStruct((GRID, 2 * GRID), BF16),
        in_specs=[VMEM],
        out_specs=VMEM,
        scratch_shapes=[
            pltpu.VMEM((SUBS * ROWS, 128), F32),
            pltpu.VMEM((CAP, 8, 128), jnp.int32),
            pltpu.SMEM((CAP, 8, 128), jnp.int32),
            pltpu.SemaphoreType.DMA,
        ]
        + [pltpu.VMEM((slots * 8, 128), F32)] * 4
        + [pltpu.VMEM((8, slots, 128), F32)] * 2
        + [pltpu.VMEM((GRID // SUB + 1, GRID, 128), F32)] * 2
        + [pltpu.VMEM((UNROLL, SUB, 128), F32)] * 2,
        compiler_params=pltpu.CompilerParams(vmem_limit_bytes=22 << 20),
        name="grid",
    )(recv)


def chain_kernel(
    grid_ref, row_ref, phase_ref, out_ref, col, phase, p_re, p_im, image, from_h, from_s, mine,
    h_recv, s_recv, h_send, s_send, p_sems,
):
    z, f = lax.axis_index("wa"), lax.axis_index("facet")
    core = f & 1
    seat = 2 * z + core
    pair = f - core

    def at(other_seat):
        return (other_seat >> 1, pair + (other_seat & 1))

    def is_seat(*seats):
        hit = seat == seats[0]
        for other in seats[1:]:
            hit = jnp.logical_or(hit, seat == other)
        return hit

    barrier = pltpu.get_barrier_semaphore()
    for step in range(1, 8):
        pl.semaphore_signal(barrier, inc=1, device_id=at((seat + step) & 7), device_id_type=MESH)

    gives = is_seat(0, 2, 5)
    takes = is_seat(1, 3, 4)
    keeps = is_seat(2, 5, 7)

    def phase_out():
        return pltpu.make_async_remote_copy(
            src_ref=phase_ref, dst_ref=phase, send_sem=p_sems.at[0], recv_sem=p_sems.at[1],
            device_id=at(seat ^ 1), device_id_type=MESH,
        )

    def phase_own():
        return pltpu.make_async_copy(phase_ref, phase, p_sems.at[2])

    @pl.when(keeps)
    def _():
        phase_own().start()

    for tile in range(GRID // SUB):
        rows = row_ref[pl.ds(tile * SUB, SUB), :]
        col[pl.ds(tile * 128, SUB), :] = rows
        col[pl.ds(tile * 128 + SUB, SUB), pl.ds(0, GRID)] = -rows[:, GRID:]
        col[pl.ds(tile * 128 + SUB, SUB), pl.ds(GRID, GRID)] = rows[:, :GRID]

    pl.semaphore_wait(barrier, 7)

    @pl.when(gives)
    def _():
        phase_out().start()

    to_h = jnp.where(seat == 0, 2, jnp.where(seat == 2, 3, jnp.where(seat == 3, 1,
           jnp.where(seat == 6, 4, jnp.where(seat == 4, 5, 7)))))
    to_s = jnp.where(seat == 1, 6, jnp.where(seat == 3, 4, jnp.where(seat == 4, 3, 1)))
    sends_h = is_seat(0, 2, 3, 4, 5, 6)
    takes_h = is_seat(1, 2, 3, 4, 5, 7)
    away = is_seat(1, 3, 4, 6)

    def chunk_rows(i):
        return pl.ds(pl.multiple_of(i * CHUNK, CHUNK), CHUNK)

    def copy_h(i):
        rows = chunk_rows(i)
        return pltpu.make_async_remote_copy(
            src_ref=mine.at[rows], dst_ref=from_h.at[rows], send_sem=h_send.at[i], recv_sem=h_recv.at[i],
            device_id=at(to_h), device_id_type=MESH,
        )

    def copy_s(i):
        rows = chunk_rows(i)
        return pltpu.make_async_remote_copy(
            src_ref=mine.at[rows], dst_ref=from_s.at[rows], send_sem=s_send.at[i], recv_sem=s_recv.at[i],
            device_id=at(to_s), device_id_type=MESH,
        )

    real = lax.broadcasted_iota(jnp.int32, (BLOCK, 2 * GRID), 1) & 127 < 64

    def work(i, carry):
        rows = pl.ds(pl.multiple_of(i * BLOCK, BLOCK), BLOCK)
        both = jnp.concatenate([row_ref[rows, pl.ds(0, GRID)], row_ref[rows, pl.ds(GRID, GRID)]], axis=0)
        parts = jnp.dot(both, grid_ref[...], preferred_element_type=F32)
        turned = jnp.concatenate(
            [pltpu.roll(parts[BLOCK:, t * 128 : (t + 1) * 128], 64, 1) for t in range(GRID // SUB)], axis=1
        )
        half = parts[:BLOCK] + jnp.where(real, -turned, turned)
        image[...] = jnp.dot(half.astype(BF16), col[...], preferred_element_type=F32)

        @pl.when(takes_h)
        def _():
            @pl.when(i == 0)
            def _():
                @pl.when(takes)
                def _():
                    phase_out().wait_recv()

                @pl.when(keeps)
                def _():
                    phase_own().wait()

            c, s = sincos(phase[rows, :])
            p_re[...] = c
            p_im[...] = s

        for part in range(BLOCK // CHUNK):
            chunk = i * (BLOCK // CHUNK) + part
            at_rows = chunk_rows(chunk)
            local = pl.ds(part * CHUNK, CHUNK)

            @pl.when(takes_h)
            def _():
                copy_h(chunk).wait_recv()
                f_re = from_h[at_rows, pl.ds(0, GRID)].astype(F32)
                f_im = from_h[at_rows, pl.ds(GRID, GRID)].astype(F32)
                c, s = p_re[local, :], p_im[local, :]
                im_re, im_im = image[local, pl.ds(0, GRID)], image[local, pl.ds(GRID, GRID)]
                mine[at_rows, pl.ds(0, GRID)] = (c * f_re - s * f_im + im_re).astype(BF16)
                mine[at_rows, pl.ds(GRID, GRID)] = (c * f_im + s * f_re + im_im).astype(BF16)

            @pl.when(jnp.logical_not(takes_h))
            def _():
                mine[at_rows, :] = image[local, :].astype(BF16)

            @pl.when(sends_h)
            def _():
                copy_h(chunk).start()

            @pl.when(away)
            def _():
                copy_s(chunk).start()

            @pl.when(jnp.logical_not(away))
            def _():
                out_ref[at_rows, :] = mine[at_rows, :]

        return carry

    lax.fori_loop(0, GRID // BLOCK, work, 0)

    @pl.when(away)
    def _():
        def finish(i, carry):
            copy_s(i).wait_recv()
            out_ref[chunk_rows(i), :] = from_s[chunk_rows(i), :]
            return carry

        lax.fori_loop(0, CHUNKS, finish, 0)

    @pl.when(gives)
    def _():
        phase_out().wait_send()

    def drain(i, carry):
        @pl.when(sends_h)
        def _():
            copy_h(i).wait_send()

        @pl.when(away)
        def _():
            copy_s(i).wait_send()

        return carry

    lax.fori_loop(0, CHUNKS, drain, 0)


def chain(grid, row_table, phase):
    band = (GRID, 2 * GRID)
    return pl.pallas_call(
        chain_kernel,
        out_shape=jax.ShapeDtypeStruct(band, BF16),
        in_specs=[VMEM, VMEM, pl.BlockSpec(memory_space=pl.ANY)],
        out_specs=VMEM,
        scratch_shapes=[
            pltpu.VMEM((2 * GRID, 2 * GRID), BF16),
            pltpu.VMEM((GRID, GRID), F32),
            pltpu.VMEM((BLOCK, GRID), F32),
            pltpu.VMEM((BLOCK, GRID), F32),
            pltpu.VMEM((BLOCK, 2 * GRID), F32),
            pltpu.VMEM(band, BF16),
            pltpu.VMEM(band, BF16),
            pltpu.VMEM(band, BF16),
        ]
        + [pltpu.SemaphoreType.DMA((CHUNKS,))] * 4
        + [pltpu.SemaphoreType.DMA((3,))],
        compiler_params=pltpu.CompilerParams(
            collective_id=1, has_side_effects=True, vmem_limit_bytes=18 << 20
        ),
        name="chain",
    )(grid, row_table, phase)


def dft_rows():
    line = np.arange(GRID)
    angle = (line[:, None] * line[None, :] % GRID) * (2.0 * math.pi / GRID)
    table = np.concatenate([np.cos(angle), np.sin(angle)], axis=1) / math.sqrt(GRID)
    return table.astype(np.float32).astype(ml_dtypes.bfloat16)


def on_device(visibilities, uv_angles, routes, offsets, pixel_phase):
    vis = visibilities.transpose(1, 2, 0).reshape(2 * NVIS, SUBS)
    ang = uv_angles.transpose(1, 2, 0).reshape(2 * NVIS, SUBS)
    recv = route(vis, ang, routes.reshape(1, SUBS), offsets.T)
    grid = grid_owner(recv.reshape(SUBS * ROWS, 128))
    result = chain(grid, jnp.asarray(dft_rows()), pixel_phase[0])
    return result.astype(F32).reshape(1, 1, GRID, 2 * GRID)


def solution(mesh):
    in_specs = (
        P(("wa", "facet"), None, None),
        P(("wa", "facet"), None, None),
        P(("wa", "facet"), None),
        P(("wa", "facet"), None),
        P("facet", None, None),
    )
    out_specs = P("wa", "facet", None, None)
    return jax.shard_map(
        on_device, mesh=mesh, in_specs=in_specs, out_specs=out_specs, check_vma=False
    )
```

```python
import functools
import math

import jax
import jax.numpy as jnp
import ml_dtypes
import numpy as np
from jax import lax
from jax.experimental import pallas as pl
from jax.experimental.pallas import tpu as pltpu
from jax.sharding import PartitionSpec as P

SUB = 64
GRID = 512
NVIS = 64
SUBS = 128
CAP = 2
KINDS = 4
ROWS = CAP * KINDS
BLOCK = 64
CHUNK = 16
CHUNKS = GRID // CHUNK
UNROLL = 8
BF16 = jnp.bfloat16
F32 = jnp.float32
MESH = pl.DeviceIdType.MESH
VMEM = pl.BlockSpec(memory_space=pltpu.VMEM)
HBM = pl.BlockSpec(memory_space=pltpu.HBM)
NT = (((1,), (1,)), ((), ()))


def sincos(x):
    h = x * 0.5
    q = h * h
    s = h + h * q * (
        -1.6666666666666602e-1
        + q * (8.333333333320001e-3
        + q * (-1.9841269829589539e-4
        + q * (2.7557314297030280e-6
        + q * (-2.5050747762850355e-8
        + q * 1.5891812000000000e-10))))
    )
    c = 1.0 + q * (
        -0.5
        + q * (4.16666666666665929218e-2
        + q * (-1.38888888888730564116e-3
        + q * (2.48015872888517045348e-5
        + q * (-2.75573141792967388112e-7
        + q * 2.08757008419747316778e-9))))
    )
    return 1.0 - 2.0 * s * s, 2.0 * s * c


def route_kernel(
    vis_hbm, ang_hbm, route_hbm, off_hbm, out_ref, vis_ref, ang_ref, route_ref, off_ref, send, recv,
    in_sems, send_sem, recv_sem,
):
    inputs = [
        pltpu.make_async_copy(source, target, in_sems.at[n])
        for n, (source, target) in enumerate(
            ((route_hbm, route_ref), (off_hbm, off_ref), (ang_hbm, ang_ref), (vis_hbm, vis_ref))
        )
    ]
    for copy in inputs:
        copy.start()

    me = lax.axis_index("wa") * 32 + lax.axis_index("facet")

    def each_peer(act):
        def early(i, carry):
            for n in range(5):
                act(me ^ (i * 5 + n) ^ 85)
            return carry

        def late(i, carry):
            for n in range(6):
                act(me ^ (i * 6 + n + 86) ^ 85)
            return carry

        lax.fori_loop(0, 17, early, 0)
        lax.fori_loop(0, 7, late, 0)

    barrier = pltpu.get_barrier_semaphore()
    each_peer(
        lambda to: pl.semaphore_signal(
            barrier, inc=1, device_id=(to >> 5, to & 31), device_id_type=MESH
        )
    )
    for copy in inputs:
        copy.wait()

    owner = route_ref[...]
    facet = owner & 31
    plane = owner >> 5
    odd = facet & 1
    seat = jnp.where(odd == 1, 6, 0)
    seat = jnp.where(plane == 1, jnp.where(odd == 1, 4, 2), seat)
    seat = jnp.where(plane == 2, jnp.where(odd == 1, 5, 3), seat)
    seat = jnp.where(plane == 3, jnp.where(odd == 1, 7, 1), seat)
    device = ((seat >> 1) << 5) + (facet - odd) + (seat & 1)
    owner_b = jnp.broadcast_to(owner.astype(F32), (SUBS, SUBS))
    row_i = lax.broadcasted_iota(jnp.int32, (SUBS, SUBS), 0)
    col_i = lax.broadcasted_iota(jnp.int32, (SUBS, SUBS), 1)
    earlier = jnp.where((owner_b == owner_b.T) & (row_i < col_i), 1.0, 0.0)
    rank = jnp.sum(earlier, axis=0, keepdims=True).astype(jnp.int32)
    slot = device * CAP + rank
    total = SUBS * CAP
    col_key = jnp.concatenate([slot + kind * total for kind in range(KINDS)], axis=1)

    angle = ang_ref[...]
    high = angle.astype(BF16)
    low = (angle - high.astype(F32)).astype(BF16)
    off_u, off_v = off_ref[0:1, :], off_ref[1:2, :]
    meta = jnp.where(row_i == 0, off_u >> 4, 0)
    meta = jnp.where(row_i == 1, off_u & 15, meta)
    meta = jnp.where(row_i == 2, off_v >> 4, meta)
    meta = jnp.where(row_i == 3, off_v & 15, meta)
    meta = meta.astype(F32).astype(BF16)
    data = jnp.concatenate([high, low, vis_ref[...], meta], axis=1)

    for block in range(ROWS):
        row = lax.broadcasted_iota(jnp.int32, (SUBS, KINDS * SUBS), 0) + block * SUBS
        place = row & (ROWS - 1)
        row_key = (place // CAP) * total + (row // ROWS) * CAP + place % CAP
        one_hot = jnp.where(row_key == col_key, 1.0, 0.0).astype(BF16)
        picked = lax.dot_general(one_hot, data, NT, preferred_element_type=F32)
        per = SUBS // ROWS
        send[pl.ds(block * per, per)] = picked.astype(BF16).reshape(per, ROWS, 128)

    pl.semaphore_wait(barrier, SUBS - 1)

    each_peer(
        lambda to: pltpu.make_async_remote_copy(
            src_ref=send.at[to], dst_ref=recv.at[me], send_sem=send_sem, recv_sem=recv_sem,
            device_id=(to >> 5, to & 31), device_id_type=MESH,
        ).start()
    )
    recv[me] = send[me]
    others = pl.ds(0, SUBS - 1)
    pltpu.make_async_copy(send.at[others], recv.at[others], recv_sem).wait()
    out_ref[...] = recv[...]
    pltpu.make_async_copy(send.at[others], recv.at[others], send_sem).wait()


def route(vis, ang, owners, off):
    return pl.pallas_call(
        route_kernel,
        out_shape=jax.ShapeDtypeStruct((SUBS, ROWS, 128), BF16),
        in_specs=[HBM] * 4,
        out_specs=VMEM,
        scratch_shapes=[
            pltpu.VMEM((2 * NVIS, SUBS), BF16),
            pltpu.VMEM((2 * NVIS, SUBS), F32),
            pltpu.VMEM((1, SUBS), jnp.int32),
            pltpu.VMEM((2, SUBS), jnp.int32),
            pltpu.VMEM((SUBS, ROWS, 128), BF16),
            pltpu.VMEM((SUBS, ROWS, 128), BF16),
            pltpu.SemaphoreType.DMA((4,)),
            pltpu.SemaphoreType.DMA,
            pltpu.SemaphoreType.DMA,
        ],
        compiler_params=pltpu.CompilerParams(
            collective_id=0, has_side_effects=True, vmem_limit_bytes=8 << 20
        ),
        name="route",
    )(*[pltpu.with_memory_space_constraint(value, pltpu.HBM) for value in (vis, ang, owners, off)])


def complex_mul(a, b):
    return a[0] * b[0] - a[1] * b[1], a[0] * b[1] + a[1] * b[0]


def grid_kernel(
    recv_ref, rows_hbm, grid_ref, rows_ref, wide, pos_v, pos_s, pos_sem, rows_sem, au_r, au_i, av_r, av_i, bu, bv, acc_a, acc_b, lefts, rights, subs
):
    slots = SUBS * CAP
    rows_copy = pltpu.make_async_copy(rows_hbm, rows_ref, rows_sem)
    rows_copy.start()
    wide[...] = recv_ref[...].astype(F32)

    lane8 = lax.broadcasted_iota(jnp.int32, (8, 128), 1)
    weight = jnp.where(lane8 == 0, 8192.0, 0.0)
    weight = jnp.where(lane8 == 1, 512.0, weight)
    weight = jnp.where(lane8 == 2, 16.0, weight)
    weight = jnp.where(lane8 == 3, 1.0, weight).astype(BF16)
    for j in range(CAP):
        meta = wide[pl.ds((KINDS - 1) * CAP + j, SUBS, stride=ROWS), :].astype(BF16)
        packed = lax.dot_general(weight, meta, NT, preferred_element_type=F32)
        pos_v[j] = packed.astype(jnp.int32)
    to_scalar = pltpu.make_async_copy(pos_v, pos_s, pos_sem)
    to_scalar.start()

    lefts[...] = jnp.zeros_like(lefts)
    rights[...] = jnp.zeros_like(rights)
    subs[...] = jnp.zeros_like(subs)

    group = 16
    first = lax.broadcasted_iota(jnp.int32, (group, 128), 1) < 64

    def tables(g, carry):
        clear = pl.ds(pl.multiple_of(g * SUB, SUB), SUB)
        for tile in range(GRID // SUB + 1):
            acc_a[tile, clear, :] = jnp.zeros((SUB, 128), F32)
            acc_b[tile, clear, :] = jnp.zeros((SUB, 128), F32)
        for j in range(CAP):
            start = g * group

            def rows(kind):
                at = start * ROWS + kind * CAP + j
                return wide[pl.ds(at, group, stride=ROWS), :]

            cos_t, sin_t = sincos(rows(0) + rows(1))
            vis = rows(2) * (1.0 / math.sqrt(NVIS))
            cos_o, sin_o = pltpu.roll(cos_t, 64, 1), pltpu.roll(sin_t, 64, 1)
            vis_o = pltpu.roll(vis, 64, 1)
            vis2 = (vis, jnp.where(first, vis_o, -vis_o))
            slot = pl.multiple_of(start + j * SUBS, group)
            for side in range(2):
                if side == 0:
                    e1 = (jnp.where(first, cos_t, cos_o), jnp.where(first, sin_t, sin_o))
                else:
                    e1 = (jnp.where(first, cos_o, cos_t), jnp.where(first, sin_o, sin_t))
                e2 = complex_mul(e1, e1)
                e3 = complex_mul(e2, e1)
                e4 = complex_mul(e2, e2)
                e5 = complex_mul(e4, e1)
                e6 = complex_mul(e4, e2)
                e7 = complex_mul(e4, e3)
                e8 = complex_mul(e4, e4)
                e16 = complex_mul(e8, e8)
                e24 = complex_mul(e16, e8)
                e32 = complex_mul(e16, e16)
                one = (jnp.ones_like(cos_t), jnp.zeros_like(cos_t))
                for a, e in enumerate((one, e1, e2, e3, e4, e5, e6, e7)):
                    where = pl.ds(slot * 8 + a, group, stride=8)
                    if side == 0:
                        re, im = complex_mul(e, vis2)
                        au_r[where, :] = re
                        au_i[where, :] = im
                    else:
                        av_r[where, :] = jnp.where(first, e[0], -e[1])
                        av_i[where, :] = jnp.where(first, e[1], e[0])
                steps = bu if side == 0 else bv
                for b, e in enumerate((e8, e16, e24, e32)):
                    steps[2 * b, pl.ds(slot, group), :] = e[0]
                    steps[2 * b + 1, pl.ds(slot, group), :] = e[1]
        return carry

    lax.fori_loop(0, SUBS // group, tables, 0)
    to_scalar.wait()

    lane_in = lax.broadcasted_iota(jnp.int32, (SUB, 128), 1) & 63

    def form(n, slot):
        base = pl.multiple_of(slot * 8, 8)
        ur, ui = au_r[pl.ds(base, 8), :], au_i[pl.ds(base, 8), :]
        vr, vi = av_r[pl.ds(base, 8), :], av_i[pl.ds(base, 8), :]

        def step(table, b):
            return table[2 * b, pl.ds(slot, 1), :], table[2 * b + 1, pl.ds(slot, 1), :]

        left = [None] * 8
        right_r = [None] * 8
        right_i = [None] * 8
        left[4], right_r[4], right_i[4] = ur, vr, vi
        for b in range(4):
            br, bi = step(bu, b)
            x, y = br * ur, bi * ui
            left[3 - b] = x + y
            if b < 3:
                left[5 + b] = x - y
            br, bi = step(bv, b)
            x, y, z, w = br * vr, bi * vi, br * vi, bi * vr
            right_r[3 - b] = x + y
            right_i[3 - b] = z - w
            if b < 3:
                right_r[5 + b] = x - y
                right_i[5 + b] = z + w
        lefts[n] = jnp.concatenate(left, axis=0).astype(BF16)
        rights[n] = jnp.concatenate(right_r + right_i, axis=0).astype(BF16)

    nought = jnp.zeros((SUB, 128), BF16)

    def multiply(n):
        left = jnp.concatenate(
            [jnp.concatenate([lefts[n], nought], axis=1), jnp.concatenate([nought, lefts[n + 1]], axis=1)],
            axis=0,
        )
        right = jnp.concatenate([rights[n], rights[n + 1]], axis=1)
        subs[n // 2] = lax.dot_general(left, right, NT, preferred_element_type=F32).astype(BF16)

    def place(slot, sub, acc):
        packed = pos_s[slot >> 7, 0, slot & (SUBS - 1)]
        off_u, off_v = packed >> 9, packed & 511
        tile, shift = off_v >> 6, off_v & 63
        rows = pl.ds(off_u, SUB)
        here, there = acc.at[tile, rows, :], acc.at[tile + 1, rows, :]
        near = here[...] + pltpu.roll(sub, shift, 1).astype(F32)
        far = there[...] + pltpu.roll(sub, shift + 64, 1).astype(F32)
        pltpu.store(here, near, mask=lane_in >= shift)
        pltpu.store(there, far, mask=lane_in < shift)

    def place_all(start):
        for n in range(UNROLL):
            sub = subs[n // 2, pl.ds(n % 2 * SUB, SUB), :]
            place(start + n, sub, (acc_a, acc_b)[n % 2])

    def multiply_all():
        for n in range(0, UNROLL, 2):
            multiply(n)

    def work(i, carry):
        place_all(jnp.maximum(i - 2, 0) * UNROLL)
        multiply_all()
        for n in range(UNROLL):
            form(n, i * UNROLL + n)
        return carry

    lax.fori_loop(0, slots // UNROLL, work, 0)
    place_all(slots - 2 * UNROLL)
    multiply_all()
    place_all(slots - UNROLL)

    def finish(g, carry):
        rows = pl.ds(pl.multiple_of(g * SUB, SUB), SUB)
        for tile in range(GRID // SUB):
            grid_ref[rows, pl.ds(tile * 128, 128)] = (acc_a[tile, rows, :] + acc_b[tile, rows, :]).astype(BF16)
        return carry

    lax.fori_loop(0, GRID // SUB, finish, 0)
    rows_copy.wait()


def grid_owner(recv, row_table):
    slots = SUBS * CAP
    band = jax.ShapeDtypeStruct((GRID, 2 * GRID), BF16)
    return pl.pallas_call(
        grid_kernel,
        out_shape=(band, band),
        in_specs=[VMEM, HBM],
        out_specs=(VMEM, VMEM),
        scratch_shapes=[
            pltpu.VMEM((SUBS * ROWS, 128), F32),
            pltpu.VMEM((CAP, 8, 128), jnp.int32),
            pltpu.SMEM((CAP, 8, 128), jnp.int32),
            pltpu.SemaphoreType.DMA,
            pltpu.SemaphoreType.DMA,
        ]
        + [pltpu.VMEM((slots * 8, 128), F32)] * 4
        + [pltpu.VMEM((8, slots, 128), F32)] * 2
        + [pltpu.VMEM((GRID // SUB + 1, GRID, 128), F32)] * 2
        + [
            pltpu.VMEM((UNROLL, SUB, 128), BF16),
            pltpu.VMEM((UNROLL, 2 * SUB, 128), BF16),
            pltpu.VMEM((UNROLL // 2, 2 * SUB, 128), BF16),
        ],
        compiler_params=pltpu.CompilerParams(vmem_limit_bytes=22 << 20),
        name="grid",
    )(recv, pltpu.with_memory_space_constraint(row_table, pltpu.HBM))


def chain_kernel(
    grid_ref, row_ref, phase_ref, out_ref, col, phase, p_re, p_im, image, from_h, from_s, mine,
    h_recv, s_recv, h_send, s_send, p_sems,
):
    z, f = lax.axis_index("wa"), lax.axis_index("facet")
    core = f & 1
    seat = 2 * z + core
    pair = f - core

    def at(other_seat):
        return (other_seat >> 1, pair + (other_seat & 1))

    def is_seat(*seats):
        hit = seat == seats[0]
        for other in seats[1:]:
            hit = jnp.logical_or(hit, seat == other)
        return hit

    barrier = pltpu.get_barrier_semaphore()
    for step in range(1, 8):
        pl.semaphore_signal(barrier, inc=1, device_id=at((seat + step) & 7), device_id_type=MESH)

    gives = is_seat(0, 2, 5)
    takes = is_seat(1, 3, 4)
    keeps = is_seat(2, 5, 7)

    def phase_out():
        return pltpu.make_async_remote_copy(
            src_ref=phase_ref, dst_ref=phase, send_sem=p_sems.at[0], recv_sem=p_sems.at[1],
            device_id=at(seat ^ 1), device_id_type=MESH,
        )

    def phase_own():
        return pltpu.make_async_copy(phase_ref, phase, p_sems.at[2])

    @pl.when(keeps)
    def _():
        phase_own().start()

    for tile in range(GRID // SUB):
        rows = row_ref[pl.ds(tile * SUB, SUB), :]
        col[pl.ds(tile * 128, SUB), :] = rows
        col[pl.ds(tile * 128 + SUB, SUB), pl.ds(0, GRID)] = -rows[:, GRID:]
        col[pl.ds(tile * 128 + SUB, SUB), pl.ds(GRID, GRID)] = rows[:, :GRID]

    pl.semaphore_wait(barrier, 7)

    @pl.when(gives)
    def _():
        phase_out().start()

    to_h = jnp.where(seat == 0, 2, jnp.where(seat == 2, 3, jnp.where(seat == 3, 1,
           jnp.where(seat == 6, 4, jnp.where(seat == 4, 5, 7)))))
    to_s = jnp.where(seat == 1, 6, jnp.where(seat == 3, 4, jnp.where(seat == 4, 3, 1)))
    sends_h = is_seat(0, 2, 3, 4, 5, 6)
    takes_h = is_seat(1, 2, 3, 4, 5, 7)
    away = is_seat(1, 3, 4, 6)

    def chunk_rows(i):
        return pl.ds(pl.multiple_of(i * CHUNK, CHUNK), CHUNK)

    def copy_h(i):
        rows = chunk_rows(i)
        return pltpu.make_async_remote_copy(
            src_ref=mine.at[rows], dst_ref=from_h.at[rows], send_sem=h_send.at[i], recv_sem=h_recv.at[i],
            device_id=at(to_h), device_id_type=MESH,
        )

    def copy_s(i):
        rows = chunk_rows(i)
        return pltpu.make_async_remote_copy(
            src_ref=mine.at[rows], dst_ref=from_s.at[rows], send_sem=s_send.at[i], recv_sem=s_recv.at[i],
            device_id=at(to_s), device_id_type=MESH,
        )

    real = lax.broadcasted_iota(jnp.int32, (BLOCK, 2 * GRID), 1) & 127 < 64

    def work(i, carry):
        rows = pl.ds(pl.multiple_of(i * BLOCK, BLOCK), BLOCK)
        both = jnp.concatenate([row_ref[rows, pl.ds(0, GRID)], row_ref[rows, pl.ds(GRID, GRID)]], axis=0)
        parts = jnp.dot(both, grid_ref[...], preferred_element_type=F32)
        turned = jnp.concatenate(
            [pltpu.roll(parts[BLOCK:, t * 128 : (t + 1) * 128], 64, 1) for t in range(GRID // SUB)], axis=1
        )
        half = parts[:BLOCK] + jnp.where(real, -turned, turned)
        image[...] = jnp.dot(half.astype(BF16), col[...], preferred_element_type=F32)

        @pl.when(takes_h)
        def _():
            @pl.when(i == 0)
            def _():
                @pl.when(takes)
                def _():
                    phase_out().wait_recv()

                @pl.when(keeps)
                def _():
                    phase_own().wait()

            c, s = sincos(phase[rows, :])
            p_re[...] = c
            p_im[...] = s

        for part in range(BLOCK // CHUNK):
            chunk = i * (BLOCK // CHUNK) + part
            at_rows = chunk_rows(chunk)
            local = pl.ds(part * CHUNK, CHUNK)

            @pl.when(takes_h)
            def _():
                copy_h(chunk).wait_recv()
                f_re = from_h[at_rows, pl.ds(0, GRID)].astype(F32)
                f_im = from_h[at_rows, pl.ds(GRID, GRID)].astype(F32)
                c, s = p_re[local, :], p_im[local, :]
                im_re, im_im = image[local, pl.ds(0, GRID)], image[local, pl.ds(GRID, GRID)]
                mine[at_rows, pl.ds(0, GRID)] = (c * f_re - s * f_im + im_re).astype(BF16)
                mine[at_rows, pl.ds(GRID, GRID)] = (c * f_im + s * f_re + im_im).astype(BF16)

            @pl.when(jnp.logical_not(takes_h))
            def _():
                mine[at_rows, :] = image[local, :].astype(BF16)

            @pl.when(sends_h)
            def _():
                copy_h(chunk).start()

            @pl.when(away)
            def _():
                copy_s(chunk).start()

            @pl.when(jnp.logical_not(away))
            def _():
                out_ref[at_rows, :] = mine[at_rows, :]

        return carry

    lax.fori_loop(0, GRID // BLOCK, work, 0)

    @pl.when(away)
    def _():
        def finish(i, carry):
            copy_s(i).wait_recv()
            out_ref[chunk_rows(i), :] = from_s[chunk_rows(i), :]
            return carry

        lax.fori_loop(0, CHUNKS, finish, 0)

    @pl.when(gives)
    def _():
        phase_out().wait_send()

    def drain(i, carry):
        @pl.when(sends_h)
        def _():
            copy_h(i).wait_send()

        @pl.when(away)
        def _():
            copy_s(i).wait_send()

        return carry

    lax.fori_loop(0, CHUNKS, drain, 0)


def chain(grid, row_table, phase):
    band = (GRID, 2 * GRID)
    return pl.pallas_call(
        chain_kernel,
        out_shape=jax.ShapeDtypeStruct(band, BF16),
        in_specs=[VMEM, VMEM, pl.BlockSpec(memory_space=pl.ANY)],
        out_specs=VMEM,
        scratch_shapes=[
            pltpu.VMEM((2 * GRID, 2 * GRID), BF16),
            pltpu.VMEM((GRID, GRID), F32),
            pltpu.VMEM((BLOCK, GRID), F32),
            pltpu.VMEM((BLOCK, GRID), F32),
            pltpu.VMEM((BLOCK, 2 * GRID), F32),
            pltpu.VMEM(band, BF16),
            pltpu.VMEM(band, BF16),
            pltpu.VMEM(band, BF16),
        ]
        + [pltpu.SemaphoreType.DMA((CHUNKS,))] * 4
        + [pltpu.SemaphoreType.DMA((3,))],
        compiler_params=pltpu.CompilerParams(
            collective_id=1, has_side_effects=True, vmem_limit_bytes=18 << 20
        ),
        name="chain",
    )(grid, row_table, phase)


def dft_rows():
    line = np.arange(GRID)
    angle = (line[:, None] * line[None, :] % GRID) * (2.0 * math.pi / GRID)
    table = np.concatenate([np.cos(angle), np.sin(angle)], axis=1) / math.sqrt(GRID)
    return table.astype(np.float32).astype(ml_dtypes.bfloat16)


def on_device(visibilities, uv_angles, routes, offsets, pixel_phase):
    vis = visibilities.transpose(1, 2, 0).reshape(2 * NVIS, SUBS)
    ang = uv_angles.transpose(1, 2, 0).reshape(2 * NVIS, SUBS)
    recv = route(vis, ang, routes.reshape(1, SUBS), offsets.T)
    grid, row_table = grid_owner(recv.reshape(SUBS * ROWS, 128), jnp.asarray(dft_rows()))
    result = chain(grid, row_table, pixel_phase[0])
    return result.astype(F32).reshape(1, 1, GRID, 2 * GRID)


def solution(mesh):
    in_specs = (
        P(("wa", "facet"), None, None),
        P(("wa", "facet"), None, None),
        P(("wa", "facet"), None),
        P(("wa", "facet"), None),
        P("facet", None, None),
    )
    out_specs = P("wa", "facet", None, None)
    return jax.shard_map(
        on_device, mesh=mesh, in_specs=in_specs, out_specs=out_specs, check_vma=False
    )
```

```python
import functools
import math

import jax
import jax.numpy as jnp
import ml_dtypes
import numpy as np
from jax import lax
from jax.experimental import pallas as pl
from jax.experimental.pallas import tpu as pltpu
from jax.sharding import PartitionSpec as P

SUB = 64
GRID = 512
NVIS = 64
SUBS = 128
CAP = 2
KINDS = 4
ROWS = CAP * KINDS
BLOCK = 64
CHUNK = 32
BLOCKS = GRID // BLOCK
PARTS = BLOCK // CHUNK
CHUNKS = GRID // CHUNK
UNROLL = 8
BF16 = jnp.bfloat16
F32 = jnp.float32
MESH = pl.DeviceIdType.MESH
VMEM = pl.BlockSpec(memory_space=pltpu.VMEM)
HBM = pl.BlockSpec(memory_space=pltpu.HBM)
NT = (((1,), (1,)), ((), ()))


def sincos(x):
    h = x * 0.5
    q = h * h
    s = h + h * q * (
        -1.6666666666666602e-1
        + q * (8.333333333320001e-3
        + q * (-1.9841269829589539e-4
        + q * (2.7557314297030280e-6
        + q * (-2.5050747762850355e-8
        + q * 1.5891812000000000e-10))))
    )
    c = 1.0 + q * (
        -0.5
        + q * (4.16666666666665929218e-2
        + q * (-1.38888888888730564116e-3
        + q * (2.48015872888517045348e-5
        + q * (-2.75573141792967388112e-7
        + q * 2.08757008419747316778e-9))))
    )
    return 1.0 - 2.0 * s * s, 2.0 * s * c


def route_kernel(
    vis_hbm, ang_hbm, route_hbm, off_hbm, phase_hbm, out_ref, p_re, p_im, vis_ref, ang_ref, route_ref, off_ref, phase,
    send, recv, in_sems, send_sem, recv_sem, p_sems,
):
    inputs = [
        pltpu.make_async_copy(source, target, in_sems.at[n])
        for n, (source, target) in enumerate(
            ((route_hbm, route_ref), (off_hbm, off_ref), (ang_hbm, ang_ref), (vis_hbm, vis_ref))
        )
    ]
    for copy in inputs:
        copy.start()

    z, f = lax.axis_index("wa"), lax.axis_index("facet")
    me = z * 32 + f

    low, core = z < 2, f & 1
    takes = (low & (core == 1)) | (jnp.logical_not(low) & (core == 0))

    def phase_own():
        return pltpu.make_async_copy(phase_hbm, phase, p_sems.at[2])

    def phase_out():
        return pltpu.make_async_remote_copy(
            src_ref=phase_hbm, dst_ref=phase, send_sem=p_sems.at[0], recv_sem=p_sems.at[1],
            device_id=(z, f ^ 1), device_id_type=MESH,
        )

    @pl.when(jnp.logical_not(takes))
    def _():
        phase_own().start()

    def each_peer(act):
        def early(i, carry):
            for n in range(5):
                act(me ^ (i * 5 + n) ^ 85)
            return carry

        def late(i, carry):
            for n in range(6):
                act(me ^ (i * 6 + n + 86) ^ 85)
            return carry

        lax.fori_loop(0, 17, early, 0)
        lax.fori_loop(0, 7, late, 0)

    barrier = pltpu.get_barrier_semaphore()
    each_peer(
        lambda to: pl.semaphore_signal(
            barrier, inc=1, device_id=(to >> 5, to & 31), device_id_type=MESH
        )
    )
    for copy in inputs:
        copy.wait()

    owner = route_ref[...]
    facet = owner & 31
    plane = owner >> 5
    odd = facet & 1
    seat = jnp.where(odd == 1, 6, 0)
    seat = jnp.where(plane == 1, jnp.where(odd == 1, 4, 2), seat)
    seat = jnp.where(plane == 2, jnp.where(odd == 1, 5, 3), seat)
    seat = jnp.where(plane == 3, jnp.where(odd == 1, 7, 1), seat)
    device = ((seat >> 1) << 5) + (facet - odd) + (seat & 1)
    owner_b = jnp.broadcast_to(owner.astype(F32), (SUBS, SUBS))
    row_i = lax.broadcasted_iota(jnp.int32, (SUBS, SUBS), 0)
    col_i = lax.broadcasted_iota(jnp.int32, (SUBS, SUBS), 1)
    earlier = jnp.where((owner_b == owner_b.T) & (row_i < col_i), 1.0, 0.0)
    rank = jnp.sum(earlier, axis=0, keepdims=True).astype(jnp.int32)
    slot = device * CAP + rank
    total = SUBS * CAP
    col_key = jnp.concatenate([slot + kind * total for kind in range(KINDS)], axis=1)

    angle = ang_ref[...]
    high = angle.astype(BF16)
    low = (angle - high.astype(F32)).astype(BF16)
    off_u, off_v = off_ref[0:1, :], off_ref[1:2, :]
    meta = jnp.where(row_i == 0, off_u >> 4, 0)
    meta = jnp.where(row_i == 1, off_u & 15, meta)
    meta = jnp.where(row_i == 2, off_v >> 4, meta)
    meta = jnp.where(row_i == 3, off_v & 15, meta)
    meta = meta.astype(F32).astype(BF16)
    data = jnp.concatenate([high, low, vis_ref[...], meta], axis=1)

    for block in range(ROWS):
        row = lax.broadcasted_iota(jnp.int32, (SUBS, KINDS * SUBS), 0) + block * SUBS
        place = row & (ROWS - 1)
        row_key = (place // CAP) * total + (row // ROWS) * CAP + place % CAP
        one_hot = jnp.where(row_key == col_key, 1.0, 0.0).astype(BF16)
        picked = lax.dot_general(one_hot, data, NT, preferred_element_type=F32)
        per = SUBS // ROWS
        send[pl.ds(block * per, per)] = picked.astype(BF16).reshape(per, ROWS, 128)

    pl.semaphore_wait(barrier, SUBS - 1)

    @pl.when(jnp.logical_not(takes))
    def _():
        phase_out().start()

    each_peer(
        lambda to: pltpu.make_async_remote_copy(
            src_ref=send.at[to], dst_ref=recv.at[me], send_sem=send_sem, recv_sem=recv_sem,
            device_id=(to >> 5, to & 31), device_id_type=MESH,
        ).start()
    )
    recv[me] = send[me]

    @pl.when(takes)
    def _():
        phase_out().wait_recv()

    @pl.when(jnp.logical_not(takes))
    def _():
        phase_own().wait()

    def angles(i, carry):
        rows = pl.ds(pl.multiple_of(i * BLOCK, BLOCK), BLOCK)
        c, s = sincos(phase[rows, :])
        p_re[rows, :] = c
        p_im[rows, :] = s
        return carry

    lax.fori_loop(0, BLOCKS, angles, 0)

    others = pl.ds(0, SUBS - 1)
    pltpu.make_async_copy(send.at[others], recv.at[others], recv_sem).wait()
    out_ref[...] = recv[...]
    pltpu.make_async_copy(send.at[others], recv.at[others], send_sem).wait()

    @pl.when(jnp.logical_not(takes))
    def _():
        phase_out().wait_send()


def route(vis, ang, owners, off, phase):
    pixels = jax.ShapeDtypeStruct((GRID, GRID), F32)
    return pl.pallas_call(
        route_kernel,
        out_shape=(jax.ShapeDtypeStruct((SUBS, ROWS, 128), BF16), pixels, pixels),
        in_specs=[HBM] * 5,
        out_specs=(VMEM, VMEM, VMEM),
        scratch_shapes=[
            pltpu.VMEM((2 * NVIS, SUBS), BF16),
            pltpu.VMEM((2 * NVIS, SUBS), F32),
            pltpu.VMEM((1, SUBS), jnp.int32),
            pltpu.VMEM((2, SUBS), jnp.int32),
            pltpu.VMEM((GRID, GRID), F32),
            pltpu.VMEM((SUBS, ROWS, 128), BF16),
            pltpu.VMEM((SUBS, ROWS, 128), BF16),
            pltpu.SemaphoreType.DMA((4,)),
            pltpu.SemaphoreType.DMA,
            pltpu.SemaphoreType.DMA,
            pltpu.SemaphoreType.DMA((3,)),
        ],
        compiler_params=pltpu.CompilerParams(
            collective_id=0, has_side_effects=True, vmem_limit_bytes=10 << 20
        ),
        name="route",
    )(*[pltpu.with_memory_space_constraint(value, pltpu.HBM) for value in (vis, ang, owners, off, phase)])


def complex_mul(a, b):
    return a[0] * b[0] - a[1] * b[1], a[0] * b[1] + a[1] * b[0]


def grid_kernel(
    recv_ref, rows_hbm, grid_ref, rows_ref, wide, pos_v, pos_s, pos_sem, rows_sem, au_r, au_i, av_r, av_i, bu, bv, acc_a, acc_b, lefts, rights, subs
):
    slots = SUBS * CAP
    rows_copy = pltpu.make_async_copy(rows_hbm, rows_ref, rows_sem)
    rows_copy.start()
    wide[...] = recv_ref[...].astype(F32)

    lane8 = lax.broadcasted_iota(jnp.int32, (8, 128), 1)
    weight = jnp.where(lane8 == 0, 8192.0, 0.0)
    weight = jnp.where(lane8 == 1, 512.0, weight)
    weight = jnp.where(lane8 == 2, 16.0, weight)
    weight = jnp.where(lane8 == 3, 1.0, weight).astype(BF16)
    for j in range(CAP):
        meta = wide[pl.ds((KINDS - 1) * CAP + j, SUBS, stride=ROWS), :].astype(BF16)
        packed = lax.dot_general(weight, meta, NT, preferred_element_type=F32)
        pos_v[j] = packed.astype(jnp.int32)
    to_scalar = pltpu.make_async_copy(pos_v, pos_s, pos_sem)
    to_scalar.start()

    lefts[...] = jnp.zeros_like(lefts)
    rights[...] = jnp.zeros_like(rights)
    subs[...] = jnp.zeros_like(subs)

    group = 16
    first = lax.broadcasted_iota(jnp.int32, (group, 128), 1) < 64

    def tables(g, carry):
        clear = pl.ds(pl.multiple_of(g * SUB, SUB), SUB)
        for tile in range(GRID // SUB + 1):
            acc_a[tile, clear, :] = jnp.zeros((SUB, 128), F32)
            acc_b[tile, clear, :] = jnp.zeros((SUB, 128), F32)
        for j in range(CAP):
            start = g * group

            def rows(kind):
                at = start * ROWS + kind * CAP + j
                return wide[pl.ds(at, group, stride=ROWS), :]

            cos_t, sin_t = sincos(rows(0) + rows(1))
            vis = rows(2) * (1.0 / math.sqrt(NVIS))
            cos_o, sin_o = pltpu.roll(cos_t, 64, 1), pltpu.roll(sin_t, 64, 1)
            vis_o = pltpu.roll(vis, 64, 1)
            vis2 = (vis, jnp.where(first, vis_o, -vis_o))
            slot = pl.multiple_of(start + j * SUBS, group)
            for side in range(2):
                if side == 0:
                    e1 = (jnp.where(first, cos_t, cos_o), jnp.where(first, sin_t, sin_o))
                else:
                    e1 = (jnp.where(first, cos_o, cos_t), jnp.where(first, sin_o, sin_t))
                e2 = complex_mul(e1, e1)
                e3 = complex_mul(e2, e1)
                e4 = complex_mul(e2, e2)
                e5 = complex_mul(e4, e1)
                e6 = complex_mul(e4, e2)
                e7 = complex_mul(e4, e3)
                e8 = complex_mul(e4, e4)
                e16 = complex_mul(e8, e8)
                e24 = complex_mul(e16, e8)
                e32 = complex_mul(e16, e16)
                one = (jnp.ones_like(cos_t), jnp.zeros_like(cos_t))
                for a, e in enumerate((one, e1, e2, e3, e4, e5, e6, e7)):
                    where = pl.ds(slot * 8 + a, group, stride=8)
                    if side == 0:
                        re, im = complex_mul(e, vis2)
                        au_r[where, :] = re
                        au_i[where, :] = im
                    else:
                        av_r[where, :] = jnp.where(first, e[0], -e[1])
                        av_i[where, :] = jnp.where(first, e[1], e[0])
                steps = bu if side == 0 else bv
                for b, e in enumerate((e8, e16, e24, e32)):
                    steps[2 * b, pl.ds(slot, group), :] = e[0]
                    steps[2 * b + 1, pl.ds(slot, group), :] = e[1]
        return carry

    lax.fori_loop(0, SUBS // group, tables, 0)
    to_scalar.wait()

    lane_in = lax.broadcasted_iota(jnp.int32, (SUB, 128), 1) & 63

    def form(n, slot):
        base = pl.multiple_of(slot * 8, 8)
        ur, ui = au_r[pl.ds(base, 8), :], au_i[pl.ds(base, 8), :]
        vr, vi = av_r[pl.ds(base, 8), :], av_i[pl.ds(base, 8), :]

        def step(table, b):
            return table[2 * b, pl.ds(slot, 1), :], table[2 * b + 1, pl.ds(slot, 1), :]

        left = [None] * 8
        right_r = [None] * 8
        right_i = [None] * 8
        left[4], right_r[4], right_i[4] = ur, vr, vi
        for b in range(4):
            br, bi = step(bu, b)
            x, y = br * ur, bi * ui
            left[3 - b] = x + y
            if b < 3:
                left[5 + b] = x - y
            br, bi = step(bv, b)
            x, y, z, w = br * vr, bi * vi, br * vi, bi * vr
            right_r[3 - b] = x + y
            right_i[3 - b] = z - w
            if b < 3:
                right_r[5 + b] = x - y
                right_i[5 + b] = z + w
        lefts[n] = jnp.concatenate(left, axis=0).astype(BF16)
        rights[n] = jnp.concatenate(right_r + right_i, axis=0).astype(BF16)

    nought = jnp.zeros((SUB, 128), BF16)

    def multiply(n):
        left = jnp.concatenate(
            [jnp.concatenate([lefts[n], nought], axis=1), jnp.concatenate([nought, lefts[n + 1]], axis=1)],
            axis=0,
        )
        right = jnp.concatenate([rights[n], rights[n + 1]], axis=1)
        subs[n // 2] = lax.dot_general(left, right, NT, preferred_element_type=F32).astype(BF16)

    def place(slot, sub, acc):
        packed = pos_s[slot >> 7, 0, slot & (SUBS - 1)]
        off_u, off_v = packed >> 9, packed & 511
        tile, shift = off_v >> 6, off_v & 63
        rows = pl.ds(off_u, SUB)
        here, there = acc.at[tile, rows, :], acc.at[tile + 1, rows, :]
        near = here[...] + pltpu.roll(sub, shift, 1).astype(F32)
        far = there[...] + pltpu.roll(sub, shift + 64, 1).astype(F32)
        pltpu.store(here, near, mask=lane_in >= shift)
        pltpu.store(there, far, mask=lane_in < shift)

    def place_all(start):
        for n in range(UNROLL):
            sub = subs[n // 2, pl.ds(n % 2 * SUB, SUB), :]
            place(start + n, sub, (acc_a, acc_b)[n % 2])

    def multiply_all():
        for n in range(0, UNROLL, 2):
            multiply(n)

    def work(i, carry):
        place_all(jnp.maximum(i - 2, 0) * UNROLL)
        multiply_all()
        for n in range(UNROLL):
            form(n, i * UNROLL + n)
        return carry

    lax.fori_loop(0, slots // UNROLL, work, 0)
    place_all(slots - 2 * UNROLL)
    multiply_all()
    place_all(slots - UNROLL)

    def finish(g, carry):
        rows = pl.ds(pl.multiple_of(g * SUB, SUB), SUB)
        for tile in range(GRID // SUB):
            grid_ref[rows, pl.ds(tile * 128, 128)] = (acc_a[tile, rows, :] + acc_b[tile, rows, :]).astype(BF16)
        return carry

    lax.fori_loop(0, GRID // SUB, finish, 0)
    rows_copy.wait()


def grid_owner(recv, row_table):
    slots = SUBS * CAP
    band = jax.ShapeDtypeStruct((GRID, 2 * GRID), BF16)
    return pl.pallas_call(
        grid_kernel,
        out_shape=(band, band),
        in_specs=[VMEM, HBM],
        out_specs=(VMEM, VMEM),
        scratch_shapes=[
            pltpu.VMEM((SUBS * ROWS, 128), F32),
            pltpu.VMEM((CAP, 8, 128), jnp.int32),
            pltpu.SMEM((CAP, 8, 128), jnp.int32),
            pltpu.SemaphoreType.DMA,
            pltpu.SemaphoreType.DMA,
        ]
        + [pltpu.VMEM((slots * 8, 128), F32)] * 4
        + [pltpu.VMEM((8, slots, 128), F32)] * 2
        + [pltpu.VMEM((GRID // SUB + 1, GRID, 128), F32)] * 2
        + [
            pltpu.VMEM((UNROLL, SUB, 128), BF16),
            pltpu.VMEM((UNROLL, 2 * SUB, 128), BF16),
            pltpu.VMEM((UNROLL // 2, 2 * SUB, 128), BF16),
        ],
        compiler_params=pltpu.CompilerParams(vmem_limit_bytes=22 << 20),
        name="grid",
    )(recv, pltpu.with_memory_space_constraint(row_table, pltpu.HBM))


def chain_kernel(
    grid_ref, row_ref, p_re, p_im, out_ref, col, image, from_h, from_s, from_x, mine, other,
    h_recv, s_recv, x_recv, h_send, s_send, x_send,
):
    z, f = lax.axis_index("wa"), lax.axis_index("facet")
    core = f & 1
    seat = 2 * z + core
    pair = f - core

    def at(other_seat):
        return (other_seat >> 1, pair + (other_seat & 1))

    def is_seat(*seats):
        hit = seat == seats[0]
        for other in seats[1:]:
            hit = jnp.logical_or(hit, seat == other)
        return hit

    barrier = pltpu.get_barrier_semaphore()
    for step in range(1, 8):
        pl.semaphore_signal(barrier, inc=1, device_id=at((seat + step) & 7), device_id_type=MESH)

    for tile in range(GRID // SUB):
        rows = row_ref[pl.ds(tile * SUB, SUB), :]
        col[pl.ds(tile * 128, SUB), :] = rows
        col[pl.ds(tile * 128 + SUB, SUB), pl.ds(0, GRID)] = -rows[:, GRID:]
        col[pl.ds(tile * 128 + SUB, SUB), pl.ds(GRID, GRID)] = rows[:, :GRID]

    real = lax.broadcasted_iota(jnp.int32, (BLOCK, 2 * GRID), 1) & 127 < 64

    def block_rows(i):
        return pl.ds(pl.multiple_of(i * BLOCK, BLOCK), BLOCK)

    def chunk_rows(i):
        return pl.ds(pl.multiple_of(i * CHUNK, CHUNK), CHUNK)

    def transform(i):
        rows = block_rows(i)
        both = jnp.concatenate([row_ref[rows, pl.ds(0, GRID)], row_ref[rows, pl.ds(GRID, GRID)]], axis=0)
        parts = jnp.dot(both, grid_ref[...], preferred_element_type=F32)
        turned = jnp.concatenate(
            [pltpu.roll(parts[BLOCK:, t * 128 : (t + 1) * 128], 64, 1) for t in range(GRID // SUB)], axis=1
        )
        half = parts[:BLOCK] + jnp.where(real, -turned, turned)
        image[rows, :] = jnp.dot(half.astype(BF16), col[...], preferred_element_type=F32)

    transform(0)
    pl.semaphore_wait(barrier, 7)

    to_h = jnp.where(seat == 0, 2, jnp.where(seat == 2, 3, jnp.where(seat == 3, 1,
           jnp.where(seat == 6, 4, jnp.where(seat == 4, 5, 7)))))
    to_s = jnp.where(seat == 1, 6, jnp.where(seat == 3, 4, jnp.where(seat == 4, 3, 1)))
    sends_h = is_seat(0, 2, 3, 4, 5, 6)
    takes_h = is_seat(1, 2, 3, 4, 5, 7)
    sends_x = is_seat(0, 2)
    away = is_seat(1, 3, 4, 6)
    lag = jnp.where(is_seat(2, 4), 1, 3)

    def copy_h(i, source=mine):
        rows = chunk_rows(i)
        return pltpu.make_async_remote_copy(
            src_ref=source.at[rows], dst_ref=from_h.at[rows], send_sem=h_send.at[i], recv_sem=h_recv.at[i],
            device_id=at(to_h), device_id_type=MESH,
        )

    def copy_x(i, source=mine):
        rows = chunk_rows(i)
        return pltpu.make_async_remote_copy(
            src_ref=source.at[rows], dst_ref=from_x.at[rows], send_sem=x_send.at[i], recv_sem=x_recv.at[i],
            device_id=at(seat | 1), device_id_type=MESH,
        )

    def copy_s(i):
        rows = chunk_rows(i)
        return pltpu.make_async_remote_copy(
            src_ref=mine.at[rows], dst_ref=from_s.at[rows], send_sem=s_send.at[i], recv_sem=s_recv.at[i],
            device_id=at(to_s), device_id_type=MESH,
        )

    def turn(rows, re, im):
        c, s = p_re[rows, :], p_im[rows, :]
        return c * re - s * im, c * im + s * re

    def halves(ref, rows):
        return ref[rows, pl.ds(0, GRID)].astype(F32), ref[rows, pl.ds(GRID, GRID)].astype(F32)

    def keep(ref, rows, re, im):
        ref[rows, pl.ds(0, GRID)] = re.astype(BF16)
        ref[rows, pl.ds(GRID, GRID)] = im.astype(BF16)

    def plus(rows, ref, pair_in):
        re, im = halves(ref, rows)
        return pair_in[0] + re, pair_in[1] + im

    def work(t, carry):
        @pl.when(t < BLOCKS)
        def _():
            @pl.when(is_seat(0, 6))
            def _():
                for part in range(PARTS):
                    i = t * PARTS + part
                    mine[chunk_rows(i), :] = image[chunk_rows(i), :].astype(BF16)
                    copy_h(i).start()

                    @pl.when(seat == 0)
                    def _():
                        copy_x(i).start()
                        out_ref[chunk_rows(i), :] = mine[chunk_rows(i), :]

                    @pl.when(seat == 6)
                    def _():
                        copy_s(i).start()

            @pl.when(seat == 2)
            def _():
                for part in range(PARTS):
                    i = t * PARTS + part
                    other[chunk_rows(i), :] = image[chunk_rows(i), :].astype(BF16)
                    copy_x(i, other).start()

            @pl.when(t < BLOCKS - 1)
            def _():
                transform(t + 1)

            @pl.when(seat == 3)
            def _():
                for part in range(PARTS):
                    i = t * PARTS + part
                    rows = chunk_rows(i)
                    copy_x(i).wait_recv()
                    keep(other, rows, *plus(rows, image, turn(rows, *halves(from_x, rows))))
                    copy_h(i, other).start()

        block = t - lag

        @pl.when(takes_h & (block >= 0) & (block < BLOCKS))
        def _():
            for part in range(PARTS):
                i = block * PARTS + part
                rows = chunk_rows(i)

                @pl.when(seat == 1)
                def _():
                    copy_x(i).wait_recv()
                    twice = turn(rows, *turn(rows, *halves(from_x, rows)))
                    copy_h(i).wait_recv()
                    keep(mine, rows, *plus(rows, image, turn(rows, *plus(rows, from_h, twice))))

                @pl.when(seat != 1)
                def _():
                    copy_h(i).wait_recv()
                    keep(mine, rows, *plus(rows, image, turn(rows, *halves(from_h, rows))))

                @pl.when(is_seat(2, 4, 5))
                def _():
                    copy_h(i).start()

                @pl.when(is_seat(1, 3, 4))
                def _():
                    copy_s(i).start()

                @pl.when(is_seat(2, 5, 7))
                def _():
                    out_ref[rows, :] = mine[rows, :]

        return carry

    lax.fori_loop(0, BLOCKS + 3, work, 0)

    @pl.when(away)
    def _():
        def finish(i, carry):
            copy_s(i).wait_recv()
            out_ref[chunk_rows(i), :] = from_s[chunk_rows(i), :]
            return carry

        lax.fori_loop(0, CHUNKS, finish, 0)

    def drain(i, carry):
        @pl.when(sends_h)
        def _():
            copy_h(i).wait_send()

        @pl.when(sends_x)
        def _():
            copy_x(i).wait_send()

        @pl.when(away)
        def _():
            copy_s(i).wait_send()

        return carry

    lax.fori_loop(0, CHUNKS, drain, 0)


def chain(grid, row_table, p_re, p_im):
    band = (GRID, 2 * GRID)
    return pl.pallas_call(
        chain_kernel,
        out_shape=jax.ShapeDtypeStruct(band, BF16),
        in_specs=[VMEM] * 4,
        out_specs=VMEM,
        scratch_shapes=[
            pltpu.VMEM((2 * GRID, 2 * GRID), BF16),
            pltpu.VMEM(band, F32),
        ]
        + [pltpu.VMEM(band, BF16)] * 5
        + [pltpu.SemaphoreType.DMA((CHUNKS,))] * 6,
        compiler_params=pltpu.CompilerParams(
            collective_id=1, has_side_effects=True, vmem_limit_bytes=24 << 20
        ),
        name="chain",
    )(grid, row_table, p_re, p_im)


def dft_rows():
    line = np.arange(GRID)
    angle = (line[:, None] * line[None, :] % GRID) * (2.0 * math.pi / GRID)
    table = np.concatenate([np.cos(angle), np.sin(angle)], axis=1) / math.sqrt(GRID)
    return table.astype(np.float32).astype(ml_dtypes.bfloat16)


def on_device(visibilities, uv_angles, routes, offsets, pixel_phase):
    vis = visibilities.transpose(1, 2, 0).reshape(2 * NVIS, SUBS)
    ang = uv_angles.transpose(1, 2, 0).reshape(2 * NVIS, SUBS)
    recv, p_re, p_im = route(vis, ang, routes.reshape(1, SUBS), offsets.T, pixel_phase[0])
    grid, row_table = grid_owner(recv.reshape(SUBS * ROWS, 128), jnp.asarray(dft_rows()))
    result = chain(grid, row_table, p_re, p_im)
    return result.astype(F32).reshape(1, 1, GRID, 2 * GRID)


def solution(mesh):
    in_specs = (
        P(("wa", "facet"), None, None),
        P(("wa", "facet"), None, None),
        P(("wa", "facet"), None),
        P(("wa", "facet"), None),
        P("facet", None, None),
    )
    out_specs = P("wa", "facet", None, None)
    return jax.shard_map(
        on_device, mesh=mesh, in_specs=in_specs, out_specs=out_specs, check_vma=False
    )
```

```python
import functools
import math

import jax
import jax.numpy as jnp
import ml_dtypes
import numpy as np
from jax import lax
from jax.experimental import pallas as pl
from jax.experimental.pallas import tpu as pltpu
from jax.sharding import PartitionSpec as P

SUB = 64
GRID = 512
NVIS = 64
SUBS = 128
CAP = 2
KINDS = 4
ROWS = CAP * KINDS
BLOCK = 64
CHUNK = 32
BLOCKS = GRID // BLOCK
PARTS = BLOCK // CHUNK
CHUNKS = GRID // CHUNK
UNROLL = 32
BF16 = jnp.bfloat16
F32 = jnp.float32
MESH = pl.DeviceIdType.MESH
VMEM = pl.BlockSpec(memory_space=pltpu.VMEM)
HBM = pl.BlockSpec(memory_space=pltpu.HBM)
NT = (((1,), (1,)), ((), ()))


def sincos(x):
    h = x * 0.5
    q = h * h
    s = h + h * q * (
        -1.6666666666666602e-1
        + q * (8.333333333320001e-3
        + q * (-1.9841269829589539e-4
        + q * (2.7557314297030280e-6
        + q * (-2.5050747762850355e-8
        + q * 1.5891812000000000e-10))))
    )
    c = 1.0 + q * (
        -0.5
        + q * (4.16666666666665929218e-2
        + q * (-1.38888888888730564116e-3
        + q * (2.48015872888517045348e-5
        + q * (-2.75573141792967388112e-7
        + q * 2.08757008419747316778e-9))))
    )
    return 1.0 - 2.0 * s * s, 2.0 * s * c


def route_kernel(
    vis_hbm, ang_hbm, route_hbm, off_hbm, phase_hbm, out_ref, p_re, p_im, vis_ref, ang_ref, route_ref, off_ref, phase,
    send, recv, in_sems, send_sem, recv_sem, p_sems,
):
    inputs = [
        pltpu.make_async_copy(source, target, in_sems.at[n])
        for n, (source, target) in enumerate(
            ((route_hbm, route_ref), (off_hbm, off_ref), (ang_hbm, ang_ref), (vis_hbm, vis_ref))
        )
    ]
    for copy in inputs:
        copy.start()

    z, f = lax.axis_index("wa"), lax.axis_index("facet")
    me = z * 32 + f

    low, core = z < 2, f & 1
    takes = (low & (core == 1)) | (jnp.logical_not(low) & (core == 0))

    def phase_own():
        return pltpu.make_async_copy(phase_hbm, phase, p_sems.at[2])

    def phase_out():
        return pltpu.make_async_remote_copy(
            src_ref=phase_hbm, dst_ref=phase, send_sem=p_sems.at[0], recv_sem=p_sems.at[1],
            device_id=(z, f ^ 1), device_id_type=MESH,
        )

    @pl.when(jnp.logical_not(takes))
    def _():
        phase_own().start()

    def each_peer(act):
        def early(i, carry):
            for n in range(5):
                act(me ^ (i * 5 + n) ^ 85)
            return carry

        def late(i, carry):
            for n in range(6):
                act(me ^ (i * 6 + n + 86) ^ 85)
            return carry

        lax.fori_loop(0, 17, early, 0)
        lax.fori_loop(0, 7, late, 0)

    barrier = pltpu.get_barrier_semaphore()
    each_peer(
        lambda to: pl.semaphore_signal(
            barrier, inc=1, device_id=(to >> 5, to & 31), device_id_type=MESH
        )
    )
    for copy in inputs:
        copy.wait()

    owner = route_ref[...]
    facet = owner & 31
    plane = owner >> 5
    odd = facet & 1
    seat = jnp.where(odd == 1, 6, 0)
    seat = jnp.where(plane == 1, jnp.where(odd == 1, 4, 2), seat)
    seat = jnp.where(plane == 2, jnp.where(odd == 1, 5, 3), seat)
    seat = jnp.where(plane == 3, jnp.where(odd == 1, 7, 1), seat)
    device = ((seat >> 1) << 5) + (facet - odd) + (seat & 1)
    owner_b = jnp.broadcast_to(owner.astype(F32), (SUBS, SUBS))
    row_i = lax.broadcasted_iota(jnp.int32, (SUBS, SUBS), 0)
    col_i = lax.broadcasted_iota(jnp.int32, (SUBS, SUBS), 1)
    earlier = jnp.where((owner_b == owner_b.T) & (row_i < col_i), 1.0, 0.0)
    rank = jnp.sum(earlier, axis=0, keepdims=True).astype(jnp.int32)
    slot = device * CAP + rank
    total = SUBS * CAP
    col_key = jnp.concatenate([slot + kind * total for kind in range(KINDS)], axis=1)

    angle = ang_ref[...]
    high = angle.astype(BF16)
    low = (angle - high.astype(F32)).astype(BF16)
    off_u, off_v = off_ref[0:1, :], off_ref[1:2, :]
    meta = jnp.where(row_i == 0, off_u >> 4, 0)
    meta = jnp.where(row_i == 1, off_u & 15, meta)
    meta = jnp.where(row_i == 2, off_v >> 4, meta)
    meta = jnp.where(row_i == 3, off_v & 15, meta)
    meta = meta.astype(F32).astype(BF16)
    data = jnp.concatenate([high, low, vis_ref[...], meta], axis=1)

    for block in range(ROWS):
        row = lax.broadcasted_iota(jnp.int32, (SUBS, KINDS * SUBS), 0) + block * SUBS
        place = row & (ROWS - 1)
        row_key = (place // CAP) * total + (row // ROWS) * CAP + place % CAP
        one_hot = jnp.where(row_key == col_key, 1.0, 0.0).astype(BF16)
        picked = lax.dot_general(one_hot, data, NT, preferred_element_type=F32)
        per = SUBS // ROWS
        send[pl.ds(block * per, per)] = picked.astype(BF16).reshape(per, ROWS, 128)

    pl.semaphore_wait(barrier, SUBS - 1)

    @pl.when(jnp.logical_not(takes))
    def _():
        phase_out().start()

    each_peer(
        lambda to: pltpu.make_async_remote_copy(
            src_ref=send.at[to], dst_ref=recv.at[me], send_sem=send_sem, recv_sem=recv_sem,
            device_id=(to >> 5, to & 31), device_id_type=MESH,
        ).start()
    )
    recv[me] = send[me]

    @pl.when(takes)
    def _():
        phase_out().wait_recv()

    @pl.when(jnp.logical_not(takes))
    def _():
        phase_own().wait()

    def angles(i, carry):
        rows = pl.ds(pl.multiple_of(i * BLOCK, BLOCK), BLOCK)
        c, s = sincos(phase[rows, :])
        p_re[rows, :] = c
        p_im[rows, :] = s
        return carry

    lax.fori_loop(0, BLOCKS, angles, 0)

    others = pl.ds(0, SUBS - 1)
    pltpu.make_async_copy(send.at[others], recv.at[others], recv_sem).wait()
    out_ref[...] = recv[...]
    pltpu.make_async_copy(send.at[others], recv.at[others], send_sem).wait()

    @pl.when(jnp.logical_not(takes))
    def _():
        phase_out().wait_send()


def route(vis, ang, owners, off, phase):
    pixels = jax.ShapeDtypeStruct((GRID, GRID), F32)
    return pl.pallas_call(
        route_kernel,
        out_shape=(jax.ShapeDtypeStruct((SUBS, ROWS, 128), BF16), pixels, pixels),
        in_specs=[HBM] * 5,
        out_specs=(VMEM, VMEM, VMEM),
        scratch_shapes=[
            pltpu.VMEM((2 * NVIS, SUBS), BF16),
            pltpu.VMEM((2 * NVIS, SUBS), F32),
            pltpu.VMEM((1, SUBS), jnp.int32),
            pltpu.VMEM((2, SUBS), jnp.int32),
            pltpu.VMEM((GRID, GRID), F32),
            pltpu.VMEM((SUBS, ROWS, 128), BF16),
            pltpu.VMEM((SUBS, ROWS, 128), BF16),
            pltpu.SemaphoreType.DMA((4,)),
            pltpu.SemaphoreType.DMA,
            pltpu.SemaphoreType.DMA,
            pltpu.SemaphoreType.DMA((3,)),
        ],
        compiler_params=pltpu.CompilerParams(
            collective_id=0, has_side_effects=True, vmem_limit_bytes=10 << 20
        ),
        name="route",
    )(*[pltpu.with_memory_space_constraint(value, pltpu.HBM) for value in (vis, ang, owners, off, phase)])


def complex_mul(a, b):
    return a[0] * b[0] - a[1] * b[1], a[0] * b[1] + a[1] * b[0]


def grid_kernel(
    recv_ref, rows_hbm, grid_ref, rows_ref, wide, pos_v, pos_s, pos_sem, rows_sem, au_r, au_i, av_r, av_i, bu, bv, acc_a, acc_b, lefts, rights, subs
):
    slots = SUBS * CAP
    rows_copy = pltpu.make_async_copy(rows_hbm, rows_ref, rows_sem)
    rows_copy.start()
    wide[...] = recv_ref[...].astype(F32)

    lane8 = lax.broadcasted_iota(jnp.int32, (8, 128), 1)
    weight = jnp.where(lane8 == 0, 8192.0, 0.0)
    weight = jnp.where(lane8 == 1, 512.0, weight)
    weight = jnp.where(lane8 == 2, 16.0, weight)
    weight = jnp.where(lane8 == 3, 1.0, weight).astype(BF16)
    for j in range(CAP):
        meta = wide[pl.ds((KINDS - 1) * CAP + j, SUBS, stride=ROWS), :].astype(BF16)
        packed = lax.dot_general(weight, meta, NT, preferred_element_type=F32)
        pos_v[j] = packed.astype(jnp.int32)
    to_scalar = pltpu.make_async_copy(pos_v, pos_s, pos_sem)
    to_scalar.start()

    lefts[...] = jnp.zeros_like(lefts)
    rights[...] = jnp.zeros_like(rights)
    subs[...] = jnp.zeros_like(subs)

    group = 16
    first = lax.broadcasted_iota(jnp.int32, (group, 128), 1) < 64

    def tables(g, carry):
        clear = pl.ds(pl.multiple_of(g * SUB, SUB), SUB)
        for tile in range(GRID // SUB + 1):
            acc_a[tile, clear, :] = jnp.zeros((SUB, 128), F32)
            acc_b[tile, clear, :] = jnp.zeros((SUB, 128), F32)
        for j in range(CAP):
            start = g * group

            def rows(kind):
                at = start * ROWS + kind * CAP + j
                return wide[pl.ds(at, group, stride=ROWS), :]

            cos_t, sin_t = sincos(rows(0) + rows(1))
            vis = rows(2) * (1.0 / math.sqrt(NVIS))
            cos_o, sin_o = pltpu.roll(cos_t, 64, 1), pltpu.roll(sin_t, 64, 1)
            vis_o = pltpu.roll(vis, 64, 1)
            vis2 = (vis, jnp.where(first, vis_o, -vis_o))
            slot = pl.multiple_of(start + j * SUBS, group)
            for side in range(2):
                if side == 0:
                    e1 = (jnp.where(first, cos_t, cos_o), jnp.where(first, sin_t, sin_o))
                else:
                    e1 = (jnp.where(first, cos_o, cos_t), jnp.where(first, sin_o, sin_t))
                e2 = complex_mul(e1, e1)
                e3 = complex_mul(e2, e1)
                e4 = complex_mul(e2, e2)
                e5 = complex_mul(e4, e1)
                e6 = complex_mul(e4, e2)
                e7 = complex_mul(e4, e3)
                e8 = complex_mul(e4, e4)
                e16 = complex_mul(e8, e8)
                e24 = complex_mul(e16, e8)
                e32 = complex_mul(e16, e16)
                one = (jnp.ones_like(cos_t), jnp.zeros_like(cos_t))
                for a, e in enumerate((one, e1, e2, e3, e4, e5, e6, e7)):
                    where = pl.ds(slot * 8 + a, group, stride=8)
                    if side == 0:
                        re, im = complex_mul(e, vis2)
                        au_r[where, :] = re
                        au_i[where, :] = im
                    else:
                        av_r[where, :] = jnp.where(first, e[0], -e[1])
                        av_i[where, :] = jnp.where(first, e[1], e[0])
                steps = bu if side == 0 else bv
                for b, e in enumerate((e8, e16, e24, e32)):
                    steps[2 * b, pl.ds(slot, group), :] = e[0]
                    steps[2 * b + 1, pl.ds(slot, group), :] = e[1]
        return carry

    lax.fori_loop(0, SUBS // group, tables, 0)
    to_scalar.wait()

    lane_in = lax.broadcasted_iota(jnp.int32, (SUB, 128), 1) & 63

    def form(n, slot):
        base = pl.multiple_of(slot * 8, 8)
        ur, ui = au_r[pl.ds(base, 8), :], au_i[pl.ds(base, 8), :]
        vr, vi = av_r[pl.ds(base, 8), :], av_i[pl.ds(base, 8), :]

        def step(table, b):
            return table[2 * b, pl.ds(slot, 1), :], table[2 * b + 1, pl.ds(slot, 1), :]

        left = [None] * 8
        right_r = [None] * 8
        right_i = [None] * 8
        left[4], right_r[4], right_i[4] = ur, vr, vi
        for b in range(4):
            br, bi = step(bu, b)
            x, y = br * ur, bi * ui
            left[3 - b] = x + y
            if b < 3:
                left[5 + b] = x - y
            br, bi = step(bv, b)
            x, y, z, w = br * vr, bi * vi, br * vi, bi * vr
            right_r[3 - b] = x + y
            right_i[3 - b] = z - w
            if b < 3:
                right_r[5 + b] = x - y
                right_i[5 + b] = z + w
        lefts[n] = jnp.concatenate(left, axis=0).astype(BF16)
        rights[n] = jnp.concatenate(right_r + right_i, axis=0).astype(BF16)

    nought = jnp.zeros((SUB, 128), BF16)

    def multiply(n):
        left = jnp.concatenate(
            [jnp.concatenate([lefts[n], nought], axis=1), jnp.concatenate([nought, lefts[n + 1]], axis=1)],
            axis=0,
        )
        right = jnp.concatenate([rights[n], rights[n + 1]], axis=1)
        subs[n // 2] = lax.dot_general(left, right, NT, preferred_element_type=F32).astype(BF16)

    def place(slot, sub, acc):
        packed = pos_s[slot >> 7, 0, slot & (SUBS - 1)]
        off_u, off_v = packed >> 9, packed & 511
        tile, shift = off_v >> 6, off_v & 63
        rows = pl.ds(off_u, SUB)
        here, there = acc.at[tile, rows, :], acc.at[tile + 1, rows, :]
        near = here[...] + pltpu.roll(sub, shift, 1).astype(F32)
        far = there[...] + pltpu.roll(sub, shift + 64, 1).astype(F32)
        pltpu.store(here, near, mask=lane_in >= shift)
        pltpu.store(there, far, mask=lane_in < shift)

    def place_all(start):
        for n in range(UNROLL):
            sub = subs[n // 2, pl.ds(n % 2 * SUB, SUB), :]
            place(start + n, sub, (acc_a, acc_b)[n % 2])

    def multiply_all():
        for n in range(0, UNROLL, 2):
            multiply(n)

    def work(i, carry):
        place_all(jnp.maximum(i - 2, 0) * UNROLL)
        multiply_all()
        for n in range(UNROLL):
            form(n, i * UNROLL + n)
        return carry

    lax.fori_loop(0, slots // UNROLL, work, 0)
    place_all(slots - 2 * UNROLL)
    multiply_all()
    place_all(slots - UNROLL)

    def finish(g, carry):
        rows = pl.ds(pl.multiple_of(g * SUB, SUB), SUB)
        for tile in range(GRID // SUB):
            grid_ref[rows, pl.ds(tile * 128, 128)] = (acc_a[tile, rows, :] + acc_b[tile, rows, :]).astype(BF16)
        return carry

    lax.fori_loop(0, GRID // SUB, finish, 0)
    rows_copy.wait()


def grid_owner(recv, row_table):
    slots = SUBS * CAP
    band = jax.ShapeDtypeStruct((GRID, 2 * GRID), BF16)
    return pl.pallas_call(
        grid_kernel,
        out_shape=(band, band),
        in_specs=[VMEM, HBM],
        out_specs=(VMEM, VMEM),
        scratch_shapes=[
            pltpu.VMEM((SUBS * ROWS, 128), F32),
            pltpu.VMEM((CAP, 8, 128), jnp.int32),
            pltpu.SMEM((CAP, 8, 128), jnp.int32),
            pltpu.SemaphoreType.DMA,
            pltpu.SemaphoreType.DMA,
        ]
        + [pltpu.VMEM((slots * 8, 128), F32)] * 4
        + [pltpu.VMEM((8, slots, 128), F32)] * 2
        + [pltpu.VMEM((GRID // SUB + 1, GRID, 128), F32)] * 2
        + [
            pltpu.VMEM((UNROLL, SUB, 128), BF16),
            pltpu.VMEM((UNROLL, 2 * SUB, 128), BF16),
            pltpu.VMEM((UNROLL // 2, 2 * SUB, 128), BF16),
        ],
        compiler_params=pltpu.CompilerParams(vmem_limit_bytes=22 << 20),
        name="grid",
    )(recv, pltpu.with_memory_space_constraint(row_table, pltpu.HBM))


def chain_kernel(
    grid_ref, row_ref, p_re, p_im, out_ref, col, image, from_h, from_s, from_x, mine, other,
    h_recv, s_recv, x_recv, h_send, s_send, x_send,
):
    z, f = lax.axis_index("wa"), lax.axis_index("facet")
    core = f & 1
    seat = 2 * z + core
    pair = f - core

    def at(other_seat):
        return (other_seat >> 1, pair + (other_seat & 1))

    def is_seat(*seats):
        hit = seat == seats[0]
        for other in seats[1:]:
            hit = jnp.logical_or(hit, seat == other)
        return hit

    barrier = pltpu.get_barrier_semaphore()
    for step in range(1, 8):
        pl.semaphore_signal(barrier, inc=1, device_id=at((seat + step) & 7), device_id_type=MESH)

    for tile in range(GRID // SUB):
        rows = row_ref[pl.ds(tile * SUB, SUB), :]
        col[pl.ds(tile * 128, SUB), :] = rows
        col[pl.ds(tile * 128 + SUB, SUB), pl.ds(0, GRID)] = -rows[:, GRID:]
        col[pl.ds(tile * 128 + SUB, SUB), pl.ds(GRID, GRID)] = rows[:, :GRID]

    real = lax.broadcasted_iota(jnp.int32, (BLOCK, 2 * GRID), 1) & 127 < 64

    def block_rows(i):
        return pl.ds(pl.multiple_of(i * BLOCK, BLOCK), BLOCK)

    def chunk_rows(i):
        return pl.ds(pl.multiple_of(i * CHUNK, CHUNK), CHUNK)

    def transform(i):
        rows = block_rows(i)
        both = jnp.concatenate([row_ref[rows, pl.ds(0, GRID)], row_ref[rows, pl.ds(GRID, GRID)]], axis=0)
        parts = jnp.dot(both, grid_ref[...], preferred_element_type=F32)
        turned = jnp.concatenate(
            [pltpu.roll(parts[BLOCK:, t * 128 : (t + 1) * 128], 64, 1) for t in range(GRID // SUB)], axis=1
        )
        half = parts[:BLOCK] + jnp.where(real, -turned, turned)
        image[rows, :] = jnp.dot(half.astype(BF16), col[...], preferred_element_type=F32)

    transform(0)
    pl.semaphore_wait(barrier, 7)

    to_h = jnp.where(seat == 0, 2, jnp.where(seat == 2, 3, jnp.where(seat == 3, 1,
           jnp.where(seat == 6, 4, jnp.where(seat == 4, 5, 7)))))
    to_s = jnp.where(seat == 1, 6, jnp.where(seat == 3, 4, jnp.where(seat == 4, 3, 1)))
    sends_h = is_seat(0, 2, 3, 4, 5, 6)
    takes_h = is_seat(1, 2, 3, 4, 5, 7)
    sends_x = is_seat(0, 2)
    away = is_seat(1, 3, 4, 6)
    lag = jnp.where(is_seat(2, 4), 1, 3)

    def copy_h(i, source=mine):
        rows = chunk_rows(i)
        return pltpu.make_async_remote_copy(
            src_ref=source.at[rows], dst_ref=from_h.at[rows], send_sem=h_send.at[i], recv_sem=h_recv.at[i],
            device_id=at(to_h), device_id_type=MESH,
        )

    def copy_x(i, source=mine):
        rows = chunk_rows(i)
        return pltpu.make_async_remote_copy(
            src_ref=source.at[rows], dst_ref=from_x.at[rows], send_sem=x_send.at[i], recv_sem=x_recv.at[i],
            device_id=at(seat | 1), device_id_type=MESH,
        )

    def copy_s(i):
        rows = chunk_rows(i)
        return pltpu.make_async_remote_copy(
            src_ref=mine.at[rows], dst_ref=from_s.at[rows], send_sem=s_send.at[i], recv_sem=s_recv.at[i],
            device_id=at(to_s), device_id_type=MESH,
        )

    def turn(rows, re, im):
        c, s = p_re[rows, :], p_im[rows, :]
        return c * re - s * im, c * im + s * re

    def halves(ref, rows):
        return ref[rows, pl.ds(0, GRID)].astype(F32), ref[rows, pl.ds(GRID, GRID)].astype(F32)

    def keep(ref, rows, re, im):
        ref[rows, pl.ds(0, GRID)] = re.astype(BF16)
        ref[rows, pl.ds(GRID, GRID)] = im.astype(BF16)

    def plus(rows, ref, pair_in):
        re, im = halves(ref, rows)
        return pair_in[0] + re, pair_in[1] + im

    def work(t, carry):
        @pl.when(t < BLOCKS)
        def _():
            @pl.when(is_seat(0, 6))
            def _():
                for part in range(PARTS):
                    i = t * PARTS + part
                    mine[chunk_rows(i), :] = image[chunk_rows(i), :].astype(BF16)
                    copy_h(i).start()

                    @pl.when(seat == 0)
                    def _():
                        copy_x(i).start()
                        out_ref[chunk_rows(i), :] = mine[chunk_rows(i), :]

                    @pl.when(seat == 6)
                    def _():
                        copy_s(i).start()

            @pl.when(seat == 2)
            def _():
                for part in range(PARTS):
                    i = t * PARTS + part
                    other[chunk_rows(i), :] = image[chunk_rows(i), :].astype(BF16)
                    copy_x(i, other).start()

            @pl.when(t < BLOCKS - 1)
            def _():
                transform(t + 1)

            @pl.when(seat == 3)
            def _():
                for part in range(PARTS):
                    i = t * PARTS + part
                    rows = chunk_rows(i)
                    copy_x(i).wait_recv()
                    keep(other, rows, *plus(rows, image, turn(rows, *halves(from_x, rows))))
                    copy_h(i, other).start()

        block = t - lag

        @pl.when(takes_h & (block >= 0) & (block < BLOCKS))
        def _():
            for part in range(PARTS):
                i = block * PARTS + part
                rows = chunk_rows(i)

                @pl.when(seat == 1)
                def _():
                    copy_x(i).wait_recv()
                    twice = turn(rows, *turn(rows, *halves(from_x, rows)))
                    copy_h(i).wait_recv()
                    keep(mine, rows, *plus(rows, image, turn(rows, *plus(rows, from_h, twice))))

                @pl.when(seat != 1)
                def _():
                    copy_h(i).wait_recv()
                    keep(mine, rows, *plus(rows, image, turn(rows, *halves(from_h, rows))))

                @pl.when(is_seat(2, 4, 5))
                def _():
                    copy_h(i).start()

                @pl.when(is_seat(1, 3, 4))
                def _():
                    copy_s(i).start()

                @pl.when(is_seat(2, 5, 7))
                def _():
                    out_ref[rows, :] = mine[rows, :]

        return carry

    lax.fori_loop(0, BLOCKS + 3, work, 0)

    @pl.when(away)
    def _():
        def finish(i, carry):
            copy_s(i).wait_recv()
            out_ref[chunk_rows(i), :] = from_s[chunk_rows(i), :]
            return carry

        lax.fori_loop(0, CHUNKS, finish, 0)

    def drain(i, carry):
        @pl.when(sends_h)
        def _():
            copy_h(i).wait_send()

        @pl.when(sends_x)
        def _():
            copy_x(i).wait_send()

        @pl.when(away)
        def _():
            copy_s(i).wait_send()

        return carry

    lax.fori_loop(0, CHUNKS, drain, 0)


def chain(grid, row_table, p_re, p_im):
    band = (GRID, 2 * GRID)
    return pl.pallas_call(
        chain_kernel,
        out_shape=jax.ShapeDtypeStruct(band, BF16),
        in_specs=[VMEM] * 4,
        out_specs=VMEM,
        scratch_shapes=[
            pltpu.VMEM((2 * GRID, 2 * GRID), BF16),
            pltpu.VMEM(band, F32),
        ]
        + [pltpu.VMEM(band, BF16)] * 5
        + [pltpu.SemaphoreType.DMA((CHUNKS,))] * 6,
        compiler_params=pltpu.CompilerParams(
            collective_id=1, has_side_effects=True, vmem_limit_bytes=24 << 20
        ),
        name="chain",
    )(grid, row_table, p_re, p_im)


def dft_rows():
    line = np.arange(GRID)
    angle = (line[:, None] * line[None, :] % GRID) * (2.0 * math.pi / GRID)
    table = np.concatenate([np.cos(angle), np.sin(angle)], axis=1) / math.sqrt(GRID)
    return table.astype(np.float32).astype(ml_dtypes.bfloat16)


def on_device(visibilities, uv_angles, routes, offsets, pixel_phase):
    vis = visibilities.transpose(1, 2, 0).reshape(2 * NVIS, SUBS)
    ang = uv_angles.transpose(1, 2, 0).reshape(2 * NVIS, SUBS)
    recv, p_re, p_im = route(vis, ang, routes.reshape(1, SUBS), offsets.T, pixel_phase[0])
    grid, row_table = grid_owner(recv.reshape(SUBS * ROWS, 128), jnp.asarray(dft_rows()))
    result = chain(grid, row_table, p_re, p_im)
    return result.astype(F32).reshape(1, 1, GRID, 2 * GRID)


def solution(mesh):
    in_specs = (
        P(("wa", "facet"), None, None),
        P(("wa", "facet"), None, None),
        P(("wa", "facet"), None),
        P(("wa", "facet"), None),
        P("facet", None, None),
    )
    out_specs = P("wa", "facet", None, None)
    return jax.shard_map(
        on_device, mesh=mesh, in_specs=in_specs, out_specs=out_specs, check_vma=False
    )
```

```python
import functools
import math

import jax
import jax.numpy as jnp
import ml_dtypes
import numpy as np
from jax import lax
from jax.experimental import pallas as pl
from jax.experimental.pallas import tpu as pltpu
from jax.sharding import PartitionSpec as P

SUB = 64
GRID = 512
NVIS = 64
SUBS = 128
CAP = 2
KINDS = 4
ROWS = CAP * KINDS
BLOCK = 64
CHUNK = 32
BLOCKS = GRID // BLOCK
PARTS = BLOCK // CHUNK
CHUNKS = GRID // CHUNK
UNROLL = 32
BF16 = jnp.bfloat16
F32 = jnp.float32
MESH = pl.DeviceIdType.MESH
VMEM = pl.BlockSpec(memory_space=pltpu.VMEM)
HBM = pl.BlockSpec(memory_space=pltpu.HBM)
NT = (((1,), (1,)), ((), ()))


def sincos(x):
    h = x * 0.5
    q = h * h
    s = h + h * q * (
        -1.6666666666666602e-1
        + q * (8.333333333320001e-3
        + q * (-1.9841269829589539e-4
        + q * (2.7557314297030280e-6
        + q * (-2.5050747762850355e-8
        + q * 1.5891812000000000e-10))))
    )
    c = 1.0 + q * (
        -0.5
        + q * (4.16666666666665929218e-2
        + q * (-1.38888888888730564116e-3
        + q * (2.48015872888517045348e-5
        + q * (-2.75573141792967388112e-7
        + q * 2.08757008419747316778e-9))))
    )
    return 1.0 - 2.0 * s * s, 2.0 * s * c


def route_kernel(
    vis_hbm, ang_hbm, route_hbm, off_hbm, phase_hbm, out_ref, p_re, p_im, vis_ref, ang_ref, route_ref, off_ref, phase,
    send, recv, in_sems, send_sem, recv_sem, p_sems,
):
    inputs = [
        pltpu.make_async_copy(source, target, in_sems.at[n])
        for n, (source, target) in enumerate(
            ((route_hbm, route_ref), (off_hbm, off_ref), (ang_hbm, ang_ref), (vis_hbm, vis_ref))
        )
    ]
    for copy in inputs:
        copy.start()

    z, f = lax.axis_index("wa"), lax.axis_index("facet")
    me = z * 32 + f

    low, core = z < 2, f & 1
    takes = (low & (core == 1)) | (jnp.logical_not(low) & (core == 0))

    def phase_own():
        return pltpu.make_async_copy(phase_hbm, phase, p_sems.at[2])

    def phase_out():
        return pltpu.make_async_remote_copy(
            src_ref=phase_hbm, dst_ref=phase, send_sem=p_sems.at[0], recv_sem=p_sems.at[1],
            device_id=(z, f ^ 1), device_id_type=MESH,
        )

    @pl.when(jnp.logical_not(takes))
    def _():
        phase_own().start()

    def each_peer(act):
        def early(i, carry):
            for n in range(5):
                act(me ^ (i * 5 + n) ^ 85)
            return carry

        def late(i, carry):
            for n in range(6):
                act(me ^ (i * 6 + n + 86) ^ 85)
            return carry

        lax.fori_loop(0, 17, early, 0)
        lax.fori_loop(0, 7, late, 0)

    barrier = pltpu.get_barrier_semaphore()
    each_peer(
        lambda to: pl.semaphore_signal(
            barrier, inc=1, device_id=(to >> 5, to & 31), device_id_type=MESH
        )
    )
    for copy in inputs:
        copy.wait()

    owner = route_ref[...]
    facet = owner & 31
    plane = owner >> 5
    odd = facet & 1
    seat = jnp.where(odd == 1, 6, 0)
    seat = jnp.where(plane == 1, jnp.where(odd == 1, 4, 2), seat)
    seat = jnp.where(plane == 2, jnp.where(odd == 1, 5, 3), seat)
    seat = jnp.where(plane == 3, jnp.where(odd == 1, 7, 1), seat)
    device = ((seat >> 1) << 5) + (facet - odd) + (seat & 1)
    owner_b = jnp.broadcast_to(owner.astype(F32), (SUBS, SUBS))
    row_i = lax.broadcasted_iota(jnp.int32, (SUBS, SUBS), 0)
    col_i = lax.broadcasted_iota(jnp.int32, (SUBS, SUBS), 1)
    earlier = jnp.where((owner_b == owner_b.T) & (row_i < col_i), 1.0, 0.0)
    rank = jnp.sum(earlier, axis=0, keepdims=True).astype(jnp.int32)
    slot = device * CAP + rank
    total = SUBS * CAP
    col_key = jnp.concatenate([slot + kind * total for kind in range(KINDS)], axis=1)

    angle = ang_ref[...]
    high = angle.astype(BF16)
    low = (angle - high.astype(F32)).astype(BF16)
    off_u, off_v = off_ref[0:1, :], off_ref[1:2, :]
    meta = jnp.where(row_i == 0, off_u >> 4, 0)
    meta = jnp.where(row_i == 1, off_u & 15, meta)
    meta = jnp.where(row_i == 2, off_v >> 4, meta)
    meta = jnp.where(row_i == 3, off_v & 15, meta)
    meta = meta.astype(F32).astype(BF16)
    data = jnp.concatenate([high, low, vis_ref[...], meta], axis=1)

    for block in range(ROWS):
        row = lax.broadcasted_iota(jnp.int32, (SUBS, KINDS * SUBS), 0) + block * SUBS
        place = row & (ROWS - 1)
        row_key = (place // CAP) * total + (row // ROWS) * CAP + place % CAP
        one_hot = jnp.where(row_key == col_key, 1.0, 0.0).astype(BF16)
        picked = lax.dot_general(one_hot, data, NT, preferred_element_type=F32)
        per = SUBS // ROWS
        send[pl.ds(block * per, per)] = picked.astype(BF16).reshape(per, ROWS, 128)

    pl.semaphore_wait(barrier, SUBS - 1)

    @pl.when(jnp.logical_not(takes))
    def _():
        phase_out().start()

    each_peer(
        lambda to: pltpu.make_async_remote_copy(
            src_ref=send.at[to], dst_ref=recv.at[me], send_sem=send_sem, recv_sem=recv_sem,
            device_id=(to >> 5, to & 31), device_id_type=MESH,
        ).start()
    )
    recv[me] = send[me]

    @pl.when(takes)
    def _():
        phase_out().wait_recv()

    @pl.when(jnp.logical_not(takes))
    def _():
        phase_own().wait()

    def angles(i, carry):
        rows = pl.ds(pl.multiple_of(i * BLOCK, BLOCK), BLOCK)
        c, s = sincos(phase[rows, :])
        p_re[rows, :] = c
        p_im[rows, :] = s
        return carry

    lax.fori_loop(0, BLOCKS, angles, 0)

    others = pl.ds(0, SUBS - 1)
    pltpu.make_async_copy(send.at[others], recv.at[others], recv_sem).wait()
    out_ref[...] = recv[...]
    pltpu.make_async_copy(send.at[others], recv.at[others], send_sem).wait()

    @pl.when(jnp.logical_not(takes))
    def _():
        phase_out().wait_send()


def route(vis, ang, owners, off, phase):
    pixels = jax.ShapeDtypeStruct((GRID, GRID), F32)
    return pl.pallas_call(
        route_kernel,
        out_shape=(jax.ShapeDtypeStruct((SUBS, ROWS, 128), BF16), pixels, pixels),
        in_specs=[HBM] * 5,
        out_specs=(VMEM, VMEM, VMEM),
        scratch_shapes=[
            pltpu.VMEM((2 * NVIS, SUBS), BF16),
            pltpu.VMEM((2 * NVIS, SUBS), F32),
            pltpu.VMEM((1, SUBS), jnp.int32),
            pltpu.VMEM((2, SUBS), jnp.int32),
            pltpu.VMEM((GRID, GRID), F32),
            pltpu.VMEM((SUBS, ROWS, 128), BF16),
            pltpu.VMEM((SUBS, ROWS, 128), BF16),
            pltpu.SemaphoreType.DMA((4,)),
            pltpu.SemaphoreType.DMA,
            pltpu.SemaphoreType.DMA,
            pltpu.SemaphoreType.DMA((3,)),
        ],
        compiler_params=pltpu.CompilerParams(
            collective_id=0, has_side_effects=True, vmem_limit_bytes=10 << 20
        ),
        name="route",
    )(*[pltpu.with_memory_space_constraint(value, pltpu.HBM) for value in (vis, ang, owners, off, phase)])


def complex_mul(a, b):
    return a[0] * b[0] - a[1] * b[1], a[0] * b[1] + a[1] * b[0]


def grid_kernel(
    recv_ref, rows_hbm, grid_ref, rows_ref, wide, pos_v, pos_s, pos_sem, rows_sem, au_r, au_i, av_r, av_i, bu, bv, acc_a, acc_b, subs
):
    slots = SUBS * CAP
    rows_copy = pltpu.make_async_copy(rows_hbm, rows_ref, rows_sem)
    rows_copy.start()
    wide[...] = recv_ref[...].astype(F32)

    lane8 = lax.broadcasted_iota(jnp.int32, (8, 128), 1)
    weight = jnp.where(lane8 == 0, 8192.0, 0.0)
    weight = jnp.where(lane8 == 1, 512.0, weight)
    weight = jnp.where(lane8 == 2, 16.0, weight)
    weight = jnp.where(lane8 == 3, 1.0, weight).astype(BF16)
    for j in range(CAP):
        meta = wide[pl.ds((KINDS - 1) * CAP + j, SUBS, stride=ROWS), :].astype(BF16)
        packed = lax.dot_general(weight, meta, NT, preferred_element_type=F32)
        pos_v[j] = packed.astype(jnp.int32)
    to_scalar = pltpu.make_async_copy(pos_v, pos_s, pos_sem)
    to_scalar.start()

    subs[...] = jnp.zeros_like(subs)

    group = 16
    first = lax.broadcasted_iota(jnp.int32, (group, 128), 1) < 64

    def tables(g, carry):
        clear = pl.ds(pl.multiple_of(g * SUB, SUB), SUB)
        for tile in range(GRID // SUB + 1):
            acc_a[tile, clear, :] = jnp.zeros((SUB, 128), F32)
            acc_b[tile, clear, :] = jnp.zeros((SUB, 128), F32)
        for j in range(CAP):
            start = g * group

            def rows(kind):
                at = start * ROWS + kind * CAP + j
                return wide[pl.ds(at, group, stride=ROWS), :]

            cos_t, sin_t = sincos(rows(0) + rows(1))
            vis = rows(2) * (1.0 / math.sqrt(NVIS))
            cos_o, sin_o = pltpu.roll(cos_t, 64, 1), pltpu.roll(sin_t, 64, 1)
            vis_o = pltpu.roll(vis, 64, 1)
            vis2 = (vis, jnp.where(first, vis_o, -vis_o))
            slot = pl.multiple_of(start + j * SUBS, group)
            for side in range(2):
                if side == 0:
                    e1 = (jnp.where(first, cos_t, cos_o), jnp.where(first, sin_t, sin_o))
                else:
                    e1 = (jnp.where(first, cos_o, cos_t), jnp.where(first, sin_o, sin_t))
                e2 = complex_mul(e1, e1)
                e3 = complex_mul(e2, e1)
                e4 = complex_mul(e2, e2)
                e5 = complex_mul(e4, e1)
                e6 = complex_mul(e4, e2)
                e7 = complex_mul(e4, e3)
                e8 = complex_mul(e4, e4)
                e16 = complex_mul(e8, e8)
                e24 = complex_mul(e16, e8)
                e32 = complex_mul(e16, e16)
                one = (jnp.ones_like(cos_t), jnp.zeros_like(cos_t))
                for a, e in enumerate((one, e1, e2, e3, e4, e5, e6, e7)):
                    where = pl.ds(slot * 8 + a, group, stride=8)
                    if side == 0:
                        re, im = complex_mul(e, vis2)
                        au_r[where, :] = re
                        au_i[where, :] = im
                    else:
                        av_r[where, :] = jnp.where(first, e[0], -e[1])
                        av_i[where, :] = jnp.where(first, e[1], e[0])
                steps = bu if side == 0 else bv
                for b, e in enumerate((e8, e16, e24, e32)):
                    steps[2 * b, pl.ds(slot, group), :] = e[0]
                    steps[2 * b + 1, pl.ds(slot, group), :] = e[1]
        return carry

    lax.fori_loop(0, SUBS // group, tables, 0)
    to_scalar.wait()

    lane_in = lax.broadcasted_iota(jnp.int32, (SUB, 128), 1) & 63

    def form(slot):
        base = pl.multiple_of(slot * 8, 8)
        ur, ui = au_r[pl.ds(base, 8), :], au_i[pl.ds(base, 8), :]
        vr, vi = av_r[pl.ds(base, 8), :], av_i[pl.ds(base, 8), :]

        def step(table, b):
            return table[2 * b, pl.ds(slot, 1), :], table[2 * b + 1, pl.ds(slot, 1), :]

        left = [None] * 8
        right_r = [None] * 8
        right_i = [None] * 8
        left[4], right_r[4], right_i[4] = ur, vr, vi
        for b in range(4):
            br, bi = step(bu, b)
            x, y = br * ur, bi * ui
            left[3 - b] = x + y
            if b < 3:
                left[5 + b] = x - y
            br, bi = step(bv, b)
            x, y, z, w = br * vr, bi * vi, br * vi, bi * vr
            right_r[3 - b] = x + y
            right_i[3 - b] = z - w
            if b < 3:
                right_r[5 + b] = x - y
                right_i[5 + b] = z + w
        return jnp.concatenate(left, axis=0).astype(BF16), jnp.concatenate(right_r + right_i, axis=0).astype(BF16)

    nought = jnp.zeros((SUB, 128), BF16)

    def form_pair(slot):
        left_0, right_0 = form(slot)
        left_1, right_1 = form(slot + 1)
        left = jnp.concatenate(
            [jnp.concatenate([left_0, nought], axis=1), jnp.concatenate([nought, left_1], axis=1)], axis=0
        )
        right = jnp.concatenate([right_0, right_1], axis=1)
        return lax.dot_general(left, right, NT, preferred_element_type=F32).astype(BF16)

    def place(slot, sub, acc):
        packed = pos_s[slot >> 7, 0, slot & (SUBS - 1)]
        off_u, off_v = packed >> 9, packed & 511
        tile, shift = off_v >> 6, off_v & 63
        rows = pl.ds(off_u, SUB)
        here, there = acc.at[tile, rows, :], acc.at[tile + 1, rows, :]
        near = here[...] + pltpu.roll(sub, shift, 1).astype(F32)
        far = there[...] + pltpu.roll(sub, shift + 64, 1).astype(F32)
        pltpu.store(here, near, mask=lane_in >= shift)
        pltpu.store(there, far, mask=lane_in < shift)

    def place_all(start):
        for n in range(UNROLL):
            sub = subs[n // 2, pl.ds(n % 2 * SUB, SUB), :]
            place(start + n, sub, (acc_a, acc_b)[n % 2])

    def work(i, carry):
        place_all(jnp.maximum(i - 1, 0) * UNROLL)
        for n in range(0, UNROLL, 2):
            subs[n // 2] = form_pair(i * UNROLL + n)
        return carry

    lax.fori_loop(0, slots // UNROLL, work, 0)
    place_all(slots - UNROLL)

    def finish(g, carry):
        rows = pl.ds(pl.multiple_of(g * SUB, SUB), SUB)
        for tile in range(GRID // SUB):
            grid_ref[rows, pl.ds(tile * 128, 128)] = (acc_a[tile, rows, :] + acc_b[tile, rows, :]).astype(BF16)
        return carry

    lax.fori_loop(0, GRID // SUB, finish, 0)
    rows_copy.wait()


def grid_owner(recv, row_table):
    slots = SUBS * CAP
    band = jax.ShapeDtypeStruct((GRID, 2 * GRID), BF16)
    return pl.pallas_call(
        grid_kernel,
        out_shape=(band, band),
        in_specs=[VMEM, HBM],
        out_specs=(VMEM, VMEM),
        scratch_shapes=[
            pltpu.VMEM((SUBS * ROWS, 128), F32),
            pltpu.VMEM((CAP, 8, 128), jnp.int32),
            pltpu.SMEM((CAP, 8, 128), jnp.int32),
            pltpu.SemaphoreType.DMA,
            pltpu.SemaphoreType.DMA,
        ]
        + [pltpu.VMEM((slots * 8, 128), F32)] * 4
        + [pltpu.VMEM((8, slots, 128), F32)] * 2
        + [pltpu.VMEM((GRID // SUB + 1, GRID, 128), F32)] * 2
        + [
            pltpu.VMEM((UNROLL // 2, 2 * SUB, 128), BF16),
        ],
        compiler_params=pltpu.CompilerParams(vmem_limit_bytes=22 << 20),
        name="grid",
    )(recv, pltpu.with_memory_space_constraint(row_table, pltpu.HBM))


def chain_kernel(
    grid_ref, row_ref, p_re, p_im, out_ref, col, image, from_h, from_s, from_x, mine, other,
    h_recv, s_recv, x_recv, h_send, s_send, x_send, g_send,
):
    z, f = lax.axis_index("wa"), lax.axis_index("facet")
    core = f & 1
    seat = 2 * z + core
    pair = f - core

    def at(other_seat):
        return (other_seat >> 1, pair + (other_seat & 1))

    def is_seat(*seats):
        hit = seat == seats[0]
        for other in seats[1:]:
            hit = jnp.logical_or(hit, seat == other)
        return hit

    barrier = pltpu.get_barrier_semaphore()
    for step in range(1, 8):
        pl.semaphore_signal(barrier, inc=1, device_id=at((seat + step) & 7), device_id_type=MESH)

    for tile in range(GRID // SUB):
        rows = row_ref[pl.ds(tile * SUB, SUB), :]
        col[pl.ds(tile * 128, SUB), :] = rows
        col[pl.ds(tile * 128 + SUB, SUB), pl.ds(0, GRID)] = -rows[:, GRID:]
        col[pl.ds(tile * 128 + SUB, SUB), pl.ds(GRID, GRID)] = rows[:, :GRID]

    real = lax.broadcasted_iota(jnp.int32, (BLOCK, 2 * GRID), 1) & 127 < 64

    def block_rows(i):
        return pl.ds(pl.multiple_of(i * BLOCK, BLOCK), BLOCK)

    def chunk_rows(i):
        return pl.ds(pl.multiple_of(i * CHUNK, CHUNK), CHUNK)

    def transform(i):
        rows = block_rows(i)
        both = jnp.concatenate([row_ref[rows, pl.ds(0, GRID)], row_ref[rows, pl.ds(GRID, GRID)]], axis=0)
        parts = jnp.dot(both, grid_ref[...], preferred_element_type=F32)
        turned = jnp.concatenate(
            [pltpu.roll(parts[BLOCK:, t * 128 : (t + 1) * 128], 64, 1) for t in range(GRID // SUB)], axis=1
        )
        half = parts[:BLOCK] + jnp.where(real, -turned, turned)
        image[rows, :] = jnp.dot(half.astype(BF16), col[...], preferred_element_type=F32)

    transform(0)
    pl.semaphore_wait(barrier, 7)

    to_h = jnp.where(seat == 0, 2, jnp.where(seat == 3, 1, jnp.where(seat == 6, 4, 5)))
    to_s = jnp.where(seat == 1, 6, jnp.where(seat == 2, 4, jnp.where(seat == 4, 3, 1)))
    sends_h = is_seat(0, 3, 4, 6)
    sends_s = is_seat(1, 2, 4, 6)
    sends_x = is_seat(0, 2, 3, 5)
    takes_h = is_seat(1, 2, 4, 5, 7)
    away = is_seat(1, 3, 4, 6)
    lag = jnp.where(is_seat(2, 4), 1, 3)

    def copy_h(i):
        rows = chunk_rows(i)
        return pltpu.make_async_remote_copy(
            src_ref=mine.at[rows], dst_ref=from_h.at[rows], send_sem=h_send.at[i], recv_sem=h_recv.at[i],
            device_id=at(to_h), device_id_type=MESH,
        )

    def copy_x(i, source=mine):
        rows = chunk_rows(i)
        return pltpu.make_async_remote_copy(
            src_ref=source.at[rows], dst_ref=from_x.at[rows], send_sem=x_send.at[i], recv_sem=x_recv.at[i],
            device_id=at(seat ^ 1), device_id_type=MESH,
        )

    def copy_g(i):
        rows = chunk_rows(i)
        return pltpu.make_async_remote_copy(
            src_ref=other.at[rows], dst_ref=from_h.at[rows], send_sem=g_send.at[i], recv_sem=h_recv.at[i],
            device_id=at(7), device_id_type=MESH,
        )

    def copy_s(i):
        rows = chunk_rows(i)
        return pltpu.make_async_remote_copy(
            src_ref=mine.at[rows], dst_ref=from_s.at[rows], send_sem=s_send.at[i], recv_sem=s_recv.at[i],
            device_id=at(to_s), device_id_type=MESH,
        )

    def turn(rows, re, im):
        c, s = p_re[rows, :], p_im[rows, :]
        return c * re - s * im, c * im + s * re

    def halves(ref, rows):
        return ref[rows, pl.ds(0, GRID)].astype(F32), ref[rows, pl.ds(GRID, GRID)].astype(F32)

    def keep(ref, rows, re, im):
        ref[rows, pl.ds(0, GRID)] = re.astype(BF16)
        ref[rows, pl.ds(GRID, GRID)] = im.astype(BF16)

    def plus(rows, ref, pair_in):
        re, im = halves(ref, rows)
        return pair_in[0] + re, pair_in[1] + im

    def work(t, carry):
        @pl.when(t < BLOCKS)
        def _():
            @pl.when(is_seat(0, 6))
            def _():
                for part in range(PARTS):
                    i = t * PARTS + part
                    mine[chunk_rows(i), :] = image[chunk_rows(i), :].astype(BF16)
                    copy_h(i).start()

                    @pl.when(seat == 0)
                    def _():
                        copy_x(i).start()
                        out_ref[chunk_rows(i), :] = mine[chunk_rows(i), :]

                    @pl.when(seat == 6)
                    def _():
                        copy_s(i).start()

            @pl.when(is_seat(2, 3, 5))
            def _():
                for part in range(PARTS):
                    i = t * PARTS + part
                    other[chunk_rows(i), :] = image[chunk_rows(i), :].astype(BF16)
                    copy_x(i, other).start()

            @pl.when(t < BLOCKS - 1)
            def _():
                transform(t + 1)

            @pl.when(seat == 3)
            def _():
                for part in range(PARTS):
                    i = t * PARTS + part
                    rows = chunk_rows(i)
                    copy_x(i).wait_recv()
                    keep(mine, rows, *plus(rows, image, turn(rows, *halves(from_x, rows))))
                    copy_h(i).start()

        block = t - lag

        @pl.when(takes_h & (block >= 0) & (block < BLOCKS))
        def _():
            for part in range(PARTS):
                i = block * PARTS + part
                rows = chunk_rows(i)

                @pl.when(seat == 1)
                def _():
                    copy_x(i).wait_recv()
                    twice = turn(rows, *turn(rows, *halves(from_x, rows)))
                    copy_h(i).wait_recv()
                    keep(mine, rows, *plus(rows, image, turn(rows, *plus(rows, from_h, twice))))

                    copy_s(i).start()

                @pl.when(seat == 2)
                def _():
                    copy_h(i).wait_recv()
                    once = plus(rows, image, turn(rows, *halves(from_h, rows)))
                    keep(out_ref, rows, *once)
                    copy_x(i).wait_recv()
                    keep(mine, rows, *plus(rows, from_x, turn(rows, *once)))
                    copy_s(i).start()

                @pl.when(seat == 4)
                def _():
                    copy_h(i).wait_recv()
                    once = plus(rows, image, turn(rows, *halves(from_h, rows)))
                    keep(mine, rows, *once)
                    copy_s(i).start()
                    copy_x(i).wait_recv()
                    keep(other, rows, *plus(rows, from_x, turn(rows, *once)))
                    copy_g(i).start()
                    copy_h(i).start()

                @pl.when(is_seat(5, 7))
                def _():
                    copy_h(i).wait_recv()
                    keep(out_ref, rows, *plus(rows, image, turn(rows, *halves(from_h, rows))))

        return carry

    lax.fori_loop(0, BLOCKS + 3, work, 0)

    @pl.when(away)
    def _():
        def finish(i, carry):
            copy_s(i).wait_recv()
            out_ref[chunk_rows(i), :] = from_s[chunk_rows(i), :]
            return carry

        lax.fori_loop(0, CHUNKS, finish, 0)

    def drain(i, carry):
        @pl.when(sends_h)
        def _():
            copy_h(i).wait_send()

        @pl.when(sends_x)
        def _():
            copy_x(i).wait_send()

        @pl.when(sends_s)
        def _():
            copy_s(i).wait_send()

        @pl.when(seat == 4)
        def _():
            copy_g(i).wait_send()

        return carry

    lax.fori_loop(0, CHUNKS, drain, 0)


def chain(grid, row_table, p_re, p_im):
    band = (GRID, 2 * GRID)
    return pl.pallas_call(
        chain_kernel,
        out_shape=jax.ShapeDtypeStruct(band, BF16),
        in_specs=[VMEM] * 4,
        out_specs=VMEM,
        scratch_shapes=[
            pltpu.VMEM((2 * GRID, 2 * GRID), BF16),
            pltpu.VMEM(band, F32),
        ]
        + [pltpu.VMEM(band, BF16)] * 5
        + [pltpu.SemaphoreType.DMA((CHUNKS,))] * 7,
        compiler_params=pltpu.CompilerParams(
            collective_id=1, has_side_effects=True, vmem_limit_bytes=24 << 20
        ),
        name="chain",
    )(grid, row_table, p_re, p_im)


def widen_kernel(band_ref, out_hbm, wide, sems):
    def copy(i):
        rows = pl.ds(i * BLOCK, BLOCK)
        return pltpu.make_async_copy(wide.at[rows], out_hbm.at[rows], sems.at[i])

    for i in range(BLOCKS):
        rows = pl.ds(i * BLOCK, BLOCK)
        wide[rows, :] = band_ref[rows, :].astype(F32)
        copy(i).start()
    for i in range(BLOCKS):
        copy(i).wait()


def widen(band):
    return pl.pallas_call(
        widen_kernel,
        out_shape=jax.ShapeDtypeStruct(band.shape, F32),
        in_specs=[VMEM],
        out_specs=HBM,
        scratch_shapes=[pltpu.VMEM(band.shape, F32), pltpu.SemaphoreType.DMA((BLOCKS,))],
        compiler_params=pltpu.CompilerParams(vmem_limit_bytes=8 << 20),
        name="widen",
    )(band)


def dft_rows():
    line = np.arange(GRID)
    angle = (line[:, None] * line[None, :] % GRID) * (2.0 * math.pi / GRID)
    table = np.concatenate([np.cos(angle), np.sin(angle)], axis=1) / math.sqrt(GRID)
    return table.astype(np.float32).astype(ml_dtypes.bfloat16)


def on_device(visibilities, uv_angles, routes, offsets, pixel_phase):
    vis = visibilities.transpose(1, 2, 0).reshape(2 * NVIS, SUBS)
    ang = uv_angles.transpose(1, 2, 0).reshape(2 * NVIS, SUBS)
    recv, p_re, p_im = route(vis, ang, routes.reshape(1, SUBS), offsets.T, pixel_phase[0])
    grid, row_table = grid_owner(recv.reshape(SUBS * ROWS, 128), jnp.asarray(dft_rows()))
    result = chain(grid, row_table, p_re, p_im)
    return widen(result).reshape(1, 1, GRID, 2 * GRID)


def solution(mesh):
    in_specs = (
        P(("wa", "facet"), None, None),
        P(("wa", "facet"), None, None),
        P(("wa", "facet"), None),
        P(("wa", "facet"), None),
        P("facet", None, None),
    )
    out_specs = P("wa", "facet", None, None)
    return jax.shard_map(
        on_device, mesh=mesh, in_specs=in_specs, out_specs=out_specs, check_vma=False
    )
```

```python
import functools
import math

import jax
import jax.numpy as jnp
import ml_dtypes
import numpy as np
from jax import lax
from jax.experimental import pallas as pl
from jax.experimental.pallas import tpu as pltpu
from jax.sharding import PartitionSpec as P

SUB = 64
GRID = 512
NVIS = 64
SUBS = 128
CAP = 2
KINDS = 4
ROWS = CAP * KINDS
BLOCK = 64
CHUNK = 32
BLOCKS = GRID // BLOCK
PARTS = BLOCK // CHUNK
CHUNKS = GRID // CHUNK
UNROLL = 32
BF16 = jnp.bfloat16
F32 = jnp.float32
MESH = pl.DeviceIdType.MESH
VMEM = pl.BlockSpec(memory_space=pltpu.VMEM)
HBM = pl.BlockSpec(memory_space=pltpu.HBM)
NT = (((1,), (1,)), ((), ()))


def sincos(x):
    h = x * 0.5
    q = h * h
    s = h + h * q * (
        -1.6666666666666602e-1
        + q * (8.333333333320001e-3
        + q * (-1.9841269829589539e-4
        + q * (2.7557314297030280e-6
        + q * (-2.5050747762850355e-8
        + q * 1.5891812000000000e-10))))
    )
    c = 1.0 + q * (
        -0.5
        + q * (4.16666666666665929218e-2
        + q * (-1.38888888888730564116e-3
        + q * (2.48015872888517045348e-5
        + q * (-2.75573141792967388112e-7
        + q * 2.08757008419747316778e-9))))
    )
    return 1.0 - 2.0 * s * s, 2.0 * s * c


def route_kernel(
    vis_hbm, ang_hbm, route_hbm, off_hbm, phase_hbm, rows_hbm, out_ref, p_re, p_im, row_ref, col, vis_ref, ang_ref, route_ref, off_ref, phase,
    send, recv, in_sems, send_sem, recv_sem, p_sems,
):
    inputs = [
        pltpu.make_async_copy(source, target, in_sems.at[n])
        for n, (source, target) in enumerate(
            ((route_hbm, route_ref), (off_hbm, off_ref), (ang_hbm, ang_ref), (vis_hbm, vis_ref), (rows_hbm, row_ref))
        )
    ]
    for copy in inputs:
        copy.start()

    z, f = lax.axis_index("wa"), lax.axis_index("facet")
    me = z * 32 + f

    low, core = z < 2, f & 1
    takes = (low & (core == 1)) | (jnp.logical_not(low) & (core == 0))

    def phase_own():
        return pltpu.make_async_copy(phase_hbm, phase, p_sems.at[2])

    def phase_out():
        return pltpu.make_async_remote_copy(
            src_ref=phase_hbm, dst_ref=phase, send_sem=p_sems.at[0], recv_sem=p_sems.at[1],
            device_id=(z, f ^ 1), device_id_type=MESH,
        )

    @pl.when(jnp.logical_not(takes))
    def _():
        phase_own().start()

    def each_peer(act):
        def early(i, carry):
            for n in range(5):
                act(me ^ (i * 5 + n) ^ 85)
            return carry

        def late(i, carry):
            for n in range(6):
                act(me ^ (i * 6 + n + 86) ^ 85)
            return carry

        lax.fori_loop(0, 17, early, 0)
        lax.fori_loop(0, 7, late, 0)

    barrier = pltpu.get_barrier_semaphore()
    each_peer(
        lambda to: pl.semaphore_signal(
            barrier, inc=1, device_id=(to >> 5, to & 31), device_id_type=MESH
        )
    )
    for copy in inputs[:4]:
        copy.wait()

    owner = route_ref[...]
    facet = owner & 31
    plane = owner >> 5
    odd = facet & 1
    seat = jnp.where(odd == 1, 6, 0)
    seat = jnp.where(plane == 1, jnp.where(odd == 1, 4, 2), seat)
    seat = jnp.where(plane == 2, jnp.where(odd == 1, 5, 3), seat)
    seat = jnp.where(plane == 3, jnp.where(odd == 1, 7, 1), seat)
    device = ((seat >> 1) << 5) + (facet - odd) + (seat & 1)
    owner_b = jnp.broadcast_to(owner.astype(F32), (SUBS, SUBS))
    row_i = lax.broadcasted_iota(jnp.int32, (SUBS, SUBS), 0)
    col_i = lax.broadcasted_iota(jnp.int32, (SUBS, SUBS), 1)
    earlier = jnp.where((owner_b == owner_b.T) & (row_i < col_i), 1.0, 0.0)
    rank = jnp.sum(earlier, axis=0, keepdims=True).astype(jnp.int32)
    slot = device * CAP + rank
    total = SUBS * CAP
    col_key = jnp.concatenate([slot + kind * total for kind in range(KINDS)], axis=1)

    angle = ang_ref[...]
    high = angle.astype(BF16)
    low = (angle - high.astype(F32)).astype(BF16)
    off_u, off_v = off_ref[0:1, :], off_ref[1:2, :]
    meta = jnp.where(row_i == 0, off_u >> 4, 0)
    meta = jnp.where(row_i == 1, off_u & 15, meta)
    meta = jnp.where(row_i == 2, off_v >> 4, meta)
    meta = jnp.where(row_i == 3, off_v & 15, meta)
    meta = meta.astype(F32).astype(BF16)
    data = jnp.concatenate([high, low, vis_ref[...], meta], axis=1)

    for block in range(ROWS):
        row = lax.broadcasted_iota(jnp.int32, (SUBS, KINDS * SUBS), 0) + block * SUBS
        place = row & (ROWS - 1)
        row_key = (place // CAP) * total + (row // ROWS) * CAP + place % CAP
        one_hot = jnp.where(row_key == col_key, 1.0, 0.0).astype(BF16)
        picked = lax.dot_general(one_hot, data, NT, preferred_element_type=F32)
        per = SUBS // ROWS
        send[pl.ds(block * per, per)] = picked.astype(BF16).reshape(per, ROWS, 128)

    pl.semaphore_wait(barrier, SUBS - 1)

    @pl.when(jnp.logical_not(takes))
    def _():
        phase_out().start()

    each_peer(
        lambda to: pltpu.make_async_remote_copy(
            src_ref=send.at[to], dst_ref=recv.at[me], send_sem=send_sem, recv_sem=recv_sem,
            device_id=(to >> 5, to & 31), device_id_type=MESH,
        ).start()
    )
    recv[me] = send[me]

    @pl.when(takes)
    def _():
        phase_out().wait_recv()

    @pl.when(jnp.logical_not(takes))
    def _():
        phase_own().wait()

    def angles(i, carry):
        rows = pl.ds(pl.multiple_of(i * BLOCK, BLOCK), BLOCK)
        c, s = sincos(phase[rows, :])
        p_re[rows, :] = c
        p_im[rows, :] = s
        return carry

    lax.fori_loop(0, BLOCKS, angles, 0)
    inputs[4].wait()
    for tile in range(GRID // SUB):
        rows = row_ref[pl.ds(tile * SUB, SUB), :]
        col[pl.ds(tile * 128, SUB), :] = rows
        col[pl.ds(tile * 128 + SUB, SUB), pl.ds(0, GRID)] = -rows[:, GRID:]
        col[pl.ds(tile * 128 + SUB, SUB), pl.ds(GRID, GRID)] = rows[:, :GRID]


    others = pl.ds(0, SUBS - 1)
    pltpu.make_async_copy(send.at[others], recv.at[others], recv_sem).wait()
    out_ref[...] = recv[...]
    pltpu.make_async_copy(send.at[others], recv.at[others], send_sem).wait()

    @pl.when(jnp.logical_not(takes))
    def _():
        phase_out().wait_send()


def route(vis, ang, owners, off, phase, row_table):
    pixels = jax.ShapeDtypeStruct((GRID, GRID), F32)
    return pl.pallas_call(
        route_kernel,
        out_shape=(
            jax.ShapeDtypeStruct((SUBS, ROWS, 128), BF16),
            pixels,
            pixels,
            jax.ShapeDtypeStruct((GRID, 2 * GRID), BF16),
            jax.ShapeDtypeStruct((2 * GRID, 2 * GRID), BF16),
        ),
        in_specs=[HBM] * 6,
        out_specs=(VMEM,) * 5,
        scratch_shapes=[
            pltpu.VMEM((2 * NVIS, SUBS), BF16),
            pltpu.VMEM((2 * NVIS, SUBS), F32),
            pltpu.VMEM((1, SUBS), jnp.int32),
            pltpu.VMEM((2, SUBS), jnp.int32),
            pltpu.VMEM((GRID, GRID), F32),
            pltpu.VMEM((SUBS, ROWS, 128), BF16),
            pltpu.VMEM((SUBS, ROWS, 128), BF16),
            pltpu.SemaphoreType.DMA((5,)),
            pltpu.SemaphoreType.DMA,
            pltpu.SemaphoreType.DMA,
            pltpu.SemaphoreType.DMA((3,)),
        ],
        compiler_params=pltpu.CompilerParams(
            collective_id=0, has_side_effects=True, vmem_limit_bytes=14 << 20
        ),
        name="route",
    )(*[pltpu.with_memory_space_constraint(value, pltpu.HBM) for value in (vis, ang, owners, off, phase, row_table)])


def complex_mul(a, b):
    return a[0] * b[0] - a[1] * b[1], a[0] * b[1] + a[1] * b[0]


def grid_kernel(
    recv_ref, grid_ref, wide, pos_v, pos_s, pos_sem, au_r, au_i, av_r, av_i, bu, bv, acc_a, acc_b, subs
):
    slots = SUBS * CAP
    wide[...] = recv_ref[...].astype(F32)

    lane8 = lax.broadcasted_iota(jnp.int32, (8, 128), 1)
    weight = jnp.where(lane8 == 0, 8192.0, 0.0)
    weight = jnp.where(lane8 == 1, 512.0, weight)
    weight = jnp.where(lane8 == 2, 16.0, weight)
    weight = jnp.where(lane8 == 3, 1.0, weight).astype(BF16)
    for j in range(CAP):
        meta = wide[pl.ds((KINDS - 1) * CAP + j, SUBS, stride=ROWS), :].astype(BF16)
        packed = lax.dot_general(weight, meta, NT, preferred_element_type=F32)
        pos_v[j] = packed.astype(jnp.int32)
    to_scalar = pltpu.make_async_copy(pos_v, pos_s, pos_sem)
    to_scalar.start()

    subs[...] = jnp.zeros_like(subs)

    group = 16
    first = lax.broadcasted_iota(jnp.int32, (group, 128), 1) < 64

    def tables(g, carry):
        clear = pl.ds(pl.multiple_of(g * SUB, SUB), SUB)
        for tile in range(GRID // SUB + 1):
            acc_a[tile, clear, :] = jnp.zeros((SUB, 128), F32)
            acc_b[tile, clear, :] = jnp.zeros((SUB, 128), F32)
        for j in range(CAP):
            start = g * group

            def rows(kind):
                at = start * ROWS + kind * CAP + j
                return wide[pl.ds(at, group, stride=ROWS), :]

            cos_t, sin_t = sincos(rows(0) + rows(1))
            vis = rows(2) * (1.0 / math.sqrt(NVIS))
            cos_o, sin_o = pltpu.roll(cos_t, 64, 1), pltpu.roll(sin_t, 64, 1)
            vis_o = pltpu.roll(vis, 64, 1)
            vis2 = (vis, jnp.where(first, vis_o, -vis_o))
            slot = pl.multiple_of(start + j * SUBS, group)
            for side in range(2):
                if side == 0:
                    e1 = (jnp.where(first, cos_t, cos_o), jnp.where(first, sin_t, sin_o))
                else:
                    e1 = (jnp.where(first, cos_o, cos_t), jnp.where(first, sin_o, sin_t))
                e2 = complex_mul(e1, e1)
                e4 = complex_mul(e2, e2)
                e8 = complex_mul(e4, e4)
                e16 = complex_mul(e8, e8)
                e24 = complex_mul(e16, e8)
                e32 = complex_mul(e16, e16)
                if side == 0:
                    tree = [vis2]
                    tree += [complex_mul(tree[0], e1)]
                    tree += [complex_mul(e, e2) for e in tree]
                    tree += [complex_mul(e, e4) for e in tree]
                else:
                    e3 = complex_mul(e2, e1)
                    one = (jnp.ones_like(cos_t), jnp.zeros_like(cos_t))
                    tree = [one, e1, e2, e3, e4] + [complex_mul(e4, e) for e in (e1, e2, e3)]
                for a, (re, im) in enumerate(tree):
                    where = pl.ds(slot * 8 + a, group, stride=8)
                    if side == 0:
                        au_r[where, :] = re
                        au_i[where, :] = im
                    else:
                        av_r[where, :] = jnp.where(first, re, -im)
                        av_i[where, :] = jnp.where(first, im, re)
                steps = bu if side == 0 else bv
                for b, e in enumerate((e8, e16, e24, e32)):
                    steps[2 * b, pl.ds(slot, group), :] = e[0]
                    steps[2 * b + 1, pl.ds(slot, group), :] = e[1]
        return carry

    lax.fori_loop(0, SUBS // group, tables, 0)
    to_scalar.wait()

    lane_in = lax.broadcasted_iota(jnp.int32, (SUB, 128), 1) & 63

    def form(slot):
        base = pl.multiple_of(slot * 8, 8)
        ur, ui = au_r[pl.ds(base, 8), :], au_i[pl.ds(base, 8), :]
        vr, vi = av_r[pl.ds(base, 8), :], av_i[pl.ds(base, 8), :]

        def step(table, b):
            return table[2 * b, pl.ds(slot, 1), :], table[2 * b + 1, pl.ds(slot, 1), :]

        left = [None] * 8
        right_r = [None] * 8
        right_i = [None] * 8
        left[4], right_r[4], right_i[4] = ur, vr, vi
        for b in range(4):
            br, bi = step(bu, b)
            x, y = br * ur, bi * ui
            left[3 - b] = x + y
            if b < 3:
                left[5 + b] = x - y
            br, bi = step(bv, b)
            x, y, z, w = br * vr, bi * vi, br * vi, bi * vr
            right_r[3 - b] = x + y
            right_i[3 - b] = z - w
            if b < 3:
                right_r[5 + b] = x - y
                right_i[5 + b] = z + w
        return jnp.concatenate(left, axis=0).astype(BF16), jnp.concatenate(right_r + right_i, axis=0).astype(BF16)

    nought = jnp.zeros((SUB, 128), BF16)

    def form_pair(slot):
        left_0, right_0 = form(slot)
        left_1, right_1 = form(slot + 1)
        left = jnp.concatenate(
            [jnp.concatenate([left_0, nought], axis=1), jnp.concatenate([nought, left_1], axis=1)], axis=0
        )
        right = jnp.concatenate([right_0, right_1], axis=1)
        return lax.dot_general(left, right, NT, preferred_element_type=F32).astype(BF16)

    def place(slot, sub, acc):
        packed = pos_s[slot >> 7, 0, slot & (SUBS - 1)]
        off_u, off_v = packed >> 9, packed & 511
        tile, shift = off_v >> 6, off_v & 63
        rows = pl.ds(off_u, SUB)
        here, there = acc.at[tile, rows, :], acc.at[tile + 1, rows, :]
        near = here[...] + pltpu.roll(sub, shift, 1).astype(F32)
        far = there[...] + pltpu.roll(sub, shift + 64, 1).astype(F32)
        pltpu.store(here, near, mask=lane_in >= shift)
        pltpu.store(there, far, mask=lane_in < shift)

    def place_all(start):
        for n in range(UNROLL):
            sub = subs[n // 2, pl.ds(n % 2 * SUB, SUB), :]
            place(start + n, sub, (acc_a, acc_b)[n % 2])

    def work(i, carry):
        place_all(jnp.maximum(i - 1, 0) * UNROLL)
        for n in range(0, UNROLL, 2):
            subs[n // 2] = form_pair(i * UNROLL + n)
        return carry

    lax.fori_loop(0, slots // UNROLL, work, 0)
    place_all(slots - UNROLL)

    def finish(g, carry):
        rows = pl.ds(pl.multiple_of(g * SUB, SUB), SUB)
        for tile in range(GRID // SUB):
            grid_ref[rows, pl.ds(tile * 128, 128)] = (acc_a[tile, rows, :] + acc_b[tile, rows, :]).astype(BF16)
        return carry

    lax.fori_loop(0, GRID // SUB, finish, 0)


def grid_owner(recv):
    slots = SUBS * CAP
    return pl.pallas_call(
        grid_kernel,
        out_shape=jax.ShapeDtypeStruct((GRID, 2 * GRID), BF16),
        in_specs=[VMEM],
        out_specs=VMEM,
        scratch_shapes=[
            pltpu.VMEM((SUBS * ROWS, 128), F32),
            pltpu.VMEM((CAP, 8, 128), jnp.int32),
            pltpu.SMEM((CAP, 8, 128), jnp.int32),
            pltpu.SemaphoreType.DMA,
        ]
        + [pltpu.VMEM((slots * 8, 128), F32)] * 4
        + [pltpu.VMEM((8, slots, 128), F32)] * 2
        + [pltpu.VMEM((GRID // SUB + 1, GRID, 128), F32)] * 2
        + [
            pltpu.VMEM((UNROLL // 2, 2 * SUB, 128), BF16),
        ],
        compiler_params=pltpu.CompilerParams(
            vmem_limit_bytes=22 << 20
        ),
        name="grid",
    )(recv)


def chain_kernel(
    grid_ref, row_ref, col, p_re, p_im, out_ref, image, from_h, from_s, from_x, mine, other,
    h_recv, s_recv, x_recv, h_send, s_send, x_send, g_send,
):
    z, f = lax.axis_index("wa"), lax.axis_index("facet")
    core = f & 1
    seat = 2 * z + core
    pair = f - core

    def at(other_seat):
        return (other_seat >> 1, pair + (other_seat & 1))

    def is_seat(*seats):
        hit = seat == seats[0]
        for other in seats[1:]:
            hit = jnp.logical_or(hit, seat == other)
        return hit

    barrier = pltpu.get_barrier_semaphore()
    for step in range(1, 8):
        pl.semaphore_signal(barrier, inc=1, device_id=at((seat + step) & 7), device_id_type=MESH)

    real = lax.broadcasted_iota(jnp.int32, (BLOCK, 2 * GRID), 1) & 127 < 64

    def block_rows(i):
        return pl.ds(pl.multiple_of(i * BLOCK, BLOCK), BLOCK)

    def chunk_rows(i):
        return pl.ds(pl.multiple_of(i * CHUNK, CHUNK), CHUNK)

    def transform(i):
        rows = block_rows(i)
        both = jnp.concatenate([row_ref[rows, pl.ds(0, GRID)], row_ref[rows, pl.ds(GRID, GRID)]], axis=0)
        parts = jnp.dot(both, grid_ref[...], preferred_element_type=F32)
        turned = jnp.concatenate(
            [pltpu.roll(parts[BLOCK:, t * 128 : (t + 1) * 128], 64, 1) for t in range(GRID // SUB)], axis=1
        )
        half = parts[:BLOCK] + jnp.where(real, -turned, turned)
        image[rows, :] = jnp.dot(half.astype(BF16), col[...], preferred_element_type=F32)

    transform(0)
    pl.semaphore_wait(barrier, 7)

    to_h = jnp.where(seat == 0, 2, jnp.where(seat == 3, 1, jnp.where(seat == 6, 4, 5)))
    to_s = jnp.where(seat == 1, 6, jnp.where(seat == 2, 4, jnp.where(seat == 4, 3, 1)))
    sends_h = is_seat(0, 3, 4, 6)
    sends_s = is_seat(1, 2, 4, 6)
    sends_x = is_seat(0, 2, 3, 5)
    takes_h = is_seat(1, 2, 4, 5, 7)
    away = is_seat(1, 3, 4, 6)
    lag = jnp.where(is_seat(2, 4), 1, 3)

    def copy_h(i):
        rows = chunk_rows(i)
        return pltpu.make_async_remote_copy(
            src_ref=mine.at[rows], dst_ref=from_h.at[rows], send_sem=h_send.at[i], recv_sem=h_recv.at[i],
            device_id=at(to_h), device_id_type=MESH,
        )

    def copy_x(i, source=mine):
        rows = chunk_rows(i)
        return pltpu.make_async_remote_copy(
            src_ref=source.at[rows], dst_ref=from_x.at[rows], send_sem=x_send.at[i], recv_sem=x_recv.at[i],
            device_id=at(seat ^ 1), device_id_type=MESH,
        )

    def copy_g(i):
        rows = chunk_rows(i)
        return pltpu.make_async_remote_copy(
            src_ref=other.at[rows], dst_ref=from_h.at[rows], send_sem=g_send.at[i], recv_sem=h_recv.at[i],
            device_id=at(7), device_id_type=MESH,
        )

    def copy_s(i):
        rows = chunk_rows(i)
        return pltpu.make_async_remote_copy(
            src_ref=mine.at[rows], dst_ref=from_s.at[rows], send_sem=s_send.at[i], recv_sem=s_recv.at[i],
            device_id=at(to_s), device_id_type=MESH,
        )

    def turn(rows, re, im):
        c, s = p_re[rows, :], p_im[rows, :]
        return c * re - s * im, c * im + s * re

    def halves(ref, rows):
        return ref[rows, pl.ds(0, GRID)].astype(F32), ref[rows, pl.ds(GRID, GRID)].astype(F32)

    def keep(ref, rows, re, im):
        ref[rows, pl.ds(0, GRID)] = re.astype(BF16)
        ref[rows, pl.ds(GRID, GRID)] = im.astype(BF16)

    def plus(rows, ref, pair_in):
        re, im = halves(ref, rows)
        return pair_in[0] + re, pair_in[1] + im

    def work(t, carry):
        @pl.when(t < BLOCKS)
        def _():
            @pl.when(is_seat(0, 6))
            def _():
                for part in range(PARTS):
                    i = t * PARTS + part
                    mine[chunk_rows(i), :] = image[chunk_rows(i), :].astype(BF16)
                    copy_h(i).start()

                    @pl.when(seat == 0)
                    def _():
                        copy_x(i).start()
                        out_ref[chunk_rows(i), :] = mine[chunk_rows(i), :]

                    @pl.when(seat == 6)
                    def _():
                        copy_s(i).start()

            @pl.when(is_seat(2, 3, 5))
            def _():
                for part in range(PARTS):
                    i = t * PARTS + part
                    other[chunk_rows(i), :] = image[chunk_rows(i), :].astype(BF16)
                    copy_x(i, other).start()

            @pl.when(t < BLOCKS - 1)
            def _():
                transform(t + 1)

            @pl.when(seat == 3)
            def _():
                for part in range(PARTS):
                    i = t * PARTS + part
                    rows = chunk_rows(i)
                    copy_x(i).wait_recv()
                    keep(mine, rows, *plus(rows, image, turn(rows, *halves(from_x, rows))))
                    copy_h(i).start()

        block = t - lag

        @pl.when(takes_h & (block >= 0) & (block < BLOCKS))
        def _():
            for part in range(PARTS):
                i = block * PARTS + part
                rows = chunk_rows(i)

                @pl.when(seat == 1)
                def _():
                    copy_x(i).wait_recv()
                    twice = turn(rows, *turn(rows, *halves(from_x, rows)))
                    copy_h(i).wait_recv()
                    keep(mine, rows, *plus(rows, image, turn(rows, *plus(rows, from_h, twice))))

                    copy_s(i).start()

                @pl.when(seat == 2)
                def _():
                    copy_h(i).wait_recv()
                    once = plus(rows, image, turn(rows, *halves(from_h, rows)))
                    keep(out_ref, rows, *once)
                    copy_x(i).wait_recv()
                    keep(mine, rows, *plus(rows, from_x, turn(rows, *once)))
                    copy_s(i).start()

                @pl.when(seat == 4)
                def _():
                    copy_h(i).wait_recv()
                    once = plus(rows, image, turn(rows, *halves(from_h, rows)))
                    keep(mine, rows, *once)
                    copy_s(i).start()
                    copy_x(i).wait_recv()
                    keep(other, rows, *plus(rows, from_x, turn(rows, *once)))
                    copy_g(i).start()
                    copy_h(i).start()

                @pl.when(is_seat(5, 7))
                def _():
                    copy_h(i).wait_recv()
                    keep(out_ref, rows, *plus(rows, image, turn(rows, *halves(from_h, rows))))

        return carry

    lax.fori_loop(0, BLOCKS + 3, work, 0)

    @pl.when(away)
    def _():
        def finish(i, carry):
            copy_s(i).wait_recv()
            out_ref[chunk_rows(i), :] = from_s[chunk_rows(i), :]
            return carry

        lax.fori_loop(0, CHUNKS, finish, 0)

    def drain(i, carry):
        @pl.when(sends_h)
        def _():
            copy_h(i).wait_send()

        @pl.when(sends_x)
        def _():
            copy_x(i).wait_send()

        @pl.when(sends_s)
        def _():
            copy_s(i).wait_send()

        @pl.when(seat == 4)
        def _():
            copy_g(i).wait_send()

        return carry

    lax.fori_loop(0, CHUNKS, drain, 0)


def chain(grid, row_table, col_table, p_re, p_im):
    band = (GRID, 2 * GRID)
    return pl.pallas_call(
        chain_kernel,
        out_shape=jax.ShapeDtypeStruct(band, BF16),
        in_specs=[VMEM] * 5,
        out_specs=VMEM,
        scratch_shapes=[
            pltpu.VMEM(band, F32),
        ]
        + [pltpu.VMEM(band, BF16)] * 5
        + [pltpu.SemaphoreType.DMA((CHUNKS,))] * 7,
        compiler_params=pltpu.CompilerParams(
            collective_id=1, has_side_effects=True, vmem_limit_bytes=24 << 20
        ),
        name="chain",
    )(grid, row_table, col_table, p_re, p_im)


def widen_kernel(band_ref, out_hbm, wide, sems):
    def copy(i):
        rows = pl.ds(i * BLOCK, BLOCK)
        return pltpu.make_async_copy(wide.at[rows], out_hbm.at[rows], sems.at[i])

    for i in range(BLOCKS):
        rows = pl.ds(i * BLOCK, BLOCK)
        wide[rows, :] = band_ref[rows, :].astype(F32)
        copy(i).start()
    for i in range(BLOCKS):
        copy(i).wait()


def widen(band):
    return pl.pallas_call(
        widen_kernel,
        out_shape=jax.ShapeDtypeStruct(band.shape, F32),
        in_specs=[VMEM],
        out_specs=HBM,
        scratch_shapes=[pltpu.VMEM(band.shape, F32), pltpu.SemaphoreType.DMA((BLOCKS,))],
        compiler_params=pltpu.CompilerParams(vmem_limit_bytes=8 << 20),
        name="widen",
    )(band)


def dft_rows():
    line = np.arange(GRID)
    angle = (line[:, None] * line[None, :] % GRID) * (2.0 * math.pi / GRID)
    table = np.concatenate([np.cos(angle), np.sin(angle)], axis=1) / math.sqrt(GRID)
    return table.astype(np.float32).astype(ml_dtypes.bfloat16)


def on_device(visibilities, uv_angles, routes, offsets, pixel_phase):
    vis = visibilities.transpose(1, 2, 0).reshape(2 * NVIS, SUBS)
    ang = uv_angles.transpose(1, 2, 0).reshape(2 * NVIS, SUBS)
    owners = routes.reshape(1, SUBS)
    recv, p_re, p_im, row_table, col_table = route(
        vis, ang, owners, offsets.T, pixel_phase[0], jnp.asarray(dft_rows())
    )
    grid = grid_owner(recv.reshape(SUBS * ROWS, 128))
    result = chain(grid, row_table, col_table, p_re, p_im)
    return widen(result).reshape(1, 1, GRID, 2 * GRID)


def solution(mesh):
    in_specs = (
        P(("wa", "facet"), None, None),
        P(("wa", "facet"), None, None),
        P(("wa", "facet"), None),
        P(("wa", "facet"), None),
        P("facet", None, None),
    )
    out_specs = P("wa", "facet", None, None)
    return jax.shard_map(
        on_device, mesh=mesh, in_specs=in_specs, out_specs=out_specs, check_vma=False
    )
```

```python
import functools
import math

import jax
import jax.numpy as jnp
import ml_dtypes
import numpy as np
from jax import lax
from jax.experimental import pallas as pl
from jax.experimental.pallas import tpu as pltpu
from jax.sharding import PartitionSpec as P

SUB = 64
GRID = 512
NVIS = 64
SUBS = 128
CAP = 2
KINDS = 4
ROWS = CAP * KINDS
BLOCK = 64
CHUNK = 32
BLOCKS = GRID // BLOCK
PARTS = BLOCK // CHUNK
CHUNKS = GRID // CHUNK
UNROLL = 64
BF16 = jnp.bfloat16
F32 = jnp.float32
MESH = pl.DeviceIdType.MESH
VMEM = pl.BlockSpec(memory_space=pltpu.VMEM)
HBM = pl.BlockSpec(memory_space=pltpu.HBM)
NT = (((1,), (1,)), ((), ()))


def sincos(x):
    h = x * 0.5
    q = h * h
    s = h + h * q * (
        -1.6666666666666602e-1
        + q * (8.333333333320001e-3
        + q * (-1.9841269829589539e-4
        + q * (2.7557314297030280e-6
        + q * (-2.5050747762850355e-8
        + q * 1.5891812000000000e-10))))
    )
    c = 1.0 + q * (
        -0.5
        + q * (4.16666666666665929218e-2
        + q * (-1.38888888888730564116e-3
        + q * (2.48015872888517045348e-5
        + q * (-2.75573141792967388112e-7
        + q * 2.08757008419747316778e-9))))
    )
    return 1.0 - 2.0 * s * s, 2.0 * s * c


def route_kernel(
    vis_hbm, ang_hbm, route_hbm, off_hbm, phase_hbm, rows_hbm, out_ref, p_re, p_im, row_ref, col, vis_ref, ang_ref, route_ref, off_ref, phase,
    send, recv, in_sems, send_sem, recv_sem, p_sems,
):
    inputs = [
        pltpu.make_async_copy(source, target, in_sems.at[n])
        for n, (source, target) in enumerate(
            ((route_hbm, route_ref), (off_hbm, off_ref), (ang_hbm, ang_ref), (vis_hbm, vis_ref), (rows_hbm, row_ref))
        )
    ]
    for copy in inputs:
        copy.start()

    z, f = lax.axis_index("wa"), lax.axis_index("facet")
    me = z * 32 + f

    low, core = z < 2, f & 1
    takes = (low & (core == 1)) | (jnp.logical_not(low) & (core == 0))

    def phase_own():
        return pltpu.make_async_copy(phase_hbm, phase, p_sems.at[2])

    def phase_out():
        return pltpu.make_async_remote_copy(
            src_ref=phase_hbm, dst_ref=phase, send_sem=p_sems.at[0], recv_sem=p_sems.at[1],
            device_id=(z, f ^ 1), device_id_type=MESH,
        )

    @pl.when(jnp.logical_not(takes))
    def _():
        phase_own().start()

    def each_peer(act):
        def early(i, carry):
            for n in range(5):
                act(me ^ (i * 5 + n) ^ 85)
            return carry

        def late(i, carry):
            for n in range(6):
                act(me ^ (i * 6 + n + 86) ^ 85)
            return carry

        lax.fori_loop(0, 17, early, 0)
        lax.fori_loop(0, 7, late, 0)

    barrier = pltpu.get_barrier_semaphore()
    each_peer(
        lambda to: pl.semaphore_signal(
            barrier, inc=1, device_id=(to >> 5, to & 31), device_id_type=MESH
        )
    )
    for copy in inputs[:4]:
        copy.wait()

    owner = route_ref[...]
    facet = owner & 31
    plane = owner >> 5
    odd = facet & 1
    seat = jnp.where(odd == 1, 6, 0)
    seat = jnp.where(plane == 1, jnp.where(odd == 1, 4, 2), seat)
    seat = jnp.where(plane == 2, jnp.where(odd == 1, 5, 3), seat)
    seat = jnp.where(plane == 3, jnp.where(odd == 1, 7, 1), seat)
    device = ((seat >> 1) << 5) + (facet - odd) + (seat & 1)
    owner_b = jnp.broadcast_to(owner.astype(F32), (SUBS, SUBS))
    row_i = lax.broadcasted_iota(jnp.int32, (SUBS, SUBS), 0)
    col_i = lax.broadcasted_iota(jnp.int32, (SUBS, SUBS), 1)
    earlier = jnp.where((owner_b == owner_b.T) & (row_i < col_i), 1.0, 0.0)
    rank = jnp.sum(earlier, axis=0, keepdims=True).astype(jnp.int32)
    slot = device * CAP + rank
    total = SUBS * CAP
    col_key = jnp.concatenate([slot + kind * total for kind in range(KINDS)], axis=1)

    angle = ang_ref[...]
    high = angle.astype(BF16)
    low = (angle - high.astype(F32)).astype(BF16)
    off_u, off_v = off_ref[0:1, :], off_ref[1:2, :]
    meta = jnp.where(row_i == 0, off_u >> 4, 0)
    meta = jnp.where(row_i == 1, off_u & 15, meta)
    meta = jnp.where(row_i == 2, off_v >> 4, meta)
    meta = jnp.where(row_i == 3, off_v & 15, meta)
    meta = meta.astype(F32).astype(BF16)
    data = jnp.concatenate([high, low, vis_ref[...], meta], axis=1)

    for block in range(ROWS):
        row = lax.broadcasted_iota(jnp.int32, (SUBS, KINDS * SUBS), 0) + block * SUBS
        place = row & (ROWS - 1)
        row_key = (place // CAP) * total + (row // ROWS) * CAP + place % CAP
        one_hot = jnp.where(row_key == col_key, 1.0, 0.0).astype(BF16)
        picked = lax.dot_general(one_hot, data, NT, preferred_element_type=F32)
        per = SUBS // ROWS
        send[pl.ds(block * per, per)] = picked.astype(BF16).reshape(per, ROWS, 128)

    pl.semaphore_wait(barrier, SUBS - 1)

    @pl.when(jnp.logical_not(takes))
    def _():
        phase_out().start()

    each_peer(
        lambda to: pltpu.make_async_remote_copy(
            src_ref=send.at[to], dst_ref=recv.at[me], send_sem=send_sem, recv_sem=recv_sem,
            device_id=(to >> 5, to & 31), device_id_type=MESH,
        ).start()
    )
    recv[me] = send[me]

    @pl.when(takes)
    def _():
        phase_out().wait_recv()

    @pl.when(jnp.logical_not(takes))
    def _():
        phase_own().wait()

    def angles(i, carry):
        rows = pl.ds(pl.multiple_of(i * BLOCK, BLOCK), BLOCK)
        c, s = sincos(phase[rows, :])
        p_re[rows, :] = c
        p_im[rows, :] = s
        return carry

    lax.fori_loop(0, BLOCKS, angles, 0)
    inputs[4].wait()
    for tile in range(GRID // SUB):
        rows = row_ref[pl.ds(tile * SUB, SUB), :]
        col[pl.ds(tile * 128, SUB), :] = rows
        col[pl.ds(tile * 128 + SUB, SUB), pl.ds(0, GRID)] = -rows[:, GRID:]
        col[pl.ds(tile * 128 + SUB, SUB), pl.ds(GRID, GRID)] = rows[:, :GRID]


    others = pl.ds(0, SUBS - 1)
    pltpu.make_async_copy(send.at[others], recv.at[others], recv_sem).wait()
    out_ref[...] = recv[...]
    pltpu.make_async_copy(send.at[others], recv.at[others], send_sem).wait()

    @pl.when(jnp.logical_not(takes))
    def _():
        phase_out().wait_send()


def route(vis, ang, owners, off, phase, row_table):
    pixels = jax.ShapeDtypeStruct((GRID, GRID), F32)
    return pl.pallas_call(
        route_kernel,
        out_shape=(
            jax.ShapeDtypeStruct((SUBS, ROWS, 128), BF16),
            pixels,
            pixels,
            jax.ShapeDtypeStruct((GRID, 2 * GRID), BF16),
            jax.ShapeDtypeStruct((2 * GRID, 2 * GRID), BF16),
        ),
        in_specs=[HBM] * 6,
        out_specs=(VMEM,) * 5,
        scratch_shapes=[
            pltpu.VMEM((2 * NVIS, SUBS), BF16),
            pltpu.VMEM((2 * NVIS, SUBS), F32),
            pltpu.VMEM((1, SUBS), jnp.int32),
            pltpu.VMEM((2, SUBS), jnp.int32),
            pltpu.VMEM((GRID, GRID), F32),
            pltpu.VMEM((SUBS, ROWS, 128), BF16),
            pltpu.VMEM((SUBS, ROWS, 128), BF16),
            pltpu.SemaphoreType.DMA((5,)),
            pltpu.SemaphoreType.DMA,
            pltpu.SemaphoreType.DMA,
            pltpu.SemaphoreType.DMA((3,)),
        ],
        compiler_params=pltpu.CompilerParams(
            collective_id=0, has_side_effects=True, vmem_limit_bytes=14 << 20
        ),
        name="route",
    )(*[pltpu.with_memory_space_constraint(value, pltpu.HBM) for value in (vis, ang, owners, off, phase, row_table)])


def complex_mul(a, b):
    return a[0] * b[0] - a[1] * b[1], a[0] * b[1] + a[1] * b[0]


def grid_kernel(
    recv_ref, grid_ref, wide, pos_v, pos_s, pos_sem, au_r, au_i, av_r, av_i, bu, bv, acc_a, acc_b, subs
):
    slots = SUBS * CAP
    wide[...] = recv_ref[...].astype(F32)

    lane8 = lax.broadcasted_iota(jnp.int32, (8, 128), 1)
    weight = jnp.where(lane8 == 0, 8192.0, 0.0)
    weight = jnp.where(lane8 == 1, 512.0, weight)
    weight = jnp.where(lane8 == 2, 16.0, weight)
    weight = jnp.where(lane8 == 3, 1.0, weight).astype(BF16)
    for j in range(CAP):
        meta = wide[pl.ds((KINDS - 1) * CAP + j, SUBS, stride=ROWS), :].astype(BF16)
        packed = lax.dot_general(weight, meta, NT, preferred_element_type=F32)
        pos_v[j] = packed.astype(jnp.int32)
    to_scalar = pltpu.make_async_copy(pos_v, pos_s, pos_sem)
    to_scalar.start()

    subs[...] = jnp.zeros_like(subs)

    group = 16
    first = lax.broadcasted_iota(jnp.int32, (group, 128), 1) < 64

    def tables(g, carry):
        clear = pl.ds(pl.multiple_of(g * SUB, SUB), SUB)
        for tile in range(GRID // SUB + 1):
            acc_a[tile, clear, :] = jnp.zeros((SUB, 128), F32)
            acc_b[tile, clear, :] = jnp.zeros((SUB, 128), F32)
        for j in range(CAP):
            start = g * group

            def rows(kind):
                at = start * ROWS + kind * CAP + j
                return wide[pl.ds(at, group, stride=ROWS), :]

            cos_t, sin_t = sincos(rows(0) + rows(1))
            vis = rows(2) * (1.0 / math.sqrt(NVIS))
            cos_o, sin_o = pltpu.roll(cos_t, 64, 1), pltpu.roll(sin_t, 64, 1)
            vis_o = pltpu.roll(vis, 64, 1)
            vis2 = (vis, jnp.where(first, vis_o, -vis_o))
            slot = pl.multiple_of(start + j * SUBS, group)
            for side in range(2):
                if side == 0:
                    e1 = (jnp.where(first, cos_t, cos_o), jnp.where(first, sin_t, sin_o))
                else:
                    e1 = (jnp.where(first, cos_o, cos_t), jnp.where(first, sin_o, sin_t))
                e2 = complex_mul(e1, e1)
                e4 = complex_mul(e2, e2)
                e8 = complex_mul(e4, e4)
                e16 = complex_mul(e8, e8)
                e24 = complex_mul(e16, e8)
                e32 = complex_mul(e16, e16)
                if side == 0:
                    tree = [vis2]
                    tree += [complex_mul(tree[0], e1)]
                    tree += [complex_mul(e, e2) for e in tree]
                    tree += [complex_mul(e, e4) for e in tree]
                else:
                    e3 = complex_mul(e2, e1)
                    one = (jnp.ones_like(cos_t), jnp.zeros_like(cos_t))
                    tree = [one, e1, e2, e3, e4] + [complex_mul(e4, e) for e in (e1, e2, e3)]
                for a, (re, im) in enumerate(tree):
                    where = pl.ds(slot * 8 + a, group, stride=8)
                    if side == 0:
                        au_r[where, :] = re
                        au_i[where, :] = im
                    else:
                        av_r[where, :] = jnp.where(first, re, -im)
                        av_i[where, :] = jnp.where(first, im, re)
                steps = bu if side == 0 else bv
                for b, e in enumerate((e8, e16, e24, e32)):
                    steps[2 * b, pl.ds(slot, group), :] = e[0]
                    steps[2 * b + 1, pl.ds(slot, group), :] = e[1]
        return carry

    lax.fori_loop(0, SUBS // group, tables, 0)
    to_scalar.wait()

    lane_in = lax.broadcasted_iota(jnp.int32, (SUB, 128), 1) & 63

    def form(slot):
        base = pl.multiple_of(slot * 8, 8)
        ur, ui = au_r[pl.ds(base, 8), :], au_i[pl.ds(base, 8), :]
        vr, vi = av_r[pl.ds(base, 8), :], av_i[pl.ds(base, 8), :]

        def step(table, b):
            return table[2 * b, pl.ds(slot, 1), :], table[2 * b + 1, pl.ds(slot, 1), :]

        left = [None] * 8
        right_r = [None] * 8
        right_i = [None] * 8
        left[4], right_r[4], right_i[4] = ur, vr, vi
        for b in range(4):
            br, bi = step(bu, b)
            x, y = br * ur, bi * ui
            left[3 - b] = x + y
            if b < 3:
                left[5 + b] = x - y
            br, bi = step(bv, b)
            x, y, z, w = br * vr, bi * vi, br * vi, bi * vr
            right_r[3 - b] = x + y
            right_i[3 - b] = z - w
            if b < 3:
                right_r[5 + b] = x - y
                right_i[5 + b] = z + w
        return jnp.concatenate(left, axis=0).astype(BF16), jnp.concatenate(right_r + right_i, axis=0).astype(BF16)

    nought = jnp.zeros((SUB, 128), BF16)

    def form_pair(slot):
        left_0, right_0 = form(slot)
        left_1, right_1 = form(slot + 1)
        left = jnp.concatenate(
            [jnp.concatenate([left_0, nought], axis=1), jnp.concatenate([nought, left_1], axis=1)], axis=0
        )
        right = jnp.concatenate([right_0, right_1], axis=1)
        return lax.dot_general(left, right, NT, preferred_element_type=F32).astype(BF16)

    def place(slot, sub, acc):
        packed = pos_s[slot >> 7, 0, slot & (SUBS - 1)]
        off_u, off_v = packed >> 9, packed & 511
        tile, shift = off_v >> 6, off_v & 63
        rows = pl.ds(off_u, SUB)
        here, there = acc.at[tile, rows, :], acc.at[tile + 1, rows, :]
        near = here[...] + pltpu.roll(sub, shift, 1).astype(F32)
        far = there[...] + pltpu.roll(sub, shift + 64, 1).astype(F32)
        pltpu.store(here, near, mask=lane_in >= shift)
        pltpu.store(there, far, mask=lane_in < shift)

    def place_all(start):
        for n in range(UNROLL):
            sub = subs[n // 2, pl.ds(n % 2 * SUB, SUB), :]
            place(start + n, sub, (acc_a, acc_b)[n % 2])

    def work(i, carry):
        place_all(jnp.maximum(i - 1, 0) * UNROLL)
        for n in range(0, UNROLL, 2):
            subs[n // 2] = form_pair(i * UNROLL + n)
        return carry

    lax.fori_loop(0, slots // UNROLL, work, 0)
    place_all(slots - UNROLL)

    def finish(g, carry):
        rows = pl.ds(pl.multiple_of(g * SUB, SUB), SUB)
        for tile in range(GRID // SUB):
            grid_ref[rows, pl.ds(tile * 128, 128)] = (acc_a[tile, rows, :] + acc_b[tile, rows, :]).astype(BF16)
        return carry

    lax.fori_loop(0, GRID // SUB, finish, 0)


def grid_owner(recv):
    slots = SUBS * CAP
    return pl.pallas_call(
        grid_kernel,
        out_shape=jax.ShapeDtypeStruct((GRID, 2 * GRID), BF16),
        in_specs=[VMEM],
        out_specs=VMEM,
        scratch_shapes=[
            pltpu.VMEM((SUBS * ROWS, 128), F32),
            pltpu.VMEM((CAP, 8, 128), jnp.int32),
            pltpu.SMEM((CAP, 8, 128), jnp.int32),
            pltpu.SemaphoreType.DMA,
        ]
        + [pltpu.VMEM((slots * 8, 128), F32)] * 4
        + [pltpu.VMEM((8, slots, 128), F32)] * 2
        + [pltpu.VMEM((GRID // SUB + 1, GRID, 128), F32)] * 2
        + [
            pltpu.VMEM((UNROLL // 2, 2 * SUB, 128), BF16),
        ],
        compiler_params=pltpu.CompilerParams(
            vmem_limit_bytes=22 << 20
        ),
        name="grid",
    )(recv)


def chain_kernel(
    grid_ref, row_ref, col, p_re, p_im, out_ref, image, from_h, from_s, from_x, mine, other,
    h_recv, s_recv, x_recv, h_send, s_send, x_send, g_send,
):
    z, f = lax.axis_index("wa"), lax.axis_index("facet")
    core = f & 1
    seat = 2 * z + core
    pair = f - core

    def at(other_seat):
        return (other_seat >> 1, pair + (other_seat & 1))

    def is_seat(*seats):
        hit = seat == seats[0]
        for other in seats[1:]:
            hit = jnp.logical_or(hit, seat == other)
        return hit

    barrier = pltpu.get_barrier_semaphore()
    for step in range(1, 8):
        pl.semaphore_signal(barrier, inc=1, device_id=at((seat + step) & 7), device_id_type=MESH)

    real = lax.broadcasted_iota(jnp.int32, (BLOCK, 2 * GRID), 1) & 127 < 64

    def block_rows(i):
        return pl.ds(pl.multiple_of(i * BLOCK, BLOCK), BLOCK)

    def chunk_rows(i):
        return pl.ds(pl.multiple_of(i * CHUNK, CHUNK), CHUNK)

    def transform(i):
        rows = block_rows(i)
        both = jnp.concatenate([row_ref[rows, pl.ds(0, GRID)], row_ref[rows, pl.ds(GRID, GRID)]], axis=0)
        parts = jnp.dot(both, grid_ref[...], preferred_element_type=F32)
        turned = jnp.concatenate(
            [pltpu.roll(parts[BLOCK:, t * 128 : (t + 1) * 128], 64, 1) for t in range(GRID // SUB)], axis=1
        )
        half = parts[:BLOCK] + jnp.where(real, -turned, turned)
        image[rows, :] = jnp.dot(half.astype(BF16), col[...], preferred_element_type=F32)

    transform(0)
    pl.semaphore_wait(barrier, 7)

    to_h = jnp.where(seat == 0, 2, jnp.where(seat == 3, 1, jnp.where(seat == 6, 4, 5)))
    to_s = jnp.where(seat == 1, 6, jnp.where(seat == 2, 4, jnp.where(seat == 4, 3, 1)))
    sends_h = is_seat(0, 3, 4, 6)
    sends_s = is_seat(1, 2, 4, 6)
    sends_x = is_seat(0, 2, 3, 5)
    takes_h = is_seat(1, 2, 4, 5, 7)
    away = is_seat(1, 3, 4, 6)
    lag = jnp.where(is_seat(2, 4), 1, 3)

    def copy_h(i):
        rows = chunk_rows(i)
        return pltpu.make_async_remote_copy(
            src_ref=mine.at[rows], dst_ref=from_h.at[rows], send_sem=h_send.at[i], recv_sem=h_recv.at[i],
            device_id=at(to_h), device_id_type=MESH,
        )

    def copy_x(i, source=mine):
        rows = chunk_rows(i)
        return pltpu.make_async_remote_copy(
            src_ref=source.at[rows], dst_ref=from_x.at[rows], send_sem=x_send.at[i], recv_sem=x_recv.at[i],
            device_id=at(seat ^ 1), device_id_type=MESH,
        )

    def copy_g(i):
        rows = chunk_rows(i)
        return pltpu.make_async_remote_copy(
            src_ref=other.at[rows], dst_ref=from_h.at[rows], send_sem=g_send.at[i], recv_sem=h_recv.at[i],
            device_id=at(7), device_id_type=MESH,
        )

    def copy_s(i):
        rows = chunk_rows(i)
        return pltpu.make_async_remote_copy(
            src_ref=mine.at[rows], dst_ref=from_s.at[rows], send_sem=s_send.at[i], recv_sem=s_recv.at[i],
            device_id=at(to_s), device_id_type=MESH,
        )

    def turn(rows, re, im):
        c, s = p_re[rows, :], p_im[rows, :]
        return c * re - s * im, c * im + s * re

    def halves(ref, rows):
        return ref[rows, pl.ds(0, GRID)].astype(F32), ref[rows, pl.ds(GRID, GRID)].astype(F32)

    def keep(ref, rows, re, im):
        ref[rows, pl.ds(0, GRID)] = re.astype(BF16)
        ref[rows, pl.ds(GRID, GRID)] = im.astype(BF16)

    def plus(rows, ref, pair_in):
        re, im = halves(ref, rows)
        return pair_in[0] + re, pair_in[1] + im

    def work(t, carry):
        @pl.when(t < BLOCKS)
        def _():
            @pl.when(is_seat(0, 6))
            def _():
                for part in range(PARTS):
                    i = t * PARTS + part
                    mine[chunk_rows(i), :] = image[chunk_rows(i), :].astype(BF16)
                    copy_h(i).start()

                    @pl.when(seat == 0)
                    def _():
                        copy_x(i).start()
                        out_ref[chunk_rows(i), :] = mine[chunk_rows(i), :]

                    @pl.when(seat == 6)
                    def _():
                        copy_s(i).start()

            @pl.when(is_seat(2, 3, 5))
            def _():
                for part in range(PARTS):
                    i = t * PARTS + part
                    other[chunk_rows(i), :] = image[chunk_rows(i), :].astype(BF16)
                    copy_x(i, other).start()

            @pl.when(t < BLOCKS - 1)
            def _():
                transform(t + 1)

            @pl.when(seat == 3)
            def _():
                for part in range(PARTS):
                    i = t * PARTS + part
                    rows = chunk_rows(i)
                    copy_x(i).wait_recv()
                    keep(mine, rows, *plus(rows, image, turn(rows, *halves(from_x, rows))))
                    copy_h(i).start()

        block = t - lag

        @pl.when(takes_h & (block >= 0) & (block < BLOCKS))
        def _():
            for part in range(PARTS):
                i = block * PARTS + part
                rows = chunk_rows(i)

                @pl.when(seat == 1)
                def _():
                    copy_x(i).wait_recv()
                    twice = turn(rows, *turn(rows, *halves(from_x, rows)))
                    copy_h(i).wait_recv()
                    keep(mine, rows, *plus(rows, image, turn(rows, *plus(rows, from_h, twice))))

                    copy_s(i).start()

                @pl.when(seat == 2)
                def _():
                    copy_h(i).wait_recv()
                    once = plus(rows, image, turn(rows, *halves(from_h, rows)))
                    keep(out_ref, rows, *once)
                    copy_x(i).wait_recv()
                    keep(mine, rows, *plus(rows, from_x, turn(rows, *once)))
                    copy_s(i).start()

                @pl.when(seat == 4)
                def _():
                    copy_h(i).wait_recv()
                    once = plus(rows, image, turn(rows, *halves(from_h, rows)))
                    keep(mine, rows, *once)
                    copy_s(i).start()
                    copy_x(i).wait_recv()
                    keep(other, rows, *plus(rows, from_x, turn(rows, *once)))
                    copy_g(i).start()
                    copy_h(i).start()

                @pl.when(is_seat(5, 7))
                def _():
                    copy_h(i).wait_recv()
                    keep(out_ref, rows, *plus(rows, image, turn(rows, *halves(from_h, rows))))

        return carry

    lax.fori_loop(0, BLOCKS + 3, work, 0)

    @pl.when(away)
    def _():
        def finish(i, carry):
            copy_s(i).wait_recv()
            out_ref[chunk_rows(i), :] = from_s[chunk_rows(i), :]
            return carry

        lax.fori_loop(0, CHUNKS, finish, 0)

    def drain(i, carry):
        @pl.when(sends_h)
        def _():
            copy_h(i).wait_send()

        @pl.when(sends_x)
        def _():
            copy_x(i).wait_send()

        @pl.when(sends_s)
        def _():
            copy_s(i).wait_send()

        @pl.when(seat == 4)
        def _():
            copy_g(i).wait_send()

        return carry

    lax.fori_loop(0, CHUNKS, drain, 0)


def chain(grid, row_table, col_table, p_re, p_im):
    band = (GRID, 2 * GRID)
    return pl.pallas_call(
        chain_kernel,
        out_shape=jax.ShapeDtypeStruct(band, BF16),
        in_specs=[VMEM] * 5,
        out_specs=VMEM,
        scratch_shapes=[
            pltpu.VMEM(band, F32),
        ]
        + [pltpu.VMEM(band, BF16)] * 5
        + [pltpu.SemaphoreType.DMA((CHUNKS,))] * 7,
        compiler_params=pltpu.CompilerParams(
            collective_id=1, has_side_effects=True, vmem_limit_bytes=24 << 20
        ),
        name="chain",
    )(grid, row_table, col_table, p_re, p_im)


def widen_kernel(band_ref, out_hbm, wide, sems):
    def copy(i):
        rows = pl.ds(i * BLOCK, BLOCK)
        return pltpu.make_async_copy(wide.at[rows], out_hbm.at[rows], sems.at[i])

    for i in range(BLOCKS):
        rows = pl.ds(i * BLOCK, BLOCK)
        wide[rows, :] = band_ref[rows, :].astype(F32)
        copy(i).start()
    for i in range(BLOCKS):
        copy(i).wait()


def widen(band):
    return pl.pallas_call(
        widen_kernel,
        out_shape=jax.ShapeDtypeStruct(band.shape, F32),
        in_specs=[VMEM],
        out_specs=HBM,
        scratch_shapes=[pltpu.VMEM(band.shape, F32), pltpu.SemaphoreType.DMA((BLOCKS,))],
        compiler_params=pltpu.CompilerParams(vmem_limit_bytes=8 << 20),
        name="widen",
    )(band)


def dft_rows():
    line = np.arange(GRID)
    angle = (line[:, None] * line[None, :] % GRID) * (2.0 * math.pi / GRID)
    table = np.concatenate([np.cos(angle), np.sin(angle)], axis=1) / math.sqrt(GRID)
    return table.astype(np.float32).astype(ml_dtypes.bfloat16)


def on_device(visibilities, uv_angles, routes, offsets, pixel_phase):
    vis = visibilities.transpose(1, 2, 0).reshape(2 * NVIS, SUBS)
    ang = uv_angles.transpose(1, 2, 0).reshape(2 * NVIS, SUBS)
    owners = routes.reshape(1, SUBS)
    recv, p_re, p_im, row_table, col_table = route(
        vis, ang, owners, offsets.T, pixel_phase[0], jnp.asarray(dft_rows())
    )
    grid = grid_owner(recv.reshape(SUBS * ROWS, 128))
    result = chain(grid, row_table, col_table, p_re, p_im)
    return widen(result).reshape(1, 1, GRID, 2 * GRID)


def solution(mesh):
    in_specs = (
        P(("wa", "facet"), None, None),
        P(("wa", "facet"), None, None),
        P(("wa", "facet"), None),
        P(("wa", "facet"), None),
        P("facet", None, None),
    )
    out_specs = P("wa", "facet", None, None)
    return jax.shard_map(
        on_device, mesh=mesh, in_specs=in_specs, out_specs=out_specs, check_vma=False
    )
```
